32 devices in a mesh: ctx: 8 (over y, x, core), mp: 4 (over z).
Axes of the slice: x: 2, y: 2, z: 4, core: 2. Of those that a mesh axis runs over, the one named last changes fastest.
Arguments:
- queries: bfloat16 [128, 6144], P('ctx', 'mp'), may hold values from -9 to 9
- cache_keys: bfloat16 [8, 4096, 128], P('mp', 'ctx'), may hold values from -9 to 9, as said below
- cache_values: bfloat16 [8, 4096, 128], P('mp', 'ctx'), may hold values from -6 to 6, as said below
- new_keys: bfloat16 [8, 128, 128], P('mp', 'ctx'), may hold values from -6 to 6, as said below
- new_values: bfloat16 [8, 128, 128], P('mp', 'ctx'), may hold values from -6 to 6, as said below
- out_proj: bfloat16 [6144, 6144], P('mp', 'ctx'), may hold values from -3 to 3
- residual: bfloat16 [128, 6144], P('mp', 'ctx'), may hold values from -24 to 24
- norm_gain: bfloat16 [6144], replicated, may hold values from 0.5 to 1.5
- gate_proj: bfloat16 [8, 6144, 8192], P('ctx', None, 'mp'), may hold values from -0.078125 to 0.078125
- up_proj: bfloat16 [8, 6144, 8192], P('ctx', None, 'mp'), may hold values from -0.078125 to 0.078125
- down_proj: bfloat16 [8, 8192, 6144], P('ctx', 'mp'), may hold values from -0.09375 to 0.09375
- expert_ids: int32 [128, 2], replicated, may hold values from 0 to 7, all different within a row; in each aligned block of 128 rows (0 to 127, 128 to 255, ...) at most 64 rows name the same one
- route_logits: float32 [128, 2], replicated, may hold values from -6 to 6
Outputs:
- layer_out: bfloat16 [128, 6144], P('mp', 'ctx')
The draws below stay inside these ranges and needn't reach their ends.
Inputs may be any that keep to these rules, and one draw needn't show every extreme that they name: `expert_ids`: each row names 2 different experts; at most 64 rows name one expert, a bound that some block reaches. `cache_keys`: slot s holds key head s * 1; slots of one key head are equal. `cache_values`: slot s holds value head s * 1; slots of one head are equal. `new_keys`: slot s holds key head s * 1; slots of one key head are equal. `new_values`: slot s holds value head s * 1; slots of one head are equal.
All inputs are finite; a program needn't handle non-finite values.
Results may differ from the reference program's by a relative error of at most 0.024.
Values may be sent and summed in bfloat16 or wider, within the bound.
No kernel may reach another device: no remote copies, remote signals or barrier semaphores. Data moves between devices by JAX's collectives and lax.ppermute only.
A program may use at most 128 MiB of HBM per device.

```python
import math
import jax
import jax.numpy as jnp
import numpy as np
from jax import lax

D = 6144
HEADS = 48
KV_HEADS = 8
HEAD_DIM = 128
EXPERTS = 8
TOP = 2
FF = 8192
TOKENS = 128
CTX_LEN = 4096
SLOTS = 8
HID_DEV = 2048
CAP = 64
N_CTX = 8
N_MP = 4


def draw_queries(key, part):
    shape = (TOKENS, HEADS * HEAD_DIM)
    field = jnp.clip(1.5 * jax.random.normal(jax.random.fold_in(key, 1), shape, jnp.float32), -9.0, 9.0)
    return field.astype(jnp.bfloat16)


def draw_cache_keys(key, part):
    shape = (KV_HEADS, CTX_LEN, HEAD_DIM)
    field = jnp.clip(jax.random.normal(jax.random.fold_in(key, 2), shape, jnp.float32), -6.0, 6.0)
    return jnp.repeat(field, SLOTS // KV_HEADS, axis=0).astype(jnp.bfloat16)


def drawn_heads(key, salt, length):
    shape = (KV_HEADS, length, HEAD_DIM)
    field = jnp.clip(jax.random.normal(jax.random.fold_in(key, salt), shape, jnp.float32), -6.0, 6.0)
    return jnp.repeat(field, SLOTS // KV_HEADS, axis=0).astype(jnp.bfloat16)


def draw_cache_values(key, part):
    return drawn_heads(key, 3, CTX_LEN)


def draw_new_keys(key, part):
    return drawn_heads(key, 4, TOKENS)


def draw_new_values(key, part):
    return drawn_heads(key, 5, TOKENS)


def draw_residual(key, part):
    column = jnp.arange(D, dtype=jnp.float32) / D
    rise = jnp.exp(math.log(3.0) * column)
    jitter = jnp.exp(jax.random.uniform(jax.random.fold_in(key, 21), (D,), jnp.float32, -0.35, 0.35))
    field = jax.random.normal(jax.random.fold_in(key, 23), (TOKENS, D), jnp.float32)
    return jnp.clip(field * rise[None, :] * jitter[None, :], -24.0, 24.0).astype(jnp.bfloat16)


def strengthened(values, key, source, target, parts, factor):
    def block_of(axis_at):
        return (jnp.arange(values.shape[axis_at]) // (values.shape[axis_at] // parts)).reshape((-1,) + (1,) * (values.ndim - 1 - axis_at))

    near = jax.random.permutation(key, parts)[block_of(target)]
    second = (block_of(target) + parts // 2) % parts
    return jnp.where((block_of(source) == near) | (block_of(source) == second), factor * values, values)


def steps_of(rng, dims, shards, least, largest):
    loudness = 1.0
    for axis_at, parts in shards:
        heights = jax.random.uniform(jax.random.fold_in(jax.random.fold_in(rng, 6), axis_at), (parts,), jnp.float32, least / len(shards), largest / len(shards))
        loudness = loudness * jnp.repeat(jnp.exp(heights), dims[axis_at] // parts).reshape((-1,) + (1,) * (len(dims) - 1 - axis_at))
    return loudness


def deal_out(stream_key, own, number, rows, amount, top, most, slope):
    ranking = jax.random.permutation(stream_key, amount)
    heavy_load, common = portions_of(amount, rows * top, most, slope, True), portions_of(amount, rows * top, most, slope, False)
    places = jnp.arange(amount)

    def named(sizes, turn):
        used = int((sizes > 0).sum())
        fixed = max(1, used // 4)
        shifted = fixed + (places - fixed + turn * (used - fixed)) % max(1, amount - fixed)
        return jnp.zeros((amount,), jnp.int32).at[ranking[jnp.where(places < fixed, places, shifted)]].set(jnp.asarray(sizes, jnp.int32))

    sizes = jnp.where(number % 4 == 0, named(heavy_load, number // 4), named(common, number - number // 4 - 1))
    mixed = jax.random.permutation(jax.random.fold_in(own, 3), amount)
    donor, taker = mixed[0:amount // 2 * 2:2], mixed[1:amount // 2 * 2:2]
    room = jnp.minimum(sizes[donor] - 1, most - sizes[taker]) // 2
    room = jnp.where((donor == ranking[0]) | (taker == ranking[0]) | (sizes[taker] == 0), 0, jnp.maximum(room, 0))
    shifted = jax.random.randint(jax.random.fold_in(own, 4), (amount // 2,), 0, 1 << 20) % (room + 1)
    sizes = sizes.at[donor].add(-shifted).at[taker].add(shifted)
    items = jnp.searchsorted(jnp.cumsum(sizes), jnp.arange(rows * top), side="right").astype(jnp.int32)
    grid = items.reshape(top, rows).T
    grid = grid[jax.random.permutation(jax.random.fold_in(own, 1), rows)]
    turn = jax.random.randint(jax.random.fold_in(own, 2), (rows, 1), 0, top)
    return jnp.take_along_axis(grid, (jnp.arange(top)[None, :] + turn) % top, axis=1)


def portions_of(amount, total, bound, lean, full):
    weights = [(1 << 20) // math.isqrt(grade ** lean) + 1 for grade in range(1, amount + 1)]
    largest = bound if full else min(bound, max(-(-total // amount), total * weights[0] // sum(weights)))
    least = 1 if total - largest >= amount - 1 else 0
    given, surplus = [largest] + [least] * (amount - 1), total - largest - least * (amount - 1)
    while surplus > 0:
        free = [i for i in range(1, amount) if given[i] < largest] or [i for i in range(1, amount) if given[i] < bound]
        pool, remaining = sum([weights[i] for i in free]), surplus
        for i in free:
            extra = min(bound - given[i], max(1, remaining * weights[i] // pool), surplus)
            given[i] = given[i] + extra
            surplus = surplus - extra
    return np.array(given)


def bell_draw(stream_key, shape, scale, bound, split=(), held_as=jnp.bfloat16):
    level = steps_of(stream_key, shape, split, -0.22, 0.18) if split else 1.0
    array = jax.random.normal(stream_key, shape, jnp.float32) * scale * level
    return jnp.minimum(jnp.maximum(array, -bound), bound).astype(held_as)


def heavy_noise(own_key, shape, scale, bound, shards, heavy, kind=jnp.bfloat16):
    array = scale * jax.random.normal(own_key, shape, jnp.float32)
    if shards:
        array = array * steps_of(own_key, shape, shards, -0.22, 0.18)
    return jnp.clip(strengthened(array, jax.random.fold_in(own_key, 3), *heavy), -bound, bound).astype(kind)


def setup_inputs(seed: int = 0) -> dict:
    key_of = jax.random.split(jax.random.key(seed), 14)
    queries = draw_queries(jax.random.fold_in(key_of[13], 71), 0)
    cache_keys = draw_cache_keys(jax.random.fold_in(key_of[13], 71), 0)
    cache_values = draw_cache_values(jax.random.fold_in(key_of[13], 71), 0)
    new_keys = draw_new_keys(jax.random.fold_in(key_of[13], 71), 0)
    new_values = draw_new_values(jax.random.fold_in(key_of[13], 71), 0)
    out_proj = bell_draw(key_of[5], (HEADS * HEAD_DIM, D), 0.5, 3.0, ((0, 4), (1, 8)))
    residual = draw_residual(jax.random.fold_in(key_of[13], 71), 0)
    norm_gain = jnp.clip(jax.random.uniform(key_of[7], (D,), jnp.float32, 0.5, 1.5), 0.5, 1.5).astype(jnp.bfloat16)
    gate_proj = bell_draw(key_of[8], (N_CTX, D, EXPERTS * FF // N_CTX), D ** -0.5, 0.078125, ((0, 8), (2, 4)))
    up_proj = bell_draw(key_of[9], (N_CTX, D, EXPERTS * FF // N_CTX), D ** -0.5, 0.078125, ((0, 8), (2, 4)))
    down_proj = heavy_noise(key_of[10], (N_CTX, EXPERTS * FF // N_CTX, D), FF ** -0.5, 0.09375, ((0, 8), (1, 4)), (0, 2, 8, 2.0))
    expert_ids_keys = jax.random.split(jax.random.fold_in(key_of[11], 1), TOKENS // TOKENS)
    expert_ids_turns = jax.random.permutation(jax.random.fold_in(key_of[11], 3), TOKENS // TOKENS)
    expert_ids = jax.vmap(lambda own, number: deal_out(jax.random.fold_in(key_of[11], 2), own, number, TOKENS, EXPERTS, TOP, CAP, 2))(expert_ids_keys, expert_ids_turns).reshape((TOKENS, TOP))
    route_logits = bell_draw(key_of[12], (TOKENS, TOP), 1.0, 6.0, (), jnp.float32)
    return dict(queries=queries, cache_keys=cache_keys, cache_values=cache_values, new_keys=new_keys, new_values=new_values, out_proj=out_proj, residual=residual, norm_gain=norm_gain, gate_proj=gate_proj, up_proj=up_proj, down_proj=down_proj, expert_ids=expert_ids, route_logits=route_logits)


def route_slots(expert_ids):
    flat = expert_ids.reshape(-1)
    onehot = (flat[:, None] == jnp.arange(EXPERTS, dtype=jnp.int32)[None, :]).astype(jnp.int32)
    before = jnp.cumsum(onehot, axis=0, dtype=jnp.int32) - onehot
    return lax.optimization_barrier(jnp.sum(before * onehot, axis=1, dtype=jnp.int32)).reshape(expert_ids.shape)

def reference(queries, cache_keys, cache_values, new_keys, new_values, out_proj, residual, norm_gain, gate_proj, up_proj, down_proj, expert_ids, route_logits):
    repeat = SLOTS // KV_HEADS
    group_size = HEADS // KV_HEADS
    scale = 1.0 / math.sqrt(HEAD_DIM)
    position = jnp.arange(TOKENS, dtype=jnp.int32)
    allowed = jnp.concatenate([jnp.ones((TOKENS, CTX_LEN), dtype=bool), position[None, :] <= position[:, None]], axis=1)

    def one_head(head):
        slot_index = head // group_size * repeat
        keys = jnp.concatenate([cache_keys[slot_index], new_keys[slot_index]], axis=0)
        values = jnp.concatenate([cache_values[slot_index], new_values[slot_index]], axis=0)
        query = lax.dynamic_slice_in_dim(queries, head * HEAD_DIM, HEAD_DIM, 1)
        scores = jnp.dot(query, keys.T, preferred_element_type=jnp.float32) * scale
        scores = jnp.where(allowed, scores, -jnp.inf)
        highest = lax.optimization_barrier(jnp.max(scores, axis=1, keepdims=True))
        expo = jnp.exp(scores - highest)
        denom = lax.optimization_barrier(jnp.sum(expo, axis=1, keepdims=True))
        probs = expo.astype(jnp.bfloat16)
        return (jnp.dot(probs, values, preferred_element_type=jnp.float32) / denom).astype(jnp.bfloat16)
    heads_out = lax.map(one_head, jnp.arange(HEADS, dtype=jnp.int32))
    attn = jnp.transpose(heads_out, (1, 0, 2)).reshape(TOKENS, HEADS * HEAD_DIM)
    hidden = (residual.astype(jnp.float32) + jnp.dot(attn, out_proj, preferred_element_type=jnp.float32)).astype(jnp.bfloat16)
    hidden_wide = hidden.astype(jnp.float32)
    rms = lax.rsqrt(lax.optimization_barrier(jnp.mean(hidden_wide * hidden_wide, axis=1)) + 1e-05)
    scaled = (hidden_wide * norm_gain.astype(jnp.float32)[None, :]).astype(jnp.bfloat16)
    slots = route_slots(expert_ids)
    weights = jax.nn.softmax(route_logits, axis=1)
    view_gate = gate_proj.reshape(N_CTX, D, N_MP, HID_DEV)
    view_up = up_proj.reshape(N_CTX, D, N_MP, HID_DEV)
    view_down = down_proj.reshape(N_CTX, N_MP, HID_DEV, D)
    per_expert = FF // HID_DEV

    def add_expert(expert, total):
        block = expert * per_expert + jnp.arange(per_expert, dtype=jnp.int32)
        ctx_of = block % N_CTX
        mp_of = block // N_CTX
        gate_w = jnp.transpose(view_gate[ctx_of, :, mp_of, :], (1, 0, 2)).reshape(D, FF)
        up_w = jnp.transpose(view_up[ctx_of, :, mp_of, :], (1, 0, 2)).reshape(D, FF)
        down_w = view_down[ctx_of, mp_of]
        match = expert_ids == expert
        place = jnp.where(match, slots, CAP)
        table = place[:, :, None] == jnp.arange(CAP, dtype=jnp.int32)[None, None, :]
        pick = jnp.any(table, axis=1)
        rows_scaled = jnp.dot(pick.T.astype(jnp.bfloat16), scaled, preferred_element_type=jnp.float32).astype(jnp.bfloat16)
        rows_rms = jnp.dot(pick.T.astype(jnp.float32), rms, precision=lax.Precision.HIGHEST)
        gate = rows_rms[:, None] * jnp.dot(rows_scaled, gate_w, preferred_element_type=jnp.float32)
        upper = rows_rms[:, None] * jnp.dot(rows_scaled, up_w, preferred_element_type=jnp.float32)
        act = (jax.nn.silu(gate) * upper).astype(jnp.bfloat16)
        act_blocks = jnp.transpose(act.reshape(CAP, per_expert, HID_DEV), (1, 0, 2))

        def add_block(accum, pair):
            part_act, part_w = pair
            term = jnp.dot(part_act, part_w, preferred_element_type=jnp.float32).astype(jnp.bfloat16)
            return (accum + lax.optimization_barrier(term).astype(jnp.float32), None)
        expert_out, _ = lax.scan(add_block, jnp.zeros((CAP, D), jnp.float32), (act_blocks, down_w))
        combine = lax.optimization_barrier(jnp.sum(jnp.where(table, weights[:, :, None], 0.0), axis=1))
        return total + jnp.dot(combine, expert_out, precision=lax.Precision.HIGHEST)
    moe = lax.fori_loop(0, EXPERTS, add_expert, jnp.zeros((TOKENS, D), jnp.float32))
    return (hidden_wide + moe).astype(jnp.bfloat16)
```

```python
import math

import jax
import jax.numpy as jnp
from jax import lax
from jax.experimental import pallas as pl
from jax.experimental.pallas import tpu as pltpu
from jax.sharding import PartitionSpec as P

D = 6144
EXPERTS = 8
TOP = 2


neg_big = -1e30
norm_eps = 1e-05


def route_slots(expert_ids):
    flat = expert_ids.reshape(-1)
    onehot = (flat[:, None] == jnp.arange(EXPERTS, dtype=jnp.int32)[None, :]).astype(jnp.int32)
    before = jnp.cumsum(onehot, axis=0, dtype=jnp.int32) - onehot
    return jnp.sum(before * onehot, axis=1, dtype=jnp.int32).reshape(expert_ids.shape)


def softmax_pieces(query_block, keys_local, values_local, allowed, scale):
    scores = (
        jnp.einsum("srd,skd->srk", query_block, keys_local, preferred_element_type=jnp.float32)
        * scale
    )
    scores = jnp.where(allowed[None, :, :], scores, neg_big)
    highest = jnp.max(scores, axis=2)
    expo = jnp.exp(scores - highest[:, :, None])
    denom = jnp.sum(expo, axis=2)
    summed = jnp.einsum(
        "srk,skd->srd", expo.astype(jnp.bfloat16), values_local, preferred_element_type=jnp.float32
    )
    return (highest, denom, summed)


def join_softmax(former, latter):
    highest = jnp.maximum(former[0], latter[0])
    right = jnp.exp(latter[0] - highest)
    denom = latter[1] * right
    summed = latter[2] * right[:, :, None]
    return (highest, denom, summed)


def gathered_path(
    queries,
    cache_keys,
    cache_values,
    new_keys,
    new_values,
    out_proj,
    residual,
    norm_gain,
    gate_proj,
    up_proj,
    down_proj,
    expert_ids,
    route_logits,
):
    ctx_count = lax.axis_size("ctx")
    mp_count = lax.axis_size("mp")
    ctx_index = lax.axis_index("ctx")
    mp_index = lax.axis_index("mp")
    tok_local = queries.shape[0]
    tokens = tok_local * ctx_count
    slot_local = cache_keys.shape[0]
    cache_local = cache_keys.shape[1]
    head_dim = cache_keys.shape[2]
    heads_local = queries.shape[1] // head_dim
    group_size = heads_local // slot_local
    width = cache_local + tok_local
    scale = 1.0 / math.sqrt(head_dim)
    d_local = out_proj.shape[1]
    key_value = jnp.stack(
        [
            jnp.concatenate([cache_keys, new_keys], axis=1),
            jnp.concatenate([cache_values, new_values], axis=1),
        ]
    )
    shaped = queries.reshape(tok_local, slot_local, group_size, head_dim)
    query_block = jnp.transpose(shaped, (1, 2, 0, 3)).reshape(
        slot_local, group_size * tok_local, head_dim
    )
    query_tok = ctx_index * tok_local + jnp.tile(jnp.arange(tok_local, dtype=jnp.int32), group_size)
    query_count = group_size * tok_local
    start_state = (
        jnp.full((slot_local, query_count), neg_big, jnp.float32),
        jnp.zeros((slot_local, query_count), jnp.float32),
        jnp.zeros((slot_local, query_count, head_dim), jnp.float32),
    )
    piece = lax.all_gather(key_value, "ctx", axis=2, tiled=True)
    position = jnp.arange(piece.shape[2], dtype=jnp.int32)
    shard = position // width
    within = position % width
    new_tok = shard * tok_local + within - cache_local
    allowed = (within[None, :] < cache_local) | (new_tok[None, :] <= query_tok[:, None])
    highest, denom, summed = join_softmax(
        start_state, softmax_pieces(query_block, piece[0], piece[1], allowed, scale)
    )
    shaped = (
        (summed / denom[:, :, None])
        .astype(jnp.bfloat16)
        .reshape(slot_local, group_size, tok_local, head_dim)
    )
    attn = jnp.transpose(shaped, (2, 0, 1, 3)).reshape(tok_local, heads_local * head_dim)
    projected = jnp.dot(
        lax.all_gather(attn, "ctx", axis=0, tiled=True),
        out_proj,
        preferred_element_type=jnp.float32,
    )
    res_rows = residual.shape[0]
    res_start = mp_index * res_rows
    current = lax.dynamic_slice_in_dim(projected, res_start, res_rows, 0)
    projected = lax.dynamic_update_slice_in_dim(
        projected, current + residual.astype(jnp.float32), res_start, 0
    )
    hidden = lax.psum(projected.astype(jnp.bfloat16), "mp")
    capacity = tokens * TOP // 4
    slots = route_slots(expert_ids)
    per_row = max(1, EXPERTS // mp_count)
    first_expert = mp_index * EXPERTS // mp_count
    own_expert = (mp_index * ctx_count + ctx_index) * EXPERTS // (ctx_count * mp_count)
    local = own_expert - first_expert
    row_experts = first_expert + jnp.arange(per_row, dtype=jnp.int32)
    match = expert_ids[None, :, :] == row_experts[:, None, None]
    place = jnp.where(match, slots[None, :, :], capacity)
    table = place[:, :, :, None] == jnp.arange(capacity, dtype=jnp.int32)[None, None, None, :]
    pick = jnp.any(table, axis=2)
    packed = jnp.einsum(
        "rtc,td->rcd", pick.astype(jnp.bfloat16), hidden, preferred_element_type=jnp.float32
    ).astype(jnp.bfloat16)
    gate_local = gate_proj[0]
    up_local = up_proj[0]
    down_local = down_proj[0]
    chosen = lax.dynamic_index_in_dim(
        lax.all_gather(packed, "ctx", axis=2, tiled=True), local, 0, keepdims=False
    )
    wide = chosen.astype(jnp.float32)
    gains = norm_gain.astype(jnp.float32)
    scaled = (wide * gains[None, :]).astype(jnp.bfloat16)
    gate_sum = jnp.dot(scaled, gate_local, preferred_element_type=jnp.float32)
    up_sum = jnp.dot(scaled, up_local, preferred_element_type=jnp.float32)
    gate_sum, up_sum, squares = (gate_sum, up_sum, jnp.sum(wide * wide, axis=1))
    rms = lax.rsqrt(squares / D + norm_eps)
    act = (jax.nn.silu(rms[:, None] * gate_sum) * (rms[:, None] * up_sum)).astype(jnp.bfloat16)
    part = lax.dot_general(
        down_local, act, (((0,), (1,)), ((), ())), preferred_element_type=jnp.float32
    )
    returned = lax.psum_scatter(
        jnp.concatenate(
            [jnp.where(local == which, part, 0.0) for which in range(per_row)], axis=1
        ).astype(jnp.bfloat16),
        "ctx",
        scatter_dimension=0,
        tiled=True,
    ).astype(jnp.float32)
    weights = jax.nn.softmax(route_logits, axis=1)
    combine = jnp.sum(jnp.where(table, weights[None, :, :, None], 0.0), axis=2)
    moe = jnp.einsum(
        "drc,rtc->td",
        returned.reshape(d_local, per_row, capacity),
        combine,
        precision=lax.Precision.HIGHEST,
        preferred_element_type=jnp.float32,
    )
    share = lax.psum_scatter(
        moe.astype(jnp.bfloat16), "mp", scatter_dimension=0, tiled=True
    ).astype(jnp.float32)
    own_hidden = lax.dynamic_slice_in_dim(hidden, res_start, res_rows, 0).astype(jnp.float32)
    return (own_hidden + share).astype(jnp.bfloat16)


BF16 = jnp.bfloat16
F32 = jnp.float32


def swap(array, axis_name, mask):
    count = lax.axis_size(axis_name)
    return lax.ppermute(array, axis_name, [(i, i ^ mask) for i in range(count)])


def experts_kernel(
    place_ref, even_ref, odd_ref, gain_ref, gate_hbm, up_hbm, down_hbm, out_even_ref, out_odd_ref,
    scaled_ref, act_ref, gate_acc, up_acc, out_acc, gate_buf, up_buf, down_buf, gate_sem, up_sem, down_sem,
):
    own = place_ref[0]
    half = even_ref.shape[0]
    blocks = 2 * half
    deep = even_ref.shape[2]
    ring = gate_buf.shape[0]
    down_blocks, down_rows = down_buf.shape[0], down_buf.shape[1]

    def gate_copy(step):
        rows = pl.ds(pl.multiple_of((own ^ step) * deep, deep), deep)
        slot = lax.rem(step, ring)
        return (
            pltpu.make_async_copy(gate_hbm.at[0, rows, :], gate_buf.at[slot], gate_sem.at[slot]),
            pltpu.make_async_copy(up_hbm.at[0, rows, :], up_buf.at[slot], up_sem.at[slot]),
        )

    def down_copy(step):
        rows = pl.ds(pl.multiple_of(step * down_rows, down_rows), down_rows)
        return pltpu.make_async_copy(down_hbm.at[0, rows, :], down_buf.at[step], down_sem.at[step])

    for step in range(ring):
        for copy in gate_copy(jnp.int32(step)):
            copy.start()
    squares = jnp.zeros((even_ref.shape[1], 1), F32)
    for step in range(blocks):
        wide = (even_ref if step % 2 == 0 else odd_ref)[step // 2].astype(F32)
        squares = squares + jnp.sum(wide * wide, axis=1, keepdims=True)
        scaled_ref[step] = (wide * gain_ref[own ^ step]).astype(BF16)
    rms = lax.rsqrt(squares / D + norm_eps)
    gate_acc[...] = jnp.zeros_like(gate_acc)
    up_acc[...] = jnp.zeros_like(up_acc)

    def gate_step(step, carry):
        slot = lax.rem(step, ring)
        for copy in gate_copy(step):
            copy.wait()
        rows = scaled_ref[step]
        gate_acc[...] += jnp.dot(rows, gate_buf[slot], preferred_element_type=F32)
        up_acc[...] += jnp.dot(rows, up_buf[slot], preferred_element_type=F32)

        @pl.when(step + ring < blocks)
        def _():
            for copy in gate_copy(step + ring):
                copy.start()

        @pl.when(step + ring == blocks)
        def _():
            for index in range(down_blocks):
                down_copy(jnp.int32(index)).start()

        return carry

    lax.fori_loop(0, blocks, gate_step, 0)
    gate = rms * gate_acc[...]
    act = (gate / (1.0 + jnp.exp(-gate)) * (rms * up_acc[...])).astype(BF16)
    for index in range(down_blocks):
        act_ref[index] = act[:, index * down_rows : (index + 1) * down_rows]
    out_acc[...] = jnp.zeros_like(out_acc)

    def down_step(step, carry):
        down_copy(step).wait()
        out_acc[...] += jnp.dot(act_ref[step], down_buf[step], preferred_element_type=F32)
        return carry

    lax.fori_loop(0, down_blocks, down_step, 0)
    for step in range(blocks):
        columns = pl.ds(pl.multiple_of((own ^ step) * deep, deep), deep)
        (out_even_ref if step % 2 == 0 else out_odd_ref)[step // 2] = out_acc[:, columns].astype(BF16)


def run_experts(place, even, odd, gain, gate_proj, up_proj, down_proj):
    half, rows, deep = even.shape
    units = gate_proj.shape[2]
    wide = down_proj.shape[2]
    ring, down_blocks = 3, 8
    vmem = pl.BlockSpec(memory_space=pltpu.VMEM)
    hbm = pl.BlockSpec(memory_space=pl.ANY)
    weights = 2 * (2 * gate_proj.size + down_proj.size)
    return pl.pallas_call(
        experts_kernel,
        out_shape=(jax.ShapeDtypeStruct(even.shape, BF16),) * 2,
        in_specs=[pl.BlockSpec(memory_space=pltpu.SMEM), vmem, vmem, vmem, hbm, hbm, hbm],
        out_specs=(vmem, vmem),
        scratch_shapes=[
            pltpu.VMEM((2 * half, rows, deep), BF16),
            pltpu.VMEM((down_blocks, rows, units // down_blocks), BF16),
            pltpu.VMEM((rows, units), F32),
            pltpu.VMEM((rows, units), F32),
            pltpu.VMEM((rows, wide), F32),
            pltpu.VMEM((ring, deep, units), BF16),
            pltpu.VMEM((ring, deep, units), BF16),
            pltpu.VMEM((down_blocks, units // down_blocks, wide), BF16),
            pltpu.SemaphoreType.DMA((ring,)),
            pltpu.SemaphoreType.DMA((ring,)),
            pltpu.SemaphoreType.DMA((down_blocks,)),
        ],
        compiler_params=pltpu.CompilerParams(vmem_limit_bytes=58 << 20),
        cost_estimate=pl.CostEstimate(flops=rows * weights, bytes_accessed=weights, transcendentals=rows * units),
        name="experts",
    )(place, even, odd, gain, gate_proj, up_proj, down_proj)


def exchange_path(
    queries,
    cache_keys,
    cache_values,
    new_keys,
    new_values,
    out_proj,
    residual,
    norm_gain,
    gate_proj,
    up_proj,
    down_proj,
    expert_ids,
    route_logits,
):
    ctx_count = lax.axis_size("ctx")
    mp_count = lax.axis_size("mp")
    ctx_index = lax.axis_index("ctx")
    mp_index = lax.axis_index("mp")
    tok_local = queries.shape[0]
    tokens = tok_local * ctx_count
    slot_local, cache_local, head_dim = cache_keys.shape
    heads_local = queries.shape[1] // head_dim
    group_size = heads_local // slot_local
    d_local = out_proj.shape[1]
    res_rows = residual.shape[0]
    half = ctx_count // 2
    scale = 1.0 / math.sqrt(head_dim)
    capacity = tokens * TOP // 4
    per_row = max(1, EXPERTS // mp_count)
    first_expert = mp_index * EXPERTS // mp_count

    def local_expert(ctx_at):
        return (mp_index * ctx_count + ctx_at) * EXPERTS // (ctx_count * mp_count) - first_expert

    blocks = [queries] + [swap(queries, "ctx", 2 * k) for k in range(1, half)]
    pair_keys = [swap(cache_keys, "ctx", 1), swap(new_keys, "ctx", 1)]
    pair_values = [swap(cache_values, "ctx", 1), swap(new_values, "ctx", 1)]
    keys = jnp.concatenate([cache_keys, pair_keys[0], new_keys, pair_keys[1]], axis=1)
    values = jnp.concatenate([cache_values, pair_values[0], new_values, pair_values[1]], axis=1)
    rows = half * tok_local
    shaped = jnp.stack(blocks).reshape(rows, slot_local, group_size, head_dim)
    query_block = jnp.transpose(shaped, (1, 2, 0, 3)).reshape(slot_local, group_size * rows, head_dim)
    row = jnp.arange(group_size * rows, dtype=jnp.int32) % rows
    row_tok = (ctx_index ^ (2 * (row // tok_local))) * tok_local + row % tok_local
    column = jnp.arange(2 * (cache_local + tok_local), dtype=jnp.int32)
    late = column - 2 * cache_local
    key_tok = (ctx_index ^ (late // tok_local)) * tok_local + late % tok_local
    allowed = (late < 0)[None, :] | (key_tok[None, :] <= row_tok[:, None])
    scores = jnp.einsum("srd,skd->srk", query_block, keys, preferred_element_type=F32) * scale
    scores = jnp.where(allowed[None, :, :], scores, neg_big)
    shift = lax.reduce_precision(jnp.max(scores, axis=2), 8, 7)
    expo = jnp.exp(scores - shift[:, :, None])
    denom = jnp.sum(expo, axis=2)
    summed = jnp.einsum("srk,skd->srd", expo.astype(BF16), values, preferred_element_type=F32)
    denom_high = lax.reduce_precision(denom, 8, 7)
    stats = jnp.stack([shift, denom_high, denom - denom_high]).reshape(3 * heads_local, rows)
    stats = jnp.pad(stats.astype(BF16).T, ((0, 0), (0, head_dim - 3 * heads_local)))
    mine = jnp.concatenate(
        [summed.astype(BF16).reshape(heads_local, rows, head_dim), stats[None]], axis=0
    )

    def ordered(array, k):
        parts = array.reshape(heads_local + 1, half, tok_local, head_dim)
        parts = jnp.concatenate([parts[:, k ^ b : (k ^ b) + 1] for b in range(half)], axis=1)
        return parts.reshape(heads_local + 1, rows, head_dim)

    partials = [mine] + [ordered(swap(mine, "ctx", 2 * k), k) for k in range(1, half)]
    pieces = []
    for part in partials:
        held = part[heads_local, :, : 3 * heads_local].astype(F32).T.reshape(3, heads_local, rows)
        pieces.append((held[0], held[1] + held[2], part[:heads_local].astype(F32)))
    highest = pieces[0][0]
    for piece in pieces[1:]:
        highest = jnp.maximum(highest, piece[0])
    lifts = [jnp.exp(piece[0] - highest) for piece in pieces]
    total = sum(lift * piece[1] for lift, piece in zip(lifts, pieces))
    mixed = sum((lift / total)[:, :, None] * piece[2] for lift, piece in zip(lifts, pieces))
    attn = jnp.transpose(mixed.astype(BF16), (1, 0, 2)).reshape(half, tok_local, heads_local * head_dim)
    attn_pair = swap(attn, "ctx", 1)
    is_odd = (ctx_index & 1) == 1
    attn = jnp.stack([jnp.where(is_odd, attn_pair, attn), jnp.where(is_odd, attn, attn_pair)], axis=1)

    projected = jnp.dot(
        attn.reshape(tokens, heads_local * head_dim), out_proj, preferred_element_type=F32
    ).reshape(mp_count, res_rows, d_local)
    pair_at = (ctx_index // 2) ^ mp_index
    parts = [lax.dynamic_index_in_dim(projected, pair_at ^ k, 0, keepdims=False) for k in range(mp_count)]
    hidden = parts[0] + residual.astype(F32)
    for k in range(1, mp_count):
        hidden = hidden + swap(parts[k].astype(BF16), "mp", k).astype(F32)
    hidden = hidden.astype(BF16)

    order = mp_index ^ jnp.arange(mp_count, dtype=jnp.int32)

    def by_block(table):
        return jnp.take(table.reshape(mp_count, res_rows, TOP), order, axis=0).reshape(tokens, TOP)

    ids = by_block(expert_ids)
    slots = by_block(route_slots(expert_ids))
    weights = by_block(jax.nn.softmax(route_logits, axis=1))
    row_experts = first_expert + jnp.arange(per_row, dtype=jnp.int32)
    match = ids[None, :, :] == row_experts[:, None, None]
    place = jnp.where(match, slots[None, :, :], capacity)
    table = place[:, :, :, None] == jnp.arange(capacity, dtype=jnp.int32)[None, None, None, :]
    pick = jnp.any(table, axis=2).astype(BF16)
    combine = jnp.sum(jnp.where(table, weights[None, :, :, None], 0.0), axis=2)

    everyone = jnp.concatenate([hidden] + [swap(hidden, "mp", k) for k in range(1, mp_count)], axis=0)
    packed = jnp.einsum("rtc,td->rcd", pick, everyone, preferred_element_type=F32).astype(BF16)
    even = [lax.dynamic_index_in_dim(packed, local_expert(ctx_index), 0, keepdims=False)]
    for k in range(1, half):
        sent = lax.dynamic_index_in_dim(packed, local_expert(ctx_index ^ (2 * k)), 0, keepdims=False)
        even.append(swap(sent, "ctx", 2 * k))
    even = jnp.stack(even)
    odd = swap(even, "ctx", 1)
    out_even, out_odd = run_experts(
        ctx_index.reshape(1),
        even,
        odd,
        norm_gain.astype(F32).reshape(ctx_count, 1, d_local),
        gate_proj,
        up_proj,
        down_proj,
    )
    summed = (out_even.astype(F32) + swap(out_odd, "ctx", 1).astype(F32)).astype(BF16)
    returned = [summed[0]] + [swap(summed[k], "ctx", 2 * k) for k in range(1, half)]
    spread = [
        lax.dynamic_index_in_dim(combine, local_expert(ctx_index ^ (2 * k)), 0, keepdims=False)
        for k in range(half)
    ]
    spread = jnp.concatenate(spread, axis=1)
    spread_high = lax.reduce_precision(spread, 8, 7)
    spread = jnp.concatenate([spread_high, spread - spread_high], axis=1).astype(BF16)
    moe = jnp.dot(
        spread, jnp.concatenate(returned + returned, axis=0), preferred_element_type=F32
    ).reshape(mp_count, res_rows, d_local)
    total = hidden.astype(F32) + moe[0]
    for k in range(1, mp_count):
        total = total + swap(moe[k].astype(BF16), "mp", k).astype(F32)
    return total.astype(BF16)


def on_device(*args):
    queries, cache_keys, out_proj, gate_proj, down_proj = (args[i] for i in (0, 1, 5, 8, 10))
    ctx_count, mp_count = lax.axis_size("ctx"), lax.axis_size("mp")
    per_row = max(1, EXPERTS // mp_count)
    fits = (
        ctx_count == 2 * mp_count
        and ctx_count & (ctx_count - 1) == 0
        and (ctx_count // per_row) % 2 == 0
        and out_proj.shape[1] % 256 == 0
        and gate_proj.shape[2] % 2048 == 0
        and queries.shape[0] % 16 == 0
        and 3 * (queries.shape[1] // cache_keys.shape[2]) <= cache_keys.shape[2]
    )
    return exchange_path(*args) if fits else gathered_path(*args)


def solution(mesh):
    placed = (
        P("ctx", "mp"),
        P("mp", "ctx", None),
        P("mp", "ctx", None),
        P("mp", "ctx", None),
        P("mp", "ctx", None),
        P("mp", "ctx"),
        P("mp", "ctx"),
        P(),
        P("ctx", None, "mp"),
        P("ctx", None, "mp"),
        P("ctx", "mp", None),
        P(),
        P(),
    )
    return jax.shard_map(
        on_device, mesh=mesh, in_specs=placed, out_specs=P("mp", "ctx"), check_vma=False
    )
```

```python
import functools
import math

import jax
import jax.numpy as jnp
from jax import lax
from jax.experimental import pallas as pl
from jax.experimental.pallas import tpu as pltpu
from jax.sharding import PartitionSpec as P

D = 6144
EXPERTS = 8
TOP = 2


neg_big = -1e30
norm_eps = 1e-05


def route_slots(expert_ids):
    flat = expert_ids.reshape(-1)
    onehot = (flat[:, None] == jnp.arange(EXPERTS, dtype=jnp.int32)[None, :]).astype(jnp.int32)
    before = jnp.cumsum(onehot, axis=0, dtype=jnp.int32) - onehot
    return jnp.sum(before * onehot, axis=1, dtype=jnp.int32).reshape(expert_ids.shape)


def softmax_pieces(query_block, keys_local, values_local, allowed, scale):
    scores = (
        jnp.einsum("srd,skd->srk", query_block, keys_local, preferred_element_type=jnp.float32)
        * scale
    )
    scores = jnp.where(allowed[None, :, :], scores, neg_big)
    highest = jnp.max(scores, axis=2)
    expo = jnp.exp(scores - highest[:, :, None])
    denom = jnp.sum(expo, axis=2)
    summed = jnp.einsum(
        "srk,skd->srd", expo.astype(jnp.bfloat16), values_local, preferred_element_type=jnp.float32
    )
    return (highest, denom, summed)


def join_softmax(former, latter):
    highest = jnp.maximum(former[0], latter[0])
    right = jnp.exp(latter[0] - highest)
    denom = latter[1] * right
    summed = latter[2] * right[:, :, None]
    return (highest, denom, summed)


def gathered_path(
    queries,
    cache_keys,
    cache_values,
    new_keys,
    new_values,
    out_proj,
    residual,
    norm_gain,
    gate_proj,
    up_proj,
    down_proj,
    expert_ids,
    route_logits,
):
    ctx_count = lax.axis_size("ctx")
    mp_count = lax.axis_size("mp")
    ctx_index = lax.axis_index("ctx")
    mp_index = lax.axis_index("mp")
    tok_local = queries.shape[0]
    tokens = tok_local * ctx_count
    slot_local = cache_keys.shape[0]
    cache_local = cache_keys.shape[1]
    head_dim = cache_keys.shape[2]
    heads_local = queries.shape[1] // head_dim
    group_size = heads_local // slot_local
    width = cache_local + tok_local
    scale = 1.0 / math.sqrt(head_dim)
    d_local = out_proj.shape[1]
    key_value = jnp.stack(
        [
            jnp.concatenate([cache_keys, new_keys], axis=1),
            jnp.concatenate([cache_values, new_values], axis=1),
        ]
    )
    shaped = queries.reshape(tok_local, slot_local, group_size, head_dim)
    query_block = jnp.transpose(shaped, (1, 2, 0, 3)).reshape(
        slot_local, group_size * tok_local, head_dim
    )
    query_tok = ctx_index * tok_local + jnp.tile(jnp.arange(tok_local, dtype=jnp.int32), group_size)
    query_count = group_size * tok_local
    start_state = (
        jnp.full((slot_local, query_count), neg_big, jnp.float32),
        jnp.zeros((slot_local, query_count), jnp.float32),
        jnp.zeros((slot_local, query_count, head_dim), jnp.float32),
    )
    piece = lax.all_gather(key_value, "ctx", axis=2, tiled=True)
    position = jnp.arange(piece.shape[2], dtype=jnp.int32)
    shard = position // width
    within = position % width
    new_tok = shard * tok_local + within - cache_local
    allowed = (within[None, :] < cache_local) | (new_tok[None, :] <= query_tok[:, None])
    highest, denom, summed = join_softmax(
        start_state, softmax_pieces(query_block, piece[0], piece[1], allowed, scale)
    )
    shaped = (
        (summed / denom[:, :, None])
        .astype(jnp.bfloat16)
        .reshape(slot_local, group_size, tok_local, head_dim)
    )
    attn = jnp.transpose(shaped, (2, 0, 1, 3)).reshape(tok_local, heads_local * head_dim)
    projected = jnp.dot(
        lax.all_gather(attn, "ctx", axis=0, tiled=True),
        out_proj,
        preferred_element_type=jnp.float32,
    )
    res_rows = residual.shape[0]
    res_start = mp_index * res_rows
    current = lax.dynamic_slice_in_dim(projected, res_start, res_rows, 0)
    projected = lax.dynamic_update_slice_in_dim(
        projected, current + residual.astype(jnp.float32), res_start, 0
    )
    hidden = lax.psum(projected.astype(jnp.bfloat16), "mp")
    capacity = tokens * TOP // 4
    slots = route_slots(expert_ids)
    per_row = max(1, EXPERTS // mp_count)
    first_expert = mp_index * EXPERTS // mp_count
    own_expert = (mp_index * ctx_count + ctx_index) * EXPERTS // (ctx_count * mp_count)
    local = own_expert - first_expert
    row_experts = first_expert + jnp.arange(per_row, dtype=jnp.int32)
    match = expert_ids[None, :, :] == row_experts[:, None, None]
    place = jnp.where(match, slots[None, :, :], capacity)
    table = place[:, :, :, None] == jnp.arange(capacity, dtype=jnp.int32)[None, None, None, :]
    pick = jnp.any(table, axis=2)
    packed = jnp.einsum(
        "rtc,td->rcd", pick.astype(jnp.bfloat16), hidden, preferred_element_type=jnp.float32
    ).astype(jnp.bfloat16)
    gate_local = gate_proj[0]
    up_local = up_proj[0]
    down_local = down_proj[0]
    chosen = lax.dynamic_index_in_dim(
        lax.all_gather(packed, "ctx", axis=2, tiled=True), local, 0, keepdims=False
    )
    wide = chosen.astype(jnp.float32)
    gains = norm_gain.astype(jnp.float32)
    scaled = (wide * gains[None, :]).astype(jnp.bfloat16)
    gate_sum = jnp.dot(scaled, gate_local, preferred_element_type=jnp.float32)
    up_sum = jnp.dot(scaled, up_local, preferred_element_type=jnp.float32)
    gate_sum, up_sum, squares = (gate_sum, up_sum, jnp.sum(wide * wide, axis=1))
    rms = lax.rsqrt(squares / D + norm_eps)
    act = (jax.nn.silu(rms[:, None] * gate_sum) * (rms[:, None] * up_sum)).astype(jnp.bfloat16)
    part = lax.dot_general(
        down_local, act, (((0,), (1,)), ((), ())), preferred_element_type=jnp.float32
    )
    returned = lax.psum_scatter(
        jnp.concatenate(
            [jnp.where(local == which, part, 0.0) for which in range(per_row)], axis=1
        ).astype(jnp.bfloat16),
        "ctx",
        scatter_dimension=0,
        tiled=True,
    ).astype(jnp.float32)
    weights = jax.nn.softmax(route_logits, axis=1)
    combine = jnp.sum(jnp.where(table, weights[None, :, :, None], 0.0), axis=2)
    moe = jnp.einsum(
        "drc,rtc->td",
        returned.reshape(d_local, per_row, capacity),
        combine,
        precision=lax.Precision.HIGHEST,
        preferred_element_type=jnp.float32,
    )
    share = lax.psum_scatter(
        moe.astype(jnp.bfloat16), "mp", scatter_dimension=0, tiled=True
    ).astype(jnp.float32)
    own_hidden = lax.dynamic_slice_in_dim(hidden, res_start, res_rows, 0).astype(jnp.float32)
    return (own_hidden + share).astype(jnp.bfloat16)


BF16 = jnp.bfloat16
F32 = jnp.float32
VMEM_SPEC = pl.BlockSpec(memory_space=pltpu.VMEM)
HBM_SPEC = pl.BlockSpec(memory_space=pl.ANY)
SMALL_MIB = 12
STAGED = (3, 1)
RING = 2
DOWN_RING = 3
EXPERTS_MIB = 27


def swap(array, axis_name, mask):
    count = lax.axis_size(axis_name)
    return lax.ppermute(array, axis_name, [(i, i ^ mask) for i in range(count)])


def device_call(kernel, name, outs, arrays, scratch=(), flops=0, limit=SMALL_MIB, specs=None):
    moved = sum(a.size * a.dtype.itemsize for a in arrays if specs is None)
    return pl.pallas_call(
        kernel,
        out_shape=outs,
        in_specs=specs or [VMEM_SPEC] * len(arrays),
        out_specs=jax.tree.map(lambda _: VMEM_SPEC, outs),
        scratch_shapes=list(scratch),
        compiler_params=pltpu.CompilerParams(vmem_limit_bytes=limit << 20),
        cost_estimate=pl.CostEstimate(flops=flops, bytes_accessed=moved, transcendentals=0),
        name=name,
    )(*arrays)


def in_hbm(array):
    return pltpu.with_memory_space_constraint(array, pltpu.HBM)


def in_vmem(array):
    return pltpu.with_memory_space_constraint(array, pltpu.VMEM)


def like(shape, dtype=BF16):
    return jax.ShapeDtypeStruct(shape, dtype)


def expert_at(shape, ctx_at):
    ctx_count, mp_count = shape
    mp_index = lax.axis_index("mp")
    own = lax.div((mp_index * ctx_count + ctx_at) * EXPERTS, ctx_count * mp_count)
    return own - lax.div(mp_index * EXPERTS, mp_count)


def tables_kernel(shape, ids_ref, logits_ref, pick_ref, high_ref, low_ref):
    mp_index = lax.axis_index("mp")
    mp_count = shape[1]
    per_row, capacity, tokens = pick_ref.shape
    rows = tokens // mp_count
    first = lax.div(mp_index * EXPERTS, mp_count)
    lane = lax.broadcasted_iota(jnp.int32, (1, tokens), 1)

    def by_block(values):
        for bit in range(mp_count.bit_length() - 1):
            size = rows << bit
            forward = pltpu.roll(values, size, 1)
            back = pltpu.roll(values, tokens - size, 1)
            moved = jnp.where((lane & size) != 0, forward, back)
            values = jnp.where(((mp_index >> bit) & 1) == 1, moved, values)
        return values

    logits = logits_ref[...]
    weights = jnp.exp(logits - jnp.max(logits, axis=0, keepdims=True))
    weights = weights / jnp.sum(weights, axis=0, keepdims=True)
    ids = ids_ref[...]
    earlier = lax.broadcasted_iota(jnp.int32, (tokens, tokens), 0) < lax.broadcasted_iota(
        jnp.int32, (tokens, tokens), 1
    )
    earlier = earlier.astype(F32).astype(BF16)
    for which in range(per_row):
        named = (ids == first + which).astype(F32)
        member = jnp.max(named, axis=0, keepdims=True)
        weight = jnp.sum(named * weights, axis=0, keepdims=True)
        slot = jnp.dot(
            jnp.broadcast_to(member, (8, tokens)).astype(BF16), earlier, preferred_element_type=F32
        )[0:1]
        slot = by_block(jnp.where(member > 0, slot, float(capacity)))
        weight = by_block(weight)
        taken = lax.broadcasted_iota(jnp.int32, (capacity, tokens), 0) == slot.astype(jnp.int32)
        pick_ref[which] = jnp.where(taken, 1.0, 0.0).astype(BF16)
        weight = jnp.where(taken, weight, 0.0)
        high = weight.astype(BF16)
        high_ref[which] = high
        low_ref[which] = (weight - high.astype(F32)).astype(BF16)


def attention_kernel(*refs):
    half = len(refs) - 8 - 1 - 3 - 4 - 1
    query_refs = refs[:half]
    sources = refs[half : half + 4]
    pair_k, pair_v, pair_nk, pair_nv = refs[half + 4 : half + 8]
    mine_ref, query_buf, key_buf, value_buf = refs[half + 8 : half + 12]
    held, copy_sem = refs[half + 12 : -1], refs[-1]
    copies = [
        pltpu.make_async_copy(source, buf, copy_sem.at[at]) for at, (source, buf) in enumerate(zip(sources, held))
    ]
    for at in (2, 0, 3, 1):
        copies[at].start()
    own_k, own_v, new_k, new_v = held
    own = lax.axis_index("ctx")
    slots, _, head_dim = own_k.shape
    tok_local = new_k.shape[1]
    rows = half * tok_local
    group = query_refs[0].shape[1] // head_dim // slots
    heads = slots * group
    factor = math.log2(math.e) / math.sqrt(head_dim)
    for at, query_ref in enumerate(query_refs):
        for head in range(heads):
            start = (head % group) * rows + at * tok_local
            query_buf[head // group, start : start + tok_local, :] = query_ref[
                :, head * head_dim : (head + 1) * head_dim
            ]
    for copy in copies:
        copy.wait()
    for part, (key_ref, value_ref) in enumerate(((new_k, new_v), (pair_nk, pair_nv))):
        for slot in range(slots):
            key_buf[slot, part * tok_local : (part + 1) * tok_local, :] = key_ref[slot]
            value_buf[slot, part * tok_local : (part + 1) * tok_local, :] = value_ref[slot]
    row = lax.rem(lax.broadcasted_iota(jnp.int32, (group * rows, 1), 0), rows)
    block = lax.div(row, tok_local)
    row_tok = (own ^ (2 * block)) * tok_local + row - block * tok_local
    column = lax.broadcasted_iota(jnp.int32, (1, 2 * tok_local), 1)
    block = lax.div(column, tok_local)
    key_tok = (own ^ block) * tok_local + column - block * tok_local
    seen = key_tok <= row_tok
    lane = lax.broadcasted_iota(jnp.int32, (rows, head_dim), 1)
    stats = jnp.zeros((rows, head_dim), F32)

    def product(left, right):
        return lax.dot_general(left, right, (((1,), (1,)), ((), ())), preferred_element_type=F32)

    for slot in range(slots):
        query = query_buf[slot]
        first = product(query, own_k[slot]) * factor
        second = product(query, pair_k[slot]) * factor
        third = jnp.where(seen, product(query, key_buf[slot]) * factor, neg_big)
        top = jnp.maximum(
            jnp.max(jnp.maximum(first, second), axis=1, keepdims=True),
            jnp.max(third, axis=1, keepdims=True),
        )
        shift = top.astype(BF16).astype(F32)
        first = jnp.exp2(first - shift)
        second = jnp.exp2(second - shift)
        third = jnp.exp2(third - shift)
        denom = jnp.sum(first + second, axis=1, keepdims=True) + jnp.sum(third, axis=1, keepdims=True)
        summed = jnp.dot(first.astype(BF16), own_v[slot], preferred_element_type=F32)
        summed += jnp.dot(second.astype(BF16), pair_v[slot], preferred_element_type=F32)
        summed += jnp.dot(third.astype(BF16), value_buf[slot], preferred_element_type=F32)
        summed = summed.astype(BF16)
        high = denom.astype(BF16).astype(F32)
        low = denom - high
        for index in range(group):
            head = slot * group + index
            span = slice(index * rows, (index + 1) * rows)
            mine_ref[head] = summed[span]
            stats = jnp.where(lane == head, shift[span], stats)
            stats = jnp.where(lane == heads + head, high[span], stats)
            stats = jnp.where(lane == 2 * heads + head, low[span], stats)
    mine_ref[heads] = stats.astype(BF16)


def join_kernel(*refs):
    part_refs, attn_ref = refs[:-1], refs[-1]
    half = len(part_refs)
    heads, head_dim = part_refs[0].shape[0] - 1, part_refs[0].shape[2]
    tok = part_refs[0].shape[1] // half
    for block in range(half):
        spans = [slice((k ^ block) * tok, ((k ^ block) + 1) * tok) for k in range(half)]
        stats = [ref[heads, span, :].astype(F32) for ref, span in zip(part_refs, spans)]
        highest = functools.reduce(jnp.maximum, stats)
        lifts = [jnp.exp2(stat - highest) for stat in stats]
        denoms = [
            pltpu.roll(stat, head_dim - heads, 1) + pltpu.roll(stat, head_dim - 2 * heads, 1)
            for stat in stats
        ]
        total = sum(lift * denom for lift, denom in zip(lifts, denoms))
        shares = [lift / total for lift in lifts]
        for head in range(heads):
            mixed = sum(
                share[:, head : head + 1] * ref[head, span, :].astype(F32)
                for share, ref, span in zip(shares, part_refs, spans)
            )
            attn_ref[block * tok : (block + 1) * tok, head * head_dim : (head + 1) * head_dim] = mixed.astype(BF16)


def project_kernel(own_ref, pair_ref, weight_ref, kept_ref, *refs):
    sent_refs, left = refs[:-1], refs[-1]
    ctx_index, mp_index = lax.axis_index("ctx"), lax.axis_index("mp")
    mp_count = len(sent_refs) + 1
    tok = own_ref.shape[0] // mp_count
    odd = ctx_index & 1
    pair_at = (ctx_index >> 1) ^ mp_index
    for k in range(mp_count):
        source = pl.ds(pl.multiple_of((pair_at ^ k) * tok, tok), tok)
        left[pl.ds(pl.multiple_of((2 * k + odd) * tok, tok), tok), :] = own_ref[source, :]
        left[pl.ds(pl.multiple_of((2 * k + 1 - odd) * tok, tok), tok), :] = pair_ref[source, :]
    projected = jnp.dot(left[...], weight_ref[...], preferred_element_type=F32)
    kept_ref[...] = projected[: 2 * tok]
    for k, ref in enumerate(sent_refs, 1):
        ref[...] = projected[2 * k * tok : 2 * (k + 1) * tok].astype(BF16)


def total_kernel(*refs):
    total = refs[0][...].astype(F32)
    for ref in refs[1:-1]:
        total = total + ref[...].astype(F32)
    refs[-1][...] = total.astype(BF16)


def pack_kernel(shape, pick_ref, *refs):
    mp_count, half = shape[1], shape[0] // 2
    hidden_refs, out_refs, packed = refs[:mp_count], refs[mp_count:-1], refs[-1]
    hidden = jnp.concatenate([ref[...] for ref in hidden_refs], axis=0)
    for which in range(pick_ref.shape[0]):
        packed[which] = jnp.dot(pick_ref[which], hidden, preferred_element_type=F32).astype(BF16)
    for k in range(half):
        out_refs[k][...] = packed[expert_at(shape, lax.axis_index("ctx") ^ (2 * k))]


def stage_kernel(first, *refs):
    gate_hbm, up_hbm = refs[:2]
    extra = (len(refs) - 5) // 2
    plain, gate_out, up_out = refs[2 : 2 + extra], refs[2 + extra], refs[3 + extra]
    plain_out, sem = refs[4 + extra : -1], refs[-1]
    own = lax.axis_index("ctx")
    count, deep = gate_out.shape[0], gate_out.shape[1]
    pairs = list(zip(plain, plain_out))
    for step in range(count):
        rows = pl.ds(pl.multiple_of((own ^ (first + step)) * deep, deep), deep)
        pairs.append((gate_hbm.at[0, rows, :], gate_out.at[step]))
        pairs.append((up_hbm.at[0, rows, :], up_out.at[step]))
    copies = [pltpu.make_async_copy(source, target, sem.at[at]) for at, (source, target) in enumerate(pairs)]
    for copy in copies:
        copy.start()
    for copy in copies:
        copy.wait()


def stage(gate_proj, up_proj, deep, first, count, limit, *plain):
    units = gate_proj.shape[2]
    return pl.pallas_call(
        functools.partial(stage_kernel, first),
        out_shape=(pltpu.VMEM((count, deep, units), BF16),) * 2 + tuple(pltpu.VMEM(a.shape, a.dtype) for a in plain),
        in_specs=[HBM_SPEC] * (2 + len(plain)),
        out_specs=(VMEM_SPEC,) * (2 + len(plain)),
        scratch_shapes=[pltpu.SemaphoreType.DMA((2 * count + len(plain),))],
        compiler_params=pltpu.CompilerParams(vmem_limit_bytes=limit << 20),
        cost_estimate=pl.CostEstimate(flops=0, bytes_accessed=4 * count * deep * units, transcendentals=0),
        name="stage",
    )(gate_proj, up_proj, *plain)


def experts_kernel(early, *refs):
    early_refs, refs = refs[: 2 * len(early)], refs[2 * len(early) :]
    count = len(refs) - 4 - 2 - 10
    row_refs = refs[:count]
    staged = sum(early)
    gain_ref, gate_hbm, up_hbm, down_hbm, out_even_ref, out_odd_ref = refs[count : count + 6]
    (scaled_ref, act_ref, gate_acc, up_acc, out_acc, gate_buf, up_buf, down_buf, gate_sem, down_sem) = refs[count + 6 :]
    own = lax.axis_index("ctx")
    half = count // 2
    deep = row_refs[0].shape[1]
    ring = gate_buf.shape[0]
    down_blocks, down_ring, down_rows = act_ref.shape[0], down_buf.shape[0], down_buf.shape[1]

    def gate_copy(step):
        rows = pl.ds(pl.multiple_of((own ^ step) * deep, deep), deep)
        slot = lax.rem(step, ring)
        return (
            pltpu.make_async_copy(gate_hbm.at[0, rows, :], gate_buf.at[slot], gate_sem.at[0, slot]),
            pltpu.make_async_copy(up_hbm.at[0, rows, :], up_buf.at[slot], gate_sem.at[1, slot]),
        )

    def down_copy(step):
        rows = pl.ds(pl.multiple_of(step * down_rows, down_rows), down_rows)
        slot = lax.rem(step, down_ring)
        return pltpu.make_async_copy(down_hbm.at[0, rows, :], down_buf.at[slot], down_sem.at[slot])

    for step in range(staged, min(count, staged + ring)):
        for copy in gate_copy(jnp.int32(step)):
            copy.start()
    squares = jnp.zeros((row_refs[0].shape[0], 1), F32)
    for step in range(count):
        wide = row_refs[step][...].astype(F32)
        squares = squares + jnp.sum(wide * wide, axis=1, keepdims=True)
        scaled_ref[step] = (wide * gain_ref[own ^ step]).astype(BF16)
    rms = lax.rsqrt(squares / D + norm_eps)
    gate_acc[...] = jnp.zeros_like(gate_acc)
    up_acc[...] = jnp.zeros_like(up_acc)

    begin = 0
    for at, number in enumerate(early):

        def early_step(step, carry, at=at, begin=begin):
            rows = scaled_ref[begin + step]
            gate_acc[...] += jnp.dot(rows, early_refs[2 * at][step], preferred_element_type=F32)
            up_acc[...] += jnp.dot(rows, early_refs[2 * at + 1][step], preferred_element_type=F32)
            return carry

        lax.fori_loop(0, number, early_step, 0)
        begin += number

    def gate_step(step, carry):
        slot = lax.rem(step, ring)
        for copy in gate_copy(step):
            copy.wait()
        rows = scaled_ref[step]
        gate_acc[...] += jnp.dot(rows, gate_buf[slot], preferred_element_type=F32)
        up_acc[...] += jnp.dot(rows, up_buf[slot], preferred_element_type=F32)

        @pl.when(step + ring < count)
        def _():
            for copy in gate_copy(step + ring):
                copy.start()

        @pl.when(step + ring == count)
        def _():
            for index in range(down_ring):
                down_copy(jnp.int32(index)).start()

        return carry

    lax.fori_loop(staged, count, gate_step, 0)
    gate = rms * gate_acc[...]
    act = (gate / (1.0 + jnp.exp(-gate)) * (rms * up_acc[...])).astype(BF16)
    for index in range(down_blocks):
        act_ref[index] = act[:, index * down_rows : (index + 1) * down_rows]
    out_acc[...] = jnp.zeros_like(out_acc)

    def down_step(step, carry):
        down_copy(step).wait()
        slot = lax.rem(step, down_ring)
        out_acc[...] += jnp.dot(act_ref[step], down_buf[slot], preferred_element_type=F32)

        @pl.when(step + down_ring < down_blocks)
        def _():
            down_copy(step + down_ring).start()

        return carry

    lax.fori_loop(0, down_blocks, down_step, 0)
    for step in range(count):
        columns = pl.ds(pl.multiple_of((own ^ step) * deep, deep), deep)
        (out_even_ref if step % 2 == 0 else out_odd_ref)[step // 2] = out_acc[:, columns].astype(BF16)


def run_experts(early, row_blocks, gain, gate_proj, up_proj, down_proj):
    rows, deep = row_blocks[0].shape
    count = len(row_blocks)
    units = gate_proj.shape[2]
    wide = down_proj.shape[2]
    ring, down_blocks, down_ring = RING, 8, DOWN_RING
    weights = 2 * (2 * gate_proj.size + down_proj.size)
    return pl.pallas_call(
        functools.partial(experts_kernel, tuple(gate.shape[0] for gate, _ in early)),
        out_shape=(like((count // 2, rows, deep)),) * 2,
        in_specs=[VMEM_SPEC] * (2 * len(early) + count + 1) + [HBM_SPEC] * 3,
        out_specs=(VMEM_SPEC, VMEM_SPEC),
        scratch_shapes=[
            pltpu.VMEM((count, rows, deep), BF16),
            pltpu.VMEM((down_blocks, rows, units // down_blocks), BF16),
            pltpu.VMEM((rows, units), F32),
            pltpu.VMEM((rows, units), F32),
            pltpu.VMEM((rows, wide), F32),
            pltpu.VMEM((ring, deep, units), BF16),
            pltpu.VMEM((ring, deep, units), BF16),
            pltpu.VMEM((down_ring, units // down_blocks, wide), BF16),
            pltpu.SemaphoreType.DMA((2, ring)),
            pltpu.SemaphoreType.DMA((down_ring,)),
        ],
        compiler_params=pltpu.CompilerParams(vmem_limit_bytes=EXPERTS_MIB << 20),
        cost_estimate=pl.CostEstimate(flops=rows * weights, bytes_accessed=weights, transcendentals=rows * units),
        name="experts",
    )(*[in_vmem(array) for both in early for array in both], *row_blocks, gain, gate_proj, up_proj, down_proj)


def pair_total_kernel(even_ref, other_ref, *out_refs):
    for k, ref in enumerate(out_refs):
        ref[...] = (even_ref[k].astype(F32) + other_ref[k].astype(F32)).astype(BF16)


def combine_kernel(shape, high_ref, low_ref, *refs):
    half, mp_count = shape[0] // 2, shape[1]
    piece_refs, kept_ref, sent_refs = refs[:half], refs[half], refs[half + 1 :]
    pieces = jnp.concatenate([ref[...] for ref in piece_refs], axis=0)
    experts = [expert_at(shape, lax.axis_index("ctx") ^ (2 * k)) for k in range(half)]
    total = None
    for table in (high_ref, low_ref):
        spread = jnp.concatenate([table[expert] for expert in experts], axis=0)
        term = lax.dot_general(spread, pieces, (((0,), (0,)), ((), ())), preferred_element_type=F32)
        total = term if total is None else total + term
    rows = kept_ref.shape[0]
    kept_ref[...] = total[:rows]
    for k, ref in enumerate(sent_refs, 1):
        ref[...] = total[k * rows : (k + 1) * rows].astype(BF16)


def exchange_path(
    queries,
    cache_keys,
    cache_values,
    new_keys,
    new_values,
    out_proj,
    residual,
    norm_gain,
    gate_proj,
    up_proj,
    down_proj,
    expert_ids,
    route_logits,
):
    ctx_count = lax.axis_size("ctx")
    mp_count = lax.axis_size("mp")
    shape = (ctx_count, mp_count)
    gate_hbm, up_hbm, down_hbm = in_hbm(gate_proj), in_hbm(up_proj), in_hbm(down_proj)
    tok_local = queries.shape[0]
    tokens = tok_local * ctx_count
    slot_local, cache_local, head_dim = cache_keys.shape
    heads = queries.shape[1] // head_dim
    d_local = out_proj.shape[1]
    res_rows = residual.shape[0]
    half = ctx_count // 2
    rows = half * tok_local
    capacity = tokens * TOP // 4
    per_row = max(1, EXPERTS // mp_count)

    blocks = [queries] + [swap(queries, "ctx", 2 * k) for k in range(1, half)]
    own = [cache_keys, cache_values, new_keys, new_values]
    pair = [swap(array, "ctx", 1) for array in own]
    mine = device_call(
        attention_kernel,
        "attention",
        like((heads + 1, rows, head_dim)),
        [in_vmem(array) for array in blocks] + [in_hbm(array) for array in own] + [in_vmem(array) for array in pair],
        [
            pltpu.VMEM((slot_local, heads // slot_local * rows, head_dim), BF16),
            pltpu.VMEM((slot_local, 2 * tok_local, head_dim), BF16),
            pltpu.VMEM((slot_local, 2 * tok_local, head_dim), BF16),
            *[pltpu.VMEM(array.shape, BF16) for array in own],
            pltpu.SemaphoreType.DMA((4,)),
        ],
        flops=8 * heads * rows * (cache_local + tok_local) * head_dim,
        limit=24,
        specs=[VMEM_SPEC] * half + [HBM_SPEC] * 4 + [VMEM_SPEC] * 4,
    )
    others = [swap(mine, "ctx", 2 * k) for k in range(1, half)]
    ids, logits, _ = lax.optimization_barrier((expert_ids.T, route_logits.T, mine))
    pick, high, low = device_call(
        functools.partial(tables_kernel, shape),
        "tables",
        (like((per_row, capacity, tokens)),) * 3,
        [ids, logits],
    )
    gain = norm_gain.astype(F32).reshape(ctx_count, 1, d_local)
    gate_later, _ = lax.optimization_barrier((gate_proj, mine))
    gate_a, up_a, out_proj, residual = stage(in_hbm(gate_later), up_hbm, d_local, 0, STAGED[0], 2, in_hbm(out_proj), in_hbm(residual)
    )
    pick, high, low, gain, gate_a, up_a, out_proj, residual, *others = lax.optimization_barrier(
        (pick, high, low, gain, gate_a, up_a, out_proj, residual, *others)
    )
    attn = device_call(join_kernel, "join", like((rows, heads * head_dim)), [mine] + others)
    block = like((res_rows, d_local))

    kept, *sent = device_call(
        project_kernel,
        "project",
        (like((res_rows, d_local), F32),) + (block,) * (mp_count - 1),
        [attn, swap(attn, "ctx", 1), out_proj],
        [pltpu.VMEM((tokens, heads * head_dim), BF16)],
        flops=2 * tokens * heads * head_dim * d_local,
    )
    arrived = [swap(array, "mp", k) for k, array in enumerate(sent, 1)]
    early = [(gate_a, up_a)]
    if STAGED[1]:
        gate_later, _ = lax.optimization_barrier((gate_proj, kept))
        gate_b, up_b = stage(in_hbm(gate_later), up_hbm, d_local, STAGED[0], STAGED[1], 2)
        gate_b, up_b, *arrived = lax.optimization_barrier((gate_b, up_b, *arrived))
        early.append((gate_b, up_b))
    hidden = device_call(total_kernel, "hidden", block, [kept, residual] + arrived)

    everyone = [hidden] + [swap(hidden, "mp", k) for k in range(1, mp_count)]
    even = device_call(
        functools.partial(pack_kernel, shape),
        "pack",
        (like((capacity, d_local)),) * half,
        [pick] + everyone,
        [pltpu.VMEM((per_row, capacity, d_local), BF16)],
    )
    even = [even[0]] + [swap(even[k], "ctx", 2 * k) for k in range(1, half)]
    odd = [swap(array, "ctx", 1) for array in even]
    out_even, out_odd = run_experts(
        early,
        [array for both in zip(even, odd) for array in both],
        gain,
        gate_hbm,
        up_hbm,
        down_hbm,
    )
    pieces = device_call(
        pair_total_kernel,
        "pair_total",
        (like((capacity, d_local)),) * half,
        [out_even, swap(out_odd, "ctx", 1)],
    )
    pieces = [pieces[0]] + [swap(pieces[k], "ctx", 2 * k) for k in range(1, half)]
    kept, *sent = device_call(
        functools.partial(combine_kernel, shape),
        "combine",
        (like((res_rows, d_local), F32),) + (block,) * (mp_count - 1),
        [high, low] + pieces,
    )
    arrived = [swap(array, "mp", k) for k, array in enumerate(sent, 1)]
    return device_call(total_kernel, "layer_out", block, [kept, hidden] + arrived)


def on_device(*args):
    queries, cache_keys, out_proj, gate_proj, down_proj = (args[i] for i in (0, 1, 5, 8, 10))
    ctx_count, mp_count = lax.axis_size("ctx"), lax.axis_size("mp")
    per_row = max(1, EXPERTS // mp_count)
    fits = (
        ctx_count == 2 * mp_count
        and ctx_count & (ctx_count - 1) == 0
        and (ctx_count // per_row) % 2 == 0
        and out_proj.shape[1] % 256 == 0
        and gate_proj.shape[2] % 2048 == 0
        and queries.shape[0] % 16 == 0
        and 3 * (queries.shape[1] // cache_keys.shape[2]) <= cache_keys.shape[2]
    )
    return exchange_path(*args) if fits else gathered_path(*args)


def solution(mesh):
    placed = (
        P("ctx", "mp"),
        P("mp", "ctx", None),
        P("mp", "ctx", None),
        P("mp", "ctx", None),
        P("mp", "ctx", None),
        P("mp", "ctx"),
        P("mp", "ctx"),
        P(),
        P("ctx", None, "mp"),
        P("ctx", None, "mp"),
        P("ctx", "mp", None),
        P(),
        P(),
    )
    return jax.shard_map(
        on_device, mesh=mesh, in_specs=placed, out_specs=P("mp", "ctx"), check_vma=False
    )
```

```python
import functools
import math

import jax
import jax.numpy as jnp
from jax import lax
from jax.experimental import pallas as pl
from jax.experimental.pallas import tpu as pltpu
from jax.sharding import PartitionSpec as P

D = 6144
EXPERTS = 8
TOP = 2


neg_big = -1e30
norm_eps = 1e-05


def route_slots(expert_ids):
    flat = expert_ids.reshape(-1)
    onehot = (flat[:, None] == jnp.arange(EXPERTS, dtype=jnp.int32)[None, :]).astype(jnp.int32)
    before = jnp.cumsum(onehot, axis=0, dtype=jnp.int32) - onehot
    return jnp.sum(before * onehot, axis=1, dtype=jnp.int32).reshape(expert_ids.shape)


def softmax_pieces(query_block, keys_local, values_local, allowed, scale):
    scores = (
        jnp.einsum("srd,skd->srk", query_block, keys_local, preferred_element_type=jnp.float32)
        * scale
    )
    scores = jnp.where(allowed[None, :, :], scores, neg_big)
    highest = jnp.max(scores, axis=2)
    expo = jnp.exp(scores - highest[:, :, None])
    denom = jnp.sum(expo, axis=2)
    summed = jnp.einsum(
        "srk,skd->srd", expo.astype(jnp.bfloat16), values_local, preferred_element_type=jnp.float32
    )
    return (highest, denom, summed)


def join_softmax(former, latter):
    highest = jnp.maximum(former[0], latter[0])
    right = jnp.exp(latter[0] - highest)
    denom = latter[1] * right
    summed = latter[2] * right[:, :, None]
    return (highest, denom, summed)


def gathered_path(
    queries,
    cache_keys,
    cache_values,
    new_keys,
    new_values,
    out_proj,
    residual,
    norm_gain,
    gate_proj,
    up_proj,
    down_proj,
    expert_ids,
    route_logits,
):
    ctx_count = lax.axis_size("ctx")
    mp_count = lax.axis_size("mp")
    ctx_index = lax.axis_index("ctx")
    mp_index = lax.axis_index("mp")
    tok_local = queries.shape[0]
    tokens = tok_local * ctx_count
    slot_local = cache_keys.shape[0]
    cache_local = cache_keys.shape[1]
    head_dim = cache_keys.shape[2]
    heads_local = queries.shape[1] // head_dim
    group_size = heads_local // slot_local
    width = cache_local + tok_local
    scale = 1.0 / math.sqrt(head_dim)
    d_local = out_proj.shape[1]
    key_value = jnp.stack(
        [
            jnp.concatenate([cache_keys, new_keys], axis=1),
            jnp.concatenate([cache_values, new_values], axis=1),
        ]
    )
    shaped = queries.reshape(tok_local, slot_local, group_size, head_dim)
    query_block = jnp.transpose(shaped, (1, 2, 0, 3)).reshape(
        slot_local, group_size * tok_local, head_dim
    )
    query_tok = ctx_index * tok_local + jnp.tile(jnp.arange(tok_local, dtype=jnp.int32), group_size)
    query_count = group_size * tok_local
    start_state = (
        jnp.full((slot_local, query_count), neg_big, jnp.float32),
        jnp.zeros((slot_local, query_count), jnp.float32),
        jnp.zeros((slot_local, query_count, head_dim), jnp.float32),
    )
    piece = lax.all_gather(key_value, "ctx", axis=2, tiled=True)
    position = jnp.arange(piece.shape[2], dtype=jnp.int32)
    shard = position // width
    within = position % width
    new_tok = shard * tok_local + within - cache_local
    allowed = (within[None, :] < cache_local) | (new_tok[None, :] <= query_tok[:, None])
    highest, denom, summed = join_softmax(
        start_state, softmax_pieces(query_block, piece[0], piece[1], allowed, scale)
    )
    shaped = (
        (summed / denom[:, :, None])
        .astype(jnp.bfloat16)
        .reshape(slot_local, group_size, tok_local, head_dim)
    )
    attn = jnp.transpose(shaped, (2, 0, 1, 3)).reshape(tok_local, heads_local * head_dim)
    projected = jnp.dot(
        lax.all_gather(attn, "ctx", axis=0, tiled=True),
        out_proj,
        preferred_element_type=jnp.float32,
    )
    res_rows = residual.shape[0]
    res_start = mp_index * res_rows
    current = lax.dynamic_slice_in_dim(projected, res_start, res_rows, 0)
    projected = lax.dynamic_update_slice_in_dim(
        projected, current + residual.astype(jnp.float32), res_start, 0
    )
    hidden = lax.psum(projected.astype(jnp.bfloat16), "mp")
    capacity = tokens * TOP // 4
    slots = route_slots(expert_ids)
    per_row = max(1, EXPERTS // mp_count)
    first_expert = mp_index * EXPERTS // mp_count
    own_expert = (mp_index * ctx_count + ctx_index) * EXPERTS // (ctx_count * mp_count)
    local = own_expert - first_expert
    row_experts = first_expert + jnp.arange(per_row, dtype=jnp.int32)
    match = expert_ids[None, :, :] == row_experts[:, None, None]
    place = jnp.where(match, slots[None, :, :], capacity)
    table = place[:, :, :, None] == jnp.arange(capacity, dtype=jnp.int32)[None, None, None, :]
    pick = jnp.any(table, axis=2)
    packed = jnp.einsum(
        "rtc,td->rcd", pick.astype(jnp.bfloat16), hidden, preferred_element_type=jnp.float32
    ).astype(jnp.bfloat16)
    gate_local = gate_proj[0]
    up_local = up_proj[0]
    down_local = down_proj[0]
    chosen = lax.dynamic_index_in_dim(
        lax.all_gather(packed, "ctx", axis=2, tiled=True), local, 0, keepdims=False
    )
    wide = chosen.astype(jnp.float32)
    gains = norm_gain.astype(jnp.float32)
    scaled = (wide * gains[None, :]).astype(jnp.bfloat16)
    gate_sum = jnp.dot(scaled, gate_local, preferred_element_type=jnp.float32)
    up_sum = jnp.dot(scaled, up_local, preferred_element_type=jnp.float32)
    gate_sum, up_sum, squares = (gate_sum, up_sum, jnp.sum(wide * wide, axis=1))
    rms = lax.rsqrt(squares / D + norm_eps)
    act = (jax.nn.silu(rms[:, None] * gate_sum) * (rms[:, None] * up_sum)).astype(jnp.bfloat16)
    part = lax.dot_general(
        down_local, act, (((0,), (1,)), ((), ())), preferred_element_type=jnp.float32
    )
    returned = lax.psum_scatter(
        jnp.concatenate(
            [jnp.where(local == which, part, 0.0) for which in range(per_row)], axis=1
        ).astype(jnp.bfloat16),
        "ctx",
        scatter_dimension=0,
        tiled=True,
    ).astype(jnp.float32)
    weights = jax.nn.softmax(route_logits, axis=1)
    combine = jnp.sum(jnp.where(table, weights[None, :, :, None], 0.0), axis=2)
    moe = jnp.einsum(
        "drc,rtc->td",
        returned.reshape(d_local, per_row, capacity),
        combine,
        precision=lax.Precision.HIGHEST,
        preferred_element_type=jnp.float32,
    )
    share = lax.psum_scatter(
        moe.astype(jnp.bfloat16), "mp", scatter_dimension=0, tiled=True
    ).astype(jnp.float32)
    own_hidden = lax.dynamic_slice_in_dim(hidden, res_start, res_rows, 0).astype(jnp.float32)
    return (own_hidden + share).astype(jnp.bfloat16)


BF16 = jnp.bfloat16
F32 = jnp.float32
VMEM_SPEC = pl.BlockSpec(memory_space=pltpu.VMEM)
HBM_SPEC = pl.BlockSpec(memory_space=pl.ANY)
SMALL_MIB = 12
STAGE_AT = ((0, 1, 2), (3, 4), (5,), ())
GATE_RING = 2
DOWN_RING = 4
EXPERTS_MIB = 27


def swap(array, axis_name, mask):
    count = lax.axis_size(axis_name)
    return lax.ppermute(array, axis_name, [(i, i ^ mask) for i in range(count)])


def spread(arrays, axis_name, unit=1):
    masks = range(unit, unit * (len(arrays) + 1), unit)
    moved = [swap(array, axis_name, mask) for mask, array in reversed(list(zip(masks, arrays)))]
    return moved[::-1]


def device_call(kernel, name, outs, arrays, scratch=(), flops=0, limit=SMALL_MIB, specs=None, moved=0):
    moved = moved or sum(a.size * a.dtype.itemsize for a in arrays)
    return pl.pallas_call(
        kernel,
        out_shape=outs,
        in_specs=specs or [VMEM_SPEC] * len(arrays),
        out_specs=jax.tree.map(lambda _: VMEM_SPEC, outs),
        scratch_shapes=list(scratch),
        compiler_params=pltpu.CompilerParams(vmem_limit_bytes=limit << 20),
        cost_estimate=pl.CostEstimate(flops=flops, bytes_accessed=moved, transcendentals=0),
        name=name,
    )(*arrays)


def in_hbm(array):
    return pltpu.with_memory_space_constraint(array, pltpu.HBM)


def in_vmem(array):
    return pltpu.with_memory_space_constraint(array, pltpu.VMEM)


def like(shape, dtype=BF16):
    return jax.ShapeDtypeStruct(shape, dtype)


def expert_at(shape, ctx_at):
    ctx_count, mp_count = shape
    mp_index = lax.axis_index("mp")
    own = lax.div((mp_index * ctx_count + ctx_at) * EXPERTS, ctx_count * mp_count)
    return own - lax.div(mp_index * EXPERTS, mp_count)


def tables_kernel(shape, ids_ref, logits_ref, pick_ref, high_ref, low_ref):
    mp_index = lax.axis_index("mp")
    mp_count = shape[1]
    per_row, capacity, tokens = pick_ref.shape
    rows = tokens // mp_count
    first = lax.div(mp_index * EXPERTS, mp_count)
    lane = lax.broadcasted_iota(jnp.int32, (1, tokens), 1)

    def by_block(values):
        for bit in range(mp_count.bit_length() - 1):
            size = rows << bit
            forward = pltpu.roll(values, size, 1)
            back = pltpu.roll(values, tokens - size, 1)
            moved = jnp.where((lane & size) != 0, forward, back)
            values = jnp.where(((mp_index >> bit) & 1) == 1, moved, values)
        return values

    logits = logits_ref[...]
    weights = jnp.exp(logits - jnp.max(logits, axis=0, keepdims=True))
    weights = weights / jnp.sum(weights, axis=0, keepdims=True)
    ids = ids_ref[...]
    earlier = lax.broadcasted_iota(jnp.int32, (tokens, tokens), 0) < lax.broadcasted_iota(
        jnp.int32, (tokens, tokens), 1
    )
    earlier = earlier.astype(F32).astype(BF16)
    for which in range(per_row):
        named = (ids == first + which).astype(F32)
        member = jnp.max(named, axis=0, keepdims=True)
        weight = jnp.sum(named * weights, axis=0, keepdims=True)
        slot = jnp.dot(
            jnp.broadcast_to(member, (8, tokens)).astype(BF16), earlier, preferred_element_type=F32
        )[0:1]
        slot = by_block(jnp.where(member > 0, slot, float(capacity)))
        weight = by_block(weight)
        taken = lax.broadcasted_iota(jnp.int32, (capacity, tokens), 0) == slot.astype(jnp.int32)
        pick_ref[which] = jnp.where(taken, 1.0, 0.0).astype(BF16)
        weight = jnp.where(taken, weight, 0.0)
        high = weight.astype(BF16)
        high_ref[which] = high
        low_ref[which] = (weight - high.astype(F32)).astype(BF16)


def attention_kernel(*refs):
    half = len(refs) - 8 - 1 - 3
    query_refs = refs[:half]
    own_k, own_v, new_k, new_v, pair_k, pair_v, pair_nk, pair_nv = refs[half : half + 8]
    mine_ref, query_buf, key_buf, value_buf = refs[half + 8 :]
    own = lax.axis_index("ctx")
    slots, _, head_dim = own_k.shape
    tok_local = new_k.shape[1]
    rows = half * tok_local
    group = query_refs[0].shape[1] // head_dim // slots
    heads = slots * group
    factor = math.log2(math.e) / math.sqrt(head_dim)
    for at, query_ref in enumerate(query_refs):
        for head in range(heads):
            start = (head % group) * rows + at * tok_local
            query_buf[head // group, start : start + tok_local, :] = query_ref[
                :, head * head_dim : (head + 1) * head_dim
            ]
    for part, (key_ref, value_ref) in enumerate(((new_k, new_v), (pair_nk, pair_nv))):
        for slot in range(slots):
            key_buf[slot, part * tok_local : (part + 1) * tok_local, :] = key_ref[slot]
            value_buf[slot, part * tok_local : (part + 1) * tok_local, :] = value_ref[slot]
    row = lax.rem(lax.broadcasted_iota(jnp.int32, (group * rows, 1), 0), rows)
    block = lax.div(row, tok_local)
    row_tok = (own ^ (2 * block)) * tok_local + row - block * tok_local
    column = lax.broadcasted_iota(jnp.int32, (1, 2 * tok_local), 1)
    block = lax.div(column, tok_local)
    key_tok = (own ^ block) * tok_local + column - block * tok_local
    seen = key_tok <= row_tok
    lane = lax.broadcasted_iota(jnp.int32, (rows, head_dim), 1)
    stats = jnp.zeros((rows, head_dim), F32)

    def product(left, right):
        return lax.dot_general(left, right, (((1,), (1,)), ((), ())), preferred_element_type=F32)

    for slot in range(slots):
        query = query_buf[slot]
        first = product(query, own_k[slot]) * factor
        second = product(query, pair_k[slot]) * factor
        third = jnp.where(seen, product(query, key_buf[slot]) * factor, neg_big)
        top = jnp.maximum(
            jnp.max(jnp.maximum(first, second), axis=1, keepdims=True),
            jnp.max(third, axis=1, keepdims=True),
        )
        shift = top.astype(BF16).astype(F32)
        first = jnp.exp2(first - shift)
        second = jnp.exp2(second - shift)
        third = jnp.exp2(third - shift)
        denom = jnp.sum(first + second, axis=1, keepdims=True) + jnp.sum(third, axis=1, keepdims=True)
        summed = jnp.dot(first.astype(BF16), own_v[slot], preferred_element_type=F32)
        summed += jnp.dot(second.astype(BF16), pair_v[slot], preferred_element_type=F32)
        summed += jnp.dot(third.astype(BF16), value_buf[slot], preferred_element_type=F32)
        summed = summed.astype(BF16)
        high = denom.astype(BF16).astype(F32)
        low = denom - high
        for index in range(group):
            head = slot * group + index
            span = slice(index * rows, (index + 1) * rows)
            mine_ref[head] = summed[span]
            stats = jnp.where(lane == head, shift[span], stats)
            stats = jnp.where(lane == heads + head, high[span], stats)
            stats = jnp.where(lane == 2 * heads + head, low[span], stats)
    mine_ref[heads] = stats.astype(BF16)


def join_kernel(*refs):
    part_refs, attn_ref = refs[:-1], refs[-1]
    half = len(part_refs)
    heads, head_dim = part_refs[0].shape[0] - 1, part_refs[0].shape[2]
    tok = part_refs[0].shape[1] // half
    for block in range(half):
        spans = [slice((k ^ block) * tok, ((k ^ block) + 1) * tok) for k in range(half)]
        stats = [ref[heads, span, :].astype(F32) for ref, span in zip(part_refs, spans)]
        highest = functools.reduce(jnp.maximum, stats)
        lifts = [jnp.exp2(stat - highest) for stat in stats]
        denoms = [
            pltpu.roll(stat, head_dim - heads, 1) + pltpu.roll(stat, head_dim - 2 * heads, 1)
            for stat in stats
        ]
        total = sum(lift * denom for lift, denom in zip(lifts, denoms))
        shares = [lift / total for lift in lifts]
        for head in range(heads):
            mixed = sum(
                share[:, head : head + 1] * ref[head, span, :].astype(F32)
                for share, ref, span in zip(shares, part_refs, spans)
            )
            attn_ref[block * tok : (block + 1) * tok, head * head_dim : (head + 1) * head_dim] = mixed.astype(BF16)


def project_kernel(own_ref, pair_ref, weight_ref, kept_ref, *refs):
    sent_refs, left = refs[:-1], refs[-1]
    ctx_index, mp_index = lax.axis_index("ctx"), lax.axis_index("mp")
    mp_count = len(sent_refs) + 1
    tok = own_ref.shape[0] // mp_count
    odd = ctx_index & 1
    pair_at = (ctx_index >> 1) ^ mp_index
    for k in range(mp_count):
        source = pl.ds(pl.multiple_of((pair_at ^ k) * tok, tok), tok)
        left[pl.ds(pl.multiple_of((2 * k + odd) * tok, tok), tok), :] = own_ref[source, :]
        left[pl.ds(pl.multiple_of((2 * k + 1 - odd) * tok, tok), tok), :] = pair_ref[source, :]
    projected = jnp.dot(left[...], weight_ref[...], preferred_element_type=F32)
    kept_ref[...] = projected[: 2 * tok]
    for k, ref in enumerate(sent_refs, 1):
        ref[...] = projected[2 * k * tok : 2 * (k + 1) * tok].astype(BF16)


def total_kernel(*refs):
    total = refs[0][...].astype(F32)
    for ref in refs[1:-1]:
        total = total + ref[...].astype(F32)
    refs[-1][...] = total.astype(BF16)


def pack_kernel(shape, pick_ref, *refs):
    mp_count, half = shape[1], shape[0] // 2
    hidden_refs, out_refs, packed = refs[:mp_count], refs[mp_count:-1], refs[-1]
    hidden = jnp.concatenate([ref[...] for ref in hidden_refs], axis=0)
    for which in range(pick_ref.shape[0]):
        packed[which] = jnp.dot(pick_ref[which], hidden, preferred_element_type=F32).astype(BF16)
    for k in range(half):
        out_refs[k][...] = packed[expert_at(shape, lax.axis_index("ctx") ^ (2 * k))]


def block_rows(step, deep):
    return pl.ds(pl.multiple_of((lax.axis_index("ctx") ^ step) * deep, deep), deep)


def stage_copies(steps, gate_hbm, up_hbm, outs, sem):
    copies = []
    for at, step in enumerate(steps):
        rows = block_rows(step, outs[0].shape[0])
        copies.append(pltpu.make_async_copy(gate_hbm.at[0, rows, :], outs[2 * at], sem.at[2 * at]))
        copies.append(pltpu.make_async_copy(up_hbm.at[0, rows, :], outs[2 * at + 1], sem.at[2 * at + 1]))
    return copies


def stage_kernel(steps, *refs):
    gate_hbm, up_hbm = refs[:2]
    extra = (len(refs) - 4 - 2 * len(steps)) // 2
    plain, outs = refs[2 : 2 + extra], refs[2 + extra : -2 - extra]
    plain_out, sem, plain_sem = refs[-2 - extra : -2], refs[-2], refs[-1]
    copies = [
        pltpu.make_async_copy(source, target, plain_sem.at[at])
        for at, (source, target) in enumerate(zip(plain, plain_out))
    ]
    copies += stage_copies(steps, gate_hbm, up_hbm, outs, sem)
    for copy in copies:
        copy.start()
    for copy in copies:
        copy.wait()


def staged_like(steps, deep, units):
    return (pltpu.VMEM((deep, units), BF16),) * (2 * len(steps))


def stage(gate_proj, up_proj, deep, steps, *plain):
    units = gate_proj.shape[2]
    return pl.pallas_call(
        functools.partial(stage_kernel, steps),
        out_shape=staged_like(steps, deep, units) + tuple(pltpu.VMEM(a.shape, a.dtype) for a in plain),
        in_specs=[HBM_SPEC] * (2 + len(plain)),
        out_specs=(VMEM_SPEC,) * (2 * len(steps) + len(plain)),
        scratch_shapes=[
            pltpu.SemaphoreType.DMA((max(1, 2 * len(steps)),)),
            pltpu.SemaphoreType.DMA((max(1, len(plain)),)),
        ],
        compiler_params=pltpu.CompilerParams(vmem_limit_bytes=2 << 20),
        cost_estimate=pl.CostEstimate(flops=0, bytes_accessed=4 * len(steps) * deep * units, transcendentals=0),
        name="stage",
    )(gate_proj, up_proj, *plain)


def scaled_rows(row_ref, gain_ref, step):
    wide = row_ref[...].astype(F32)
    squares = jnp.sum(wide * wide, axis=1, keepdims=True)
    return squares, (wide * gain_ref[lax.axis_index("ctx") ^ step]).astype(BF16)


def early_kernel(count, steps, *refs):
    row_refs, gain_ref, weight_refs, refs = refs[:count], refs[count], refs[count + 1 : 3 * count + 1], refs[3 * count + 1 :]
    gate_hbm, up_hbm, gate_acc, up_acc, squares_ref = refs[:5]
    copies = stage_copies(steps, gate_hbm, up_hbm, refs[5:-1], refs[-1]) if steps else []
    for copy in copies:
        copy.start()
    squares = 0.0
    for step in range(count):
        more, rows = scaled_rows(row_refs[step], gain_ref, step)
        squares = squares + more
        for acc, weights in ((gate_acc, weight_refs[2 * step]), (up_acc, weight_refs[2 * step + 1])):
            term = jnp.dot(rows, weights[...], preferred_element_type=F32)
            acc[...] = term if step == 0 else acc[...] + term
    squares_ref[...] = jnp.broadcast_to(squares, squares_ref.shape)
    for copy in copies:
        copy.wait()


def experts_kernel(first, held, count, *refs):
    own_rows = count - first
    row_refs, gain_ref = refs[:own_rows], refs[own_rows]
    weight_refs, refs = refs[own_rows + 1 : own_rows + 1 + 2 * held], refs[own_rows + 1 + 2 * held :]
    gate_in, up_in, squares_ref, gate_hbm, up_hbm, down_hbm, even_ref, odd_ref, act_ref = refs[:9]
    gate_acc, up_acc, pair_acc, gate_buf, up_buf, down_buf, gate_sem, down_sem = refs[9:]
    own = lax.axis_index("ctx")
    half = count // 2
    deep = row_refs[0].shape[1]
    units = gate_acc.shape[1]
    late = list(range(first + held, count))
    gate_ring, down_ring, down_rows = gate_buf.shape[0], down_buf.shape[0], down_buf.shape[1]
    parts = units // down_rows

    def gate_copies(at):
        rows, slot = block_rows(late[at], deep), at % gate_ring
        return (
            pltpu.make_async_copy(gate_hbm.at[0, rows, :], gate_buf.at[slot], gate_sem.at[0, slot]),
            pltpu.make_async_copy(up_hbm.at[0, rows, :], up_buf.at[slot], gate_sem.at[1, slot]),
        )

    down = [
        down_copy(down_hbm, down_buf.at[at % down_ring], down_sem.at[at % down_ring], 1 + at // parts, at % parts)
        for at in range((half - 1) * parts)
    ]
    for at in range(min(gate_ring, len(late))):
        for copy in gate_copies(at):
            copy.start()
    if len(late) <= gate_ring:
        for copy in down[:down_ring]:
            copy.start()
    squares = squares_ref[:, 0:1]
    gate_acc[...] = gate_in[...]
    up_acc[...] = up_in[...]
    for step in range(first, count):
        more, rows = scaled_rows(row_refs[step - first], gain_ref, step)
        squares = squares + more
        if step < first + held:
            gate_w, up_w = weight_refs[2 * (step - first)], weight_refs[2 * (step - first) + 1]
        else:
            at = step - first - held
            for copy in gate_copies(at):
                copy.wait()
            gate_w, up_w = gate_buf.at[at % gate_ring], up_buf.at[at % gate_ring]
        gate_acc[...] += jnp.dot(rows, gate_w[...], preferred_element_type=F32)
        up_acc[...] += jnp.dot(rows, up_w[...], preferred_element_type=F32)
        if step >= first + held and at + gate_ring < len(late):
            for copy in gate_copies(at + gate_ring):
                copy.start()
            if at + gate_ring == len(late) - 1:
                for copy in down[:down_ring]:
                    copy.start()
    rms = lax.rsqrt(squares / D + norm_eps)
    gate = rms * gate_acc[...]
    act_ref[...] = (gate / (1.0 + jnp.exp(-gate)) * (rms * up_acc[...])).astype(BF16)
    odd = own & 1
    for at, copy in enumerate(down):
        part = at % parts
        copy.wait()
        term = jnp.dot(
            act_ref[:, part * down_rows : (part + 1) * down_rows],
            down_buf[at % down_ring],
            preferred_element_type=F32,
        )
        pair_acc[...] = term if part == 0 else pair_acc[...] + term
        if at + down_ring < len(down):
            down[at + down_ring].start()
        if part == parts - 1:
            store_pair(pair_acc, even_ref.at[at // parts], odd_ref.at[at // parts], odd)


def down_copy(down_hbm, target, sem, chip, part):
    rows, columns = target.shape
    start = pl.multiple_of(((lax.axis_index("ctx") >> 1) ^ chip) * columns, columns)
    return pltpu.make_async_copy(
        down_hbm.at[0, part * rows : (part + 1) * rows, pl.ds(start, columns)], target, sem
    )


def store_pair(pair_acc, even_ref, odd_ref, odd):
    deep = even_ref.shape[1]
    even_ref[...] = pair_acc[:, pl.ds(pl.multiple_of(odd * deep, deep), deep)].astype(BF16)
    odd_ref[...] = pair_acc[:, pl.ds(pl.multiple_of((1 - odd) * deep, deep), deep)].astype(BF16)


def own_columns_kernel(act_ref, down_hbm, even_ref, odd_ref, pair_acc, down_buf, down_sem):
    parts, down_rows = down_buf.shape[0], down_buf.shape[1]
    copies = [down_copy(down_hbm, down_buf.at[part], down_sem.at[part], 0, part) for part in range(parts)]
    for copy in copies:
        copy.start()
    for part, copy in enumerate(copies):
        copy.wait()
        term = jnp.dot(
            act_ref[:, part * down_rows : (part + 1) * down_rows], down_buf[part], preferred_element_type=F32
        )
        pair_acc[...] = term if part == 0 else pair_acc[...] + term
    store_pair(pair_acc, even_ref, odd_ref, lax.axis_index("ctx") & 1)


def run_early(rows, gain, staged, steps, gate_proj, up_proj):
    tokens, deep = rows[0].shape
    units = gate_proj.shape[2]
    acc = pltpu.VMEM((tokens, units), F32)
    outs = (acc, acc, pltpu.VMEM((tokens, 128), F32)) + (staged_like(steps, deep, units) if steps else ())
    return pl.pallas_call(
        functools.partial(early_kernel, len(rows), steps),
        out_shape=outs,
        in_specs=[VMEM_SPEC] * (len(rows) + 1 + len(staged)) + [HBM_SPEC] * 2,
        out_specs=(VMEM_SPEC,) * len(outs),
        scratch_shapes=[pltpu.SemaphoreType.DMA((2 * len(steps),))] if steps else [],
        compiler_params=pltpu.CompilerParams(vmem_limit_bytes=5 << 20),
        cost_estimate=pl.CostEstimate(
            flops=4 * tokens * deep * units * len(rows),
            bytes_accessed=4 * len(steps) * deep * units,
            transcendentals=0,
        ),
        name="early",
    )(*rows, gain, *[in_vmem(array) for array in staged], gate_proj, up_proj)


def run_experts(rows, first, gain, staged, sums, gate_proj, up_proj, down_proj):
    tokens, deep = rows[0].shape
    count = first + len(rows)
    units = gate_proj.shape[2]
    parts = 2
    weights = 2 * (2 * gate_proj.size + down_proj.size)
    pieces = like((count // 2 - 1, tokens, deep))
    return pl.pallas_call(
        functools.partial(experts_kernel, first, len(staged) // 2, count),
        out_shape=(pieces, pieces, pltpu.VMEM((tokens, units), BF16)),
        in_specs=[VMEM_SPEC] * (len(rows) + 1 + len(staged) + 3) + [HBM_SPEC] * 3,
        out_specs=(VMEM_SPEC,) * 3,
        scratch_shapes=[
            pltpu.VMEM((tokens, units), F32),
            pltpu.VMEM((tokens, units), F32),
            pltpu.VMEM((tokens, 2 * deep), F32),
            pltpu.VMEM((GATE_RING, deep, units), BF16),
            pltpu.VMEM((GATE_RING, deep, units), BF16),
            pltpu.VMEM((DOWN_RING, units // parts, 2 * deep), BF16),
            pltpu.SemaphoreType.DMA((2, GATE_RING)),
            pltpu.SemaphoreType.DMA((DOWN_RING,)),
        ],
        compiler_params=pltpu.CompilerParams(vmem_limit_bytes=EXPERTS_MIB << 20),
        cost_estimate=pl.CostEstimate(flops=tokens * weights, bytes_accessed=weights // 2, transcendentals=tokens * units),
        name="experts",
    )(*rows, gain, *[in_vmem(array) for array in staged], *sums, gate_proj, up_proj, down_proj)


def pair_total_kernel(even_ref, other_ref, *out_refs):
    for k, ref in enumerate(out_refs):
        ref[...] = (even_ref[k].astype(F32) + other_ref[k].astype(F32)).astype(BF16)


def combine_kernel(shape, high_ref, low_ref, *refs):
    half, mp_count = shape[0] // 2, shape[1]
    piece_refs, even_ref, other_ref = refs[: half - 1], refs[half - 1], refs[half]
    kept_ref, sent_refs = refs[half + 1], refs[half + 2 :]
    own_piece = (even_ref[...].astype(F32) + other_ref[...].astype(F32)).astype(BF16)
    pieces = jnp.concatenate([own_piece] + [ref[...] for ref in piece_refs], axis=0)
    experts = [expert_at(shape, lax.axis_index("ctx") ^ (2 * k)) for k in range(half)]
    total = None
    for table in (high_ref, low_ref):
        spread = jnp.concatenate([table[expert] for expert in experts], axis=0)
        term = lax.dot_general(spread, pieces, (((0,), (0,)), ((), ())), preferred_element_type=F32)
        total = term if total is None else total + term
    rows = kept_ref.shape[0]
    kept_ref[...] = total[:rows]
    for k, ref in enumerate(sent_refs, 1):
        ref[...] = total[k * rows : (k + 1) * rows].astype(BF16)


def exchange_path(
    queries,
    cache_keys,
    cache_values,
    new_keys,
    new_values,
    out_proj,
    residual,
    norm_gain,
    gate_proj,
    up_proj,
    down_proj,
    expert_ids,
    route_logits,
):
    ctx_count = lax.axis_size("ctx")
    mp_count = lax.axis_size("mp")
    shape = (ctx_count, mp_count)
    gate_hbm, up_hbm, down_hbm = in_hbm(gate_proj), in_hbm(up_proj), in_hbm(down_proj)
    tok_local = queries.shape[0]
    tokens = tok_local * ctx_count
    slot_local, cache_local, head_dim = cache_keys.shape
    heads = queries.shape[1] // head_dim
    d_local = out_proj.shape[1]
    res_rows = residual.shape[0]
    half = ctx_count // 2
    rows = half * tok_local
    capacity = tokens * TOP // 4
    per_row = max(1, EXPERTS // mp_count)

    blocks = [queries] + spread([queries] * (half - 1), "ctx", 2)
    own = [cache_keys, cache_values, new_keys, new_values]
    pair = [swap(array, "ctx", 1) for array in own]
    held = stage(gate_hbm, up_hbm, d_local, (), *[in_hbm(array) for array in (*own, queries)])
    held, blocks[1:], pair = lax.optimization_barrier((held, blocks[1:], pair))
    mine = device_call(
        attention_kernel,
        "attention",
        like((heads + 1, rows, head_dim)),
        [in_vmem(array) for array in (held[4], *blocks[1:], *held[:4], *pair)],
        [
            pltpu.VMEM((slot_local, heads // slot_local * rows, head_dim), BF16),
            pltpu.VMEM((slot_local, 2 * tok_local, head_dim), BF16),
            pltpu.VMEM((slot_local, 2 * tok_local, head_dim), BF16),
        ],
        flops=8 * heads * rows * (cache_local + tok_local) * head_dim,
        limit=24,
    )
    others = spread([mine] * (half - 1), "ctx", 2)
    ids, logits, _ = lax.optimization_barrier((expert_ids.T, route_logits.T, mine))
    pick, high, low = device_call(
        functools.partial(tables_kernel, shape),
        "tables",
        (like((per_row, capacity, tokens)),) * 3,
        [ids, logits],
    )
    gain = norm_gain.astype(F32).reshape(ctx_count, 1, d_local)
    gate_later, _ = lax.optimization_barrier((gate_proj, mine))
    *staged, out_proj, residual = stage(
        in_hbm(gate_later), up_hbm, d_local, STAGE_AT[0], in_hbm(out_proj), in_hbm(residual)
    )
    pick, high, low, gain, staged, out_proj, residual, others = lax.optimization_barrier(
        (pick, high, low, gain, staged, out_proj, residual, others)
    )
    attn = device_call(join_kernel, "join", like((rows, heads * head_dim)), [mine] + others)
    block = like((res_rows, d_local))

    kept, *sent = device_call(
        project_kernel,
        "project",
        (like((res_rows, d_local), F32),) + (block,) * (mp_count - 1),
        [attn, swap(attn, "ctx", 1), out_proj],
        [pltpu.VMEM((tokens, heads * head_dim), BF16)],
        flops=2 * tokens * heads * head_dim * d_local,
    )
    arrived = spread(sent, "mp")
    gate_later, _ = lax.optimization_barrier((gate_proj, kept))
    more = stage(in_hbm(gate_later), up_hbm, d_local, STAGE_AT[1])
    more, arrived = lax.optimization_barrier((more, arrived))
    staged = [*staged, *more]
    hidden = device_call(total_kernel, "hidden", block, [kept, residual] + arrived[::-1])

    everyone = spread([hidden] * (mp_count - 1), "mp")
    gate_later, _ = lax.optimization_barrier((gate_proj, hidden))
    more = stage(in_hbm(gate_later), up_hbm, d_local, STAGE_AT[2])
    more, everyone = lax.optimization_barrier((more, everyone))
    staged, everyone = [*staged, *more], [hidden, *everyone]
    even = device_call(
        functools.partial(pack_kernel, shape),
        "pack",
        (like((capacity, d_local)),) * half,
        [pick] + everyone,
        [pltpu.VMEM((per_row, capacity, d_local), BF16)],
    )
    even = [even[0]] + spread(even[1:], "ctx", 2)
    first = [even[0], swap(even[0], "ctx", 1)]
    sums = run_early(first, gain, staged[:4], STAGE_AT[3], gate_hbm, up_hbm)
    sums, even = lax.optimization_barrier((sums, even[1:]))
    gate_sum, up_sum, squares, *more = sums
    arrived = [array for piece in even for array in (piece, swap(piece, "ctx", 1))]
    out_even, out_odd, act = run_experts(
        arrived, 2, gain, [*staged[4:], *more], (gate_sum, up_sum, squares), gate_hbm, up_hbm, down_hbm
    )
    pieces = device_call(
        pair_total_kernel,
        "pair_total",
        (like((capacity, d_local)),) * (half - 1),
        [out_even, swap(out_odd, "ctx", 1)],
    )
    act, *pieces = lax.optimization_barrier((act, *pieces))
    returned = spread(pieces, "ctx", 2)
    own_even, own_odd = device_call(
        own_columns_kernel,
        "own_columns",
        (like((capacity, d_local)),) * 2,
        [act, down_hbm],
        [
            pltpu.VMEM((capacity, 2 * d_local), F32),
            pltpu.VMEM((2, act.shape[1] // 2, 2 * d_local), BF16),
            pltpu.SemaphoreType.DMA((2,)),
        ],
        specs=[VMEM_SPEC, HBM_SPEC],
        moved=1,
    )
    pieces = returned + [own_even, swap(own_odd, "ctx", 1)]
    kept, *sent = device_call(
        functools.partial(combine_kernel, shape),
        "combine",
        (like((res_rows, d_local), F32),) + (block,) * (mp_count - 1),
        [high, low] + pieces,
    )
    arrived = spread(sent, "mp")
    return device_call(total_kernel, "layer_out", block, [kept, hidden] + arrived[::-1])


def on_device(*args):
    queries, cache_keys, out_proj, gate_proj, down_proj = (args[i] for i in (0, 1, 5, 8, 10))
    ctx_count, mp_count = lax.axis_size("ctx"), lax.axis_size("mp")
    per_row = max(1, EXPERTS // mp_count)
    fits = (
        ctx_count == 2 * mp_count
        and ctx_count & (ctx_count - 1) == 0
        and (ctx_count // per_row) % 2 == 0
        and out_proj.shape[1] % 256 == 0
        and gate_proj.shape[2] % 2048 == 0
        and queries.shape[0] % 16 == 0
        and 3 * (queries.shape[1] // cache_keys.shape[2]) <= cache_keys.shape[2]
    )
    return exchange_path(*args) if fits else gathered_path(*args)


def solution(mesh):
    placed = (
        P("ctx", "mp"),
        P("mp", "ctx", None),
        P("mp", "ctx", None),
        P("mp", "ctx", None),
        P("mp", "ctx", None),
        P("mp", "ctx"),
        P("mp", "ctx"),
        P(),
        P("ctx", None, "mp"),
        P("ctx", None, "mp"),
        P("ctx", "mp", None),
        P(),
        P(),
    )
    return jax.shard_map(
        on_device, mesh=mesh, in_specs=placed, out_specs=P("mp", "ctx"), check_vma=False
    )
```

```python
import functools
import math

import jax
import jax.numpy as jnp
from jax import lax
from jax.experimental import pallas as pl
from jax.experimental.pallas import tpu as pltpu
from jax.sharding import PartitionSpec as P

D = 6144
EXPERTS = 8
TOP = 2


neg_big = -1e30
norm_eps = 1e-05


def route_slots(expert_ids):
    flat = expert_ids.reshape(-1)
    onehot = (flat[:, None] == jnp.arange(EXPERTS, dtype=jnp.int32)[None, :]).astype(jnp.int32)
    before = jnp.cumsum(onehot, axis=0, dtype=jnp.int32) - onehot
    return jnp.sum(before * onehot, axis=1, dtype=jnp.int32).reshape(expert_ids.shape)


def softmax_pieces(query_block, keys_local, values_local, allowed, scale):
    scores = (
        jnp.einsum("srd,skd->srk", query_block, keys_local, preferred_element_type=jnp.float32)
        * scale
    )
    scores = jnp.where(allowed[None, :, :], scores, neg_big)
    highest = jnp.max(scores, axis=2)
    expo = jnp.exp(scores - highest[:, :, None])
    denom = jnp.sum(expo, axis=2)
    summed = jnp.einsum(
        "srk,skd->srd", expo.astype(jnp.bfloat16), values_local, preferred_element_type=jnp.float32
    )
    return (highest, denom, summed)


def join_softmax(former, latter):
    highest = jnp.maximum(former[0], latter[0])
    right = jnp.exp(latter[0] - highest)
    denom = latter[1] * right
    summed = latter[2] * right[:, :, None]
    return (highest, denom, summed)


def gathered_path(
    queries,
    cache_keys,
    cache_values,
    new_keys,
    new_values,
    out_proj,
    residual,
    norm_gain,
    gate_proj,
    up_proj,
    down_proj,
    expert_ids,
    route_logits,
):
    ctx_count = lax.axis_size("ctx")
    mp_count = lax.axis_size("mp")
    ctx_index = lax.axis_index("ctx")
    mp_index = lax.axis_index("mp")
    tok_local = queries.shape[0]
    tokens = tok_local * ctx_count
    slot_local = cache_keys.shape[0]
    cache_local = cache_keys.shape[1]
    head_dim = cache_keys.shape[2]
    heads_local = queries.shape[1] // head_dim
    group_size = heads_local // slot_local
    width = cache_local + tok_local
    scale = 1.0 / math.sqrt(head_dim)
    d_local = out_proj.shape[1]
    key_value = jnp.stack(
        [
            jnp.concatenate([cache_keys, new_keys], axis=1),
            jnp.concatenate([cache_values, new_values], axis=1),
        ]
    )
    shaped = queries.reshape(tok_local, slot_local, group_size, head_dim)
    query_block = jnp.transpose(shaped, (1, 2, 0, 3)).reshape(
        slot_local, group_size * tok_local, head_dim
    )
    query_tok = ctx_index * tok_local + jnp.tile(jnp.arange(tok_local, dtype=jnp.int32), group_size)
    query_count = group_size * tok_local
    start_state = (
        jnp.full((slot_local, query_count), neg_big, jnp.float32),
        jnp.zeros((slot_local, query_count), jnp.float32),
        jnp.zeros((slot_local, query_count, head_dim), jnp.float32),
    )
    piece = lax.all_gather(key_value, "ctx", axis=2, tiled=True)
    position = jnp.arange(piece.shape[2], dtype=jnp.int32)
    shard = position // width
    within = position % width
    new_tok = shard * tok_local + within - cache_local
    allowed = (within[None, :] < cache_local) | (new_tok[None, :] <= query_tok[:, None])
    highest, denom, summed = join_softmax(
        start_state, softmax_pieces(query_block, piece[0], piece[1], allowed, scale)
    )
    shaped = (
        (summed / denom[:, :, None])
        .astype(jnp.bfloat16)
        .reshape(slot_local, group_size, tok_local, head_dim)
    )
    attn = jnp.transpose(shaped, (2, 0, 1, 3)).reshape(tok_local, heads_local * head_dim)
    projected = jnp.dot(
        lax.all_gather(attn, "ctx", axis=0, tiled=True),
        out_proj,
        preferred_element_type=jnp.float32,
    )
    res_rows = residual.shape[0]
    res_start = mp_index * res_rows
    current = lax.dynamic_slice_in_dim(projected, res_start, res_rows, 0)
    projected = lax.dynamic_update_slice_in_dim(
        projected, current + residual.astype(jnp.float32), res_start, 0
    )
    hidden = lax.psum(projected.astype(jnp.bfloat16), "mp")
    capacity = tokens * TOP // 4
    slots = route_slots(expert_ids)
    per_row = max(1, EXPERTS // mp_count)
    first_expert = mp_index * EXPERTS // mp_count
    own_expert = (mp_index * ctx_count + ctx_index) * EXPERTS // (ctx_count * mp_count)
    local = own_expert - first_expert
    row_experts = first_expert + jnp.arange(per_row, dtype=jnp.int32)
    match = expert_ids[None, :, :] == row_experts[:, None, None]
    place = jnp.where(match, slots[None, :, :], capacity)
    table = place[:, :, :, None] == jnp.arange(capacity, dtype=jnp.int32)[None, None, None, :]
    pick = jnp.any(table, axis=2)
    packed = jnp.einsum(
        "rtc,td->rcd", pick.astype(jnp.bfloat16), hidden, preferred_element_type=jnp.float32
    ).astype(jnp.bfloat16)
    gate_local = gate_proj[0]
    up_local = up_proj[0]
    down_local = down_proj[0]
    chosen = lax.dynamic_index_in_dim(
        lax.all_gather(packed, "ctx", axis=2, tiled=True), local, 0, keepdims=False
    )
    wide = chosen.astype(jnp.float32)
    gains = norm_gain.astype(jnp.float32)
    scaled = (wide * gains[None, :]).astype(jnp.bfloat16)
    gate_sum = jnp.dot(scaled, gate_local, preferred_element_type=jnp.float32)
    up_sum = jnp.dot(scaled, up_local, preferred_element_type=jnp.float32)
    gate_sum, up_sum, squares = (gate_sum, up_sum, jnp.sum(wide * wide, axis=1))
    rms = lax.rsqrt(squares / D + norm_eps)
    act = (jax.nn.silu(rms[:, None] * gate_sum) * (rms[:, None] * up_sum)).astype(jnp.bfloat16)
    part = lax.dot_general(
        down_local, act, (((0,), (1,)), ((), ())), preferred_element_type=jnp.float32
    )
    returned = lax.psum_scatter(
        jnp.concatenate(
            [jnp.where(local == which, part, 0.0) for which in range(per_row)], axis=1
        ).astype(jnp.bfloat16),
        "ctx",
        scatter_dimension=0,
        tiled=True,
    ).astype(jnp.float32)
    weights = jax.nn.softmax(route_logits, axis=1)
    combine = jnp.sum(jnp.where(table, weights[None, :, :, None], 0.0), axis=2)
    moe = jnp.einsum(
        "drc,rtc->td",
        returned.reshape(d_local, per_row, capacity),
        combine,
        precision=lax.Precision.HIGHEST,
        preferred_element_type=jnp.float32,
    )
    share = lax.psum_scatter(
        moe.astype(jnp.bfloat16), "mp", scatter_dimension=0, tiled=True
    ).astype(jnp.float32)
    own_hidden = lax.dynamic_slice_in_dim(hidden, res_start, res_rows, 0).astype(jnp.float32)
    return (own_hidden + share).astype(jnp.bfloat16)


BF16 = jnp.bfloat16
F32 = jnp.float32
VMEM_SPEC = pl.BlockSpec(memory_space=pltpu.VMEM)
HBM_SPEC = pl.BlockSpec(memory_space=pl.ANY)
SMALL_MIB = 12
STAGE_AT = ((0, 1, 2), (4, 6), (3,), (7,), (5,))
GATE_RING = 1
DOWN_RING = 5
DOWN_FLIGHT = 3
EXPERTS_MIB = 19


def swap(array, axis_name, mask):
    count = lax.axis_size(axis_name)
    return lax.ppermute(array, axis_name, [(i, i ^ mask) for i in range(count)])


def spread(arrays, axis_name, unit=1):
    masks = range(unit, unit * (len(arrays) + 1), unit)
    moved = [swap(array, axis_name, mask) for mask, array in reversed(list(zip(masks, arrays)))]
    return moved[::-1]


def device_call(kernel, name, outs, arrays, scratch=(), flops=0, limit=SMALL_MIB, specs=None, moved=0):
    moved = moved or sum(a.size * a.dtype.itemsize for a in arrays)
    return pl.pallas_call(
        kernel,
        out_shape=outs,
        in_specs=specs or [VMEM_SPEC] * len(arrays),
        out_specs=jax.tree.map(lambda _: VMEM_SPEC, outs),
        scratch_shapes=list(scratch),
        compiler_params=pltpu.CompilerParams(vmem_limit_bytes=limit << 20),
        cost_estimate=pl.CostEstimate(flops=flops, bytes_accessed=moved, transcendentals=0),
        name=name,
    )(*arrays)


def in_hbm(array):
    return pltpu.with_memory_space_constraint(array, pltpu.HBM)


def in_vmem(array):
    return pltpu.with_memory_space_constraint(array, pltpu.VMEM)


def like(shape, dtype=BF16):
    return jax.ShapeDtypeStruct(shape, dtype)


def expert_at(shape, ctx_at):
    ctx_count, mp_count = shape
    mp_index = lax.axis_index("mp")
    own = lax.div((mp_index * ctx_count + ctx_at) * EXPERTS, ctx_count * mp_count)
    return own - lax.div(mp_index * EXPERTS, mp_count)


def tables_kernel(shape, ids_ref, logits_ref, pick_ref, high_ref, low_ref):
    mp_index = lax.axis_index("mp")
    mp_count = shape[1]
    per_row, capacity, tokens = pick_ref.shape
    rows = tokens // mp_count
    first = lax.div(mp_index * EXPERTS, mp_count)
    lane = lax.broadcasted_iota(jnp.int32, (1, tokens), 1)

    def by_block(values):
        for bit in range(mp_count.bit_length() - 1):
            size = rows << bit
            forward = pltpu.roll(values, size, 1)
            back = pltpu.roll(values, tokens - size, 1)
            moved = jnp.where((lane & size) != 0, forward, back)
            values = jnp.where(((mp_index >> bit) & 1) == 1, moved, values)
        return values

    logits = logits_ref[...]
    weights = jnp.exp(logits - jnp.max(logits, axis=0, keepdims=True))
    weights = weights / jnp.sum(weights, axis=0, keepdims=True)
    ids = ids_ref[...]
    earlier = lax.broadcasted_iota(jnp.int32, (tokens, tokens), 0) < lax.broadcasted_iota(
        jnp.int32, (tokens, tokens), 1
    )
    earlier = earlier.astype(F32).astype(BF16)
    for which in range(per_row):
        named = (ids == first + which).astype(F32)
        member = jnp.max(named, axis=0, keepdims=True)
        weight = jnp.sum(named * weights, axis=0, keepdims=True)
        slot = jnp.dot(
            jnp.broadcast_to(member, (8, tokens)).astype(BF16), earlier, preferred_element_type=F32
        )[0:1]
        slot = by_block(jnp.where(member > 0, slot, float(capacity)))
        weight = by_block(weight)
        taken = lax.broadcasted_iota(jnp.int32, (capacity, tokens), 0) == slot.astype(jnp.int32)
        pick_ref[which] = jnp.where(taken, 1.0, 0.0).astype(BF16)
        weight = jnp.where(taken, weight, 0.0)
        high = weight.astype(BF16)
        high_ref[which] = high
        low_ref[which] = (weight - high.astype(F32)).astype(BF16)


def attention_kernel(*refs):
    half = len(refs) - 8 - 1 - 3
    query_refs = refs[:half]
    own_k, own_v, new_k, new_v, pair_k, pair_v, pair_nk, pair_nv = refs[half : half + 8]
    mine_ref, query_buf, key_buf, value_buf = refs[half + 8 :]
    own = lax.axis_index("ctx")
    slots, _, head_dim = own_k.shape
    tok_local = new_k.shape[1]
    rows = half * tok_local
    group = query_refs[0].shape[1] // head_dim // slots
    heads = slots * group
    factor = math.log2(math.e) / math.sqrt(head_dim)
    for at, query_ref in enumerate(query_refs):
        for head in range(heads):
            start = (head % group) * rows + at * tok_local
            query_buf[head // group, start : start + tok_local, :] = query_ref[
                :, head * head_dim : (head + 1) * head_dim
            ]
    for part, (key_ref, value_ref) in enumerate(((new_k, new_v), (pair_nk, pair_nv))):
        for slot in range(slots):
            key_buf[slot, part * tok_local : (part + 1) * tok_local, :] = key_ref[slot]
            value_buf[slot, part * tok_local : (part + 1) * tok_local, :] = value_ref[slot]
    row = lax.rem(lax.broadcasted_iota(jnp.int32, (group * rows, 1), 0), rows)
    block = lax.div(row, tok_local)
    row_tok = (own ^ (2 * block)) * tok_local + row - block * tok_local
    column = lax.broadcasted_iota(jnp.int32, (1, 2 * tok_local), 1)
    block = lax.div(column, tok_local)
    key_tok = (own ^ block) * tok_local + column - block * tok_local
    seen = key_tok <= row_tok
    lane = lax.broadcasted_iota(jnp.int32, (rows, head_dim), 1)
    stats = jnp.zeros((rows, head_dim), F32)

    def product(left, right):
        return lax.dot_general(left, right, (((1,), (1,)), ((), ())), preferred_element_type=F32)

    for slot in range(slots):
        query = query_buf[slot]
        first = product(query, own_k[slot]) * factor
        second = product(query, pair_k[slot]) * factor
        third = jnp.where(seen, product(query, key_buf[slot]) * factor, neg_big)
        top = jnp.maximum(
            jnp.max(jnp.maximum(first, second), axis=1, keepdims=True),
            jnp.max(third, axis=1, keepdims=True),
        )
        shift = top.astype(BF16).astype(F32)
        first = jnp.exp2(first - shift)
        second = jnp.exp2(second - shift)
        third = jnp.exp2(third - shift)
        denom = jnp.sum(first + second, axis=1, keepdims=True) + jnp.sum(third, axis=1, keepdims=True)
        summed = jnp.dot(first.astype(BF16), own_v[slot], preferred_element_type=F32)
        summed += jnp.dot(second.astype(BF16), pair_v[slot], preferred_element_type=F32)
        summed += jnp.dot(third.astype(BF16), value_buf[slot], preferred_element_type=F32)
        summed = summed.astype(BF16)
        high = denom.astype(BF16).astype(F32)
        low = denom - high
        for index in range(group):
            head = slot * group + index
            span = slice(index * rows, (index + 1) * rows)
            mine_ref[head] = summed[span]
            stats = jnp.where(lane == head, shift[span], stats)
            stats = jnp.where(lane == heads + head, high[span], stats)
            stats = jnp.where(lane == 2 * heads + head, low[span], stats)
    mine_ref[heads] = stats.astype(BF16)


def join_kernel(*refs):
    part_refs, attn_ref = refs[:-1], refs[-1]
    half = len(part_refs)
    heads, head_dim = part_refs[0].shape[0] - 1, part_refs[0].shape[2]
    tok = part_refs[0].shape[1] // half
    for block in range(half):
        spans = [slice((k ^ block) * tok, ((k ^ block) + 1) * tok) for k in range(half)]
        stats = [ref[heads, span, :].astype(F32) for ref, span in zip(part_refs, spans)]
        highest = functools.reduce(jnp.maximum, stats)
        lifts = [jnp.exp2(stat - highest) for stat in stats]
        denoms = [
            pltpu.roll(stat, head_dim - heads, 1) + pltpu.roll(stat, head_dim - 2 * heads, 1)
            for stat in stats
        ]
        total = sum(lift * denom for lift, denom in zip(lifts, denoms))
        shares = [lift / total for lift in lifts]
        for head in range(heads):
            mixed = sum(
                share[:, head : head + 1] * ref[head, span, :].astype(F32)
                for share, ref, span in zip(shares, part_refs, spans)
            )
            attn_ref[block * tok : (block + 1) * tok, head * head_dim : (head + 1) * head_dim] = mixed.astype(BF16)


def project_kernel(own_ref, pair_ref, weight_ref, kept_ref, *refs):
    sent_refs, left = refs[:-1], refs[-1]
    ctx_index, mp_index = lax.axis_index("ctx"), lax.axis_index("mp")
    mp_count = len(sent_refs) + 1
    tok = own_ref.shape[0] // mp_count
    odd = ctx_index & 1
    pair_at = (ctx_index >> 1) ^ mp_index
    for k in range(mp_count):
        source = pl.ds(pl.multiple_of((pair_at ^ k) * tok, tok), tok)
        left[pl.ds(pl.multiple_of((2 * k + odd) * tok, tok), tok), :] = own_ref[source, :]
        left[pl.ds(pl.multiple_of((2 * k + 1 - odd) * tok, tok), tok), :] = pair_ref[source, :]
    projected = jnp.dot(left[...], weight_ref[...], preferred_element_type=F32)
    kept_ref[...] = projected[: 2 * tok]
    for k, ref in enumerate(sent_refs, 1):
        ref[...] = projected[2 * k * tok : 2 * (k + 1) * tok].astype(BF16)


def total_kernel(*refs):
    total = refs[0][...].astype(F32)
    for ref in refs[1:-1]:
        total = total + ref[...].astype(F32)
    refs[-1][...] = total.astype(BF16)


def pack_kernel(shape, pick_ref, *refs):
    mp_count, half = shape[1], shape[0] // 2
    hidden_refs, out_refs, packed = refs[:mp_count], refs[mp_count:-1], refs[-1]
    hidden = jnp.concatenate([ref[...] for ref in hidden_refs], axis=0)
    for which in range(pick_ref.shape[0]):
        packed[which] = jnp.dot(pick_ref[which], hidden, preferred_element_type=F32).astype(BF16)
    for k in range(half):
        out_refs[k][...] = packed[expert_at(shape, lax.axis_index("ctx") ^ (2 * k))]


def own_block(body):
    pl.when(lax.axis_index("ctx") >= 0)(body)


def block_rows(step, deep):
    return pl.ds(pl.multiple_of((lax.axis_index("ctx") ^ step) * deep, deep), deep)


def stage_copies(steps, gate_hbm, up_hbm, outs, sem):
    copies = []
    for at, step in enumerate(steps):
        rows = block_rows(step, outs[0].shape[0])
        copies.append(pltpu.make_async_copy(gate_hbm.at[0, rows, :], outs[2 * at], sem.at[2 * at]))
        copies.append(pltpu.make_async_copy(up_hbm.at[0, rows, :], outs[2 * at + 1], sem.at[2 * at + 1]))
    return copies


def stage_kernel(steps, *refs):
    gate_hbm, up_hbm = refs[:2]
    extra = (len(refs) - 4 - 2 * len(steps)) // 2
    plain, outs = refs[2 : 2 + extra], refs[2 + extra : -2 - extra]
    plain_out, sem, plain_sem = refs[-2 - extra : -2], refs[-2], refs[-1]
    copies = [
        pltpu.make_async_copy(source, target, plain_sem.at[at])
        for at, (source, target) in enumerate(zip(plain, plain_out))
    ]
    copies += stage_copies(steps, gate_hbm, up_hbm, outs, sem)
    for copy in copies:
        copy.start()
    for copy in copies:
        copy.wait()


def staged_like(steps, deep, units):
    return (pltpu.VMEM((deep, units), BF16),) * (2 * len(steps))


def stage(gate_proj, up_proj, deep, steps, *plain):
    units = gate_proj.shape[2]
    return pl.pallas_call(
        functools.partial(stage_kernel, steps),
        out_shape=staged_like(steps, deep, units) + tuple(pltpu.VMEM(a.shape, a.dtype) for a in plain),
        in_specs=[HBM_SPEC] * (2 + len(plain)),
        out_specs=(VMEM_SPEC,) * (2 * len(steps) + len(plain)),
        scratch_shapes=[
            pltpu.SemaphoreType.DMA((max(1, 2 * len(steps)),)),
            pltpu.SemaphoreType.DMA((max(1, len(plain)),)),
        ],
        compiler_params=pltpu.CompilerParams(vmem_limit_bytes=2 << 20),
        cost_estimate=pl.CostEstimate(flops=0, bytes_accessed=4 * len(steps) * deep * units, transcendentals=0),
        name="stage",
    )(gate_proj, up_proj, *plain)


def scaled_rows(row_ref, gain_ref, step):
    wide = row_ref[...].astype(F32)
    squares = jnp.sum(wide * wide, axis=1, keepdims=True)
    return squares, (wide * gain_ref[lax.axis_index("ctx") ^ step]).astype(BF16)


def early_kernel(numbers, steps, *refs):
    count, begun = len(numbers), 0 not in numbers
    row_refs, gain_ref, weight_refs, refs = refs[:count], refs[count], refs[count + 1 : 3 * count + 1], refs[3 * count + 1 :]
    sums_in, refs = (refs[:3], refs[3:]) if begun else (None, refs)
    gate_hbm, up_hbm, gate_acc, up_acc, squares_ref = refs[:5]
    scaled_ref = refs[-1]
    copies = stage_copies(steps, gate_hbm, up_hbm, refs[5:-2], refs[-2]) if steps else []
    for copy in copies:
        copy.start()
    squares = sums_in[2][:, 0:1] if begun else 0.0
    for at, number in enumerate(numbers):
        more, scaled_ref[at] = scaled_rows(row_refs[at], gain_ref, number)
        squares = squares + more
    for at in range(count):

        @own_block
        def _():
            for which, acc in enumerate((gate_acc, up_acc)):
                term = jnp.dot(scaled_ref[at], weight_refs[2 * at + which][...], preferred_element_type=F32)
                if at:
                    term = acc[...] + term
                elif begun:
                    term = sums_in[which][...] + term
                acc[...] = term

    squares_ref[...] = jnp.broadcast_to(squares, squares_ref.shape)
    for copy in copies:
        copy.wait()


def experts_kernel(numbers, held, count, *refs):
    own_rows = len(numbers)
    row_refs, gain_ref = refs[:own_rows], refs[own_rows]
    weight_refs, refs = refs[own_rows + 1 : own_rows + 1 + 2 * held], refs[own_rows + 1 + 2 * held :]
    gate_in, up_in, squares_ref, gate_hbm, up_hbm, down_hbm, even_ref, odd_ref, act_ref = refs[:9]
    gate_acc, up_acc, pair_acc, scaled_ref, squares_acc, gate_buf, up_buf, down_buf, gate_sem, down_sem = refs[9:]
    own = lax.axis_index("ctx")
    half = count // 2
    deep = row_refs[0].shape[1]
    units = gate_acc.shape[1]
    late = numbers[held:]
    gate_ring, down_ring, down_rows = gate_buf.shape[0], down_buf.shape[0], down_buf.shape[1]
    parts = units // down_rows

    def gate_copies(at):
        rows, slot = block_rows(late[at], deep), at % gate_ring
        return (
            pltpu.make_async_copy(gate_hbm.at[0, rows, :], gate_buf.at[slot], gate_sem.at[0, slot]),
            pltpu.make_async_copy(up_hbm.at[0, rows, :], up_buf.at[slot], gate_sem.at[1, slot]),
        )

    down = [
        down_copy(down_hbm, down_buf.at[at % down_ring], down_sem.at[at % down_ring], 1 + at // parts, at % parts)
        for at in range((half - 1) * parts)
    ]
    for at in range(min(gate_ring, len(late))):
        for copy in gate_copies(at):
            copy.start()
    flight = min(DOWN_FLIGHT, down_ring - 1)
    if not late:
        for copy in down[:flight]:
            copy.start()
    squares = squares_ref[:, 0:1]
    for order, number in enumerate(numbers):
        more, scaled_ref[order] = scaled_rows(row_refs[order], gain_ref, number)
        squares = squares + more
    squares_acc[...] = jnp.broadcast_to(squares, squares_acc.shape)
    for order, number in enumerate(numbers):
        at = order - held
        if at < 0:
            gate_w, up_w = weight_refs[2 * order], weight_refs[2 * order + 1]
        else:
            for copy in gate_copies(at):
                copy.wait()
            gate_w, up_w = gate_buf.at[at % gate_ring], up_buf.at[at % gate_ring]

        @own_block
        def _():
            for acc, start, weights in ((gate_acc, gate_in, gate_w), (up_acc, up_in, up_w)):
                former = acc if order else start
                acc[...] = former[...] + jnp.dot(scaled_ref[order], weights[...], preferred_element_type=F32)

        if 0 <= at and at + gate_ring < len(late):
            for copy in gate_copies(at + gate_ring):
                copy.start()
        elif late and at == len(late) - gate_ring - 1:
            for copy in down[:flight]:
                copy.start()
    rms = lax.rsqrt(squares_acc[:, 0:1] / D + norm_eps)
    gate = rms * gate_acc[...]
    act_ref[...] = (gate / (1.0 + jnp.exp(-gate)) * (rms * up_acc[...])).astype(BF16)
    odd = own & 1
    for at, copy in enumerate(down):
        part = at % parts
        copy.wait()
        if at + flight < len(down):
            down[at + flight].start()

        @own_block
        def _():
            term = jnp.dot(
                act_ref[:, part * down_rows : (part + 1) * down_rows],
                down_buf[at % down_ring],
                preferred_element_type=F32,
            )
            pair_acc[...] = term if part == 0 else pair_acc[...] + term

        if part == parts - 1:
            store_pair(pair_acc, even_ref.at[at // parts], odd_ref.at[at // parts], odd)


def down_copy(down_hbm, target, sem, chip, part):
    rows, columns = target.shape
    start = pl.multiple_of(((lax.axis_index("ctx") >> 1) ^ chip) * columns, columns)
    return pltpu.make_async_copy(
        down_hbm.at[0, part * rows : (part + 1) * rows, pl.ds(start, columns)], target, sem
    )


def store_pair(pair_acc, even_ref, odd_ref, odd):
    deep = even_ref.shape[1]
    even_ref[...] = pair_acc[:, pl.ds(pl.multiple_of(odd * deep, deep), deep)].astype(BF16)
    odd_ref[...] = pair_acc[:, pl.ds(pl.multiple_of((1 - odd) * deep, deep), deep)].astype(BF16)


def own_columns_kernel(act_ref, down_hbm, even_ref, odd_ref, pair_acc, down_buf, down_sem):
    parts, down_rows = down_buf.shape[0], down_buf.shape[1]
    copies = [down_copy(down_hbm, down_buf.at[part], down_sem.at[part], 0, part) for part in range(parts)]
    for copy in copies:
        copy.start()
    for part, copy in enumerate(copies):
        copy.wait()

        @own_block
        def _():
            term = jnp.dot(
                act_ref[:, part * down_rows : (part + 1) * down_rows], down_buf[part], preferred_element_type=F32
            )
            pair_acc[...] = term if part == 0 else pair_acc[...] + term

    store_pair(pair_acc, even_ref, odd_ref, lax.axis_index("ctx") & 1)


def run_early(numbers, rows, gain, staged, sums, steps, gate_proj, up_proj):
    tokens, deep = rows[0].shape
    units = gate_proj.shape[2]
    acc = pltpu.VMEM((tokens, units), F32)
    outs = (acc, acc, pltpu.VMEM((tokens, 128), F32)) + (staged_like(steps, deep, units) if steps else ())
    return pl.pallas_call(
        functools.partial(early_kernel, numbers, steps),
        out_shape=outs,
        in_specs=[VMEM_SPEC] * (len(rows) + 1 + len(staged) + len(sums)) + [HBM_SPEC] * 2,
        out_specs=(VMEM_SPEC,) * len(outs),
        scratch_shapes=([pltpu.SemaphoreType.DMA((2 * len(steps),))] if steps else [])
        + [pltpu.VMEM((len(rows), tokens, deep), BF16)],
        compiler_params=pltpu.CompilerParams(vmem_limit_bytes=5 << 20),
        cost_estimate=pl.CostEstimate(
            flops=4 * tokens * deep * units * len(rows),
            bytes_accessed=4 * len(steps) * deep * units,
            transcendentals=0,
        ),
        name="early",
    )(*rows, gain, *[in_vmem(array) for array in staged], *sums, gate_proj, up_proj)


def run_experts(numbers, rows, count, gain, staged, sums, gate_proj, up_proj, down_proj):
    tokens, deep = rows[0].shape
    units = gate_proj.shape[2]
    parts = 2
    weights = 2 * (2 * gate_proj.size + down_proj.size)
    pieces = like((count // 2 - 1, tokens, deep))
    late_rows = deep if len(staged) < 2 * len(rows) else 16
    return pl.pallas_call(
        functools.partial(experts_kernel, numbers, len(staged) // 2, count),
        out_shape=(pieces, pieces, pltpu.VMEM((tokens, units), BF16)),
        in_specs=[VMEM_SPEC] * (len(rows) + 1 + len(staged) + 3) + [HBM_SPEC] * 3,
        out_specs=(VMEM_SPEC,) * 3,
        scratch_shapes=[
            pltpu.VMEM((tokens, units), F32),
            pltpu.VMEM((tokens, units), F32),
            pltpu.VMEM((tokens, 2 * deep), F32),
            pltpu.VMEM((len(rows), tokens, deep), BF16),
            pltpu.VMEM((tokens, 128), F32),
            pltpu.VMEM((GATE_RING, late_rows, units), BF16),
            pltpu.VMEM((GATE_RING, late_rows, units), BF16),
            pltpu.VMEM((DOWN_RING, units // parts, 2 * deep), BF16),
            pltpu.SemaphoreType.DMA((2, GATE_RING)),
            pltpu.SemaphoreType.DMA((DOWN_RING,)),
        ],
        compiler_params=pltpu.CompilerParams(vmem_limit_bytes=EXPERTS_MIB << 20),
        cost_estimate=pl.CostEstimate(flops=tokens * weights, bytes_accessed=weights // 2, transcendentals=tokens * units),
        name="experts",
    )(*rows, gain, *[in_vmem(array) for array in staged], *sums, gate_proj, up_proj, down_proj)


def pair_total_kernel(even_ref, other_ref, *out_refs):
    for k, ref in enumerate(out_refs):
        ref[...] = (even_ref[k].astype(F32) + other_ref[k].astype(F32)).astype(BF16)


def combine_kernel(shape, high_ref, low_ref, *refs):
    half, mp_count = shape[0] // 2, shape[1]
    piece_refs, even_ref, other_ref = refs[: half - 1], refs[half - 1], refs[half]
    kept_ref, sent_refs = refs[half + 1], refs[half + 2 :]
    own_piece = (even_ref[...].astype(F32) + other_ref[...].astype(F32)).astype(BF16)
    pieces = jnp.concatenate([own_piece] + [ref[...] for ref in piece_refs], axis=0)
    experts = [expert_at(shape, lax.axis_index("ctx") ^ (2 * k)) for k in range(half)]
    total = None
    for table in (high_ref, low_ref):
        spread = jnp.concatenate([table[expert] for expert in experts], axis=0)
        term = lax.dot_general(spread, pieces, (((0,), (0,)), ((), ())), preferred_element_type=F32)
        total = term if total is None else total + term
    rows = kept_ref.shape[0]
    kept_ref[...] = total[:rows]
    for k, ref in enumerate(sent_refs, 1):
        ref[...] = total[k * rows : (k + 1) * rows].astype(BF16)


def exchange_path(
    queries,
    cache_keys,
    cache_values,
    new_keys,
    new_values,
    out_proj,
    residual,
    norm_gain,
    gate_proj,
    up_proj,
    down_proj,
    expert_ids,
    route_logits,
):
    ctx_count = lax.axis_size("ctx")
    mp_count = lax.axis_size("mp")
    shape = (ctx_count, mp_count)
    gate_hbm, up_hbm, down_hbm = in_hbm(gate_proj), in_hbm(up_proj), in_hbm(down_proj)
    tok_local = queries.shape[0]
    tokens = tok_local * ctx_count
    slot_local, cache_local, head_dim = cache_keys.shape
    heads = queries.shape[1] // head_dim
    d_local = out_proj.shape[1]
    res_rows = residual.shape[0]
    half = ctx_count // 2
    rows = half * tok_local
    capacity = tokens * TOP // 4
    per_row = max(1, EXPERTS // mp_count)

    blocks = [queries] + spread([queries] * (half - 1), "ctx", 2)
    own = [cache_keys, cache_values, new_keys, new_values]
    pair = [swap(array, "ctx", 1) for array in own]
    held = stage(gate_hbm, up_hbm, d_local, (), *[in_hbm(array) for array in (*own, queries)])
    held, blocks[1:], pair = lax.optimization_barrier((held, blocks[1:], pair))
    mine = device_call(
        attention_kernel,
        "attention",
        like((heads + 1, rows, head_dim)),
        [in_vmem(array) for array in (held[4], *blocks[1:], *held[:4], *pair)],
        [
            pltpu.VMEM((slot_local, heads // slot_local * rows, head_dim), BF16),
            pltpu.VMEM((slot_local, 2 * tok_local, head_dim), BF16),
            pltpu.VMEM((slot_local, 2 * tok_local, head_dim), BF16),
        ],
        flops=8 * heads * rows * (cache_local + tok_local) * head_dim,
        limit=24,
    )
    others = spread([mine] * (half - 1), "ctx", 2)
    ids, logits, _ = lax.optimization_barrier((expert_ids.T, route_logits.T, mine))
    pick, high, low = device_call(
        functools.partial(tables_kernel, shape),
        "tables",
        (like((per_row, capacity, tokens)),) * 3,
        [ids, logits],
    )
    gain = norm_gain.astype(F32).reshape(ctx_count, 1, d_local)
    gate_later, _ = lax.optimization_barrier((gate_proj, mine))
    *staged, out_proj, residual = stage(
        in_hbm(gate_later), up_hbm, d_local, STAGE_AT[0], in_hbm(out_proj), in_hbm(residual)
    )
    pick, high, low, gain, staged, out_proj, residual, others = lax.optimization_barrier(
        (pick, high, low, gain, staged, out_proj, residual, others)
    )
    attn = device_call(join_kernel, "join", like((rows, heads * head_dim)), [mine] + others)
    block = like((res_rows, d_local))

    kept, *sent = device_call(
        project_kernel,
        "project",
        (like((res_rows, d_local), F32),) + (block,) * (mp_count - 1),
        [attn, swap(attn, "ctx", 1), out_proj],
        [pltpu.VMEM((tokens, heads * head_dim), BF16)],
        flops=2 * tokens * heads * head_dim * d_local,
    )
    arrived = spread(sent, "mp")
    gate_later, _ = lax.optimization_barrier((gate_proj, kept))
    more = stage(in_hbm(gate_later), up_hbm, d_local, STAGE_AT[1])
    more, arrived = lax.optimization_barrier((more, arrived))
    staged = [*staged, *more]
    hidden = device_call(total_kernel, "hidden", block, [kept, residual] + arrived[::-1])

    everyone = spread([hidden] * (mp_count - 1), "mp")
    gate_later, _ = lax.optimization_barrier((gate_proj, hidden))
    more = stage(in_hbm(gate_later), up_hbm, d_local, STAGE_AT[2])
    more, everyone = lax.optimization_barrier((more, everyone))
    staged, everyone = [*staged, *more], [hidden, *everyone]
    even = device_call(
        functools.partial(pack_kernel, shape),
        "pack",
        (like((capacity, d_local)),) * half,
        [pick] + everyone,
        [pltpu.VMEM((per_row, capacity, d_local), BF16)],
    )
    even = [even[0]] + spread(even[1:], "ctx", 2)
    numbered = [number for steps in STAGE_AT for number in steps]
    odd = swap(even[0], "ctx", 1)
    sums = run_early((0, 1), [even[0], odd], gain, staged[:4], (), STAGE_AT[3], gate_hbm, up_hbm)
    sums, even = lax.optimization_barrier((sums, even[1:]))
    staged, sums = [*staged, *sums[3:]], sums[:3]
    odd = [swap(piece, "ctx", 1) for piece in even]
    held = {number: staged[2 * at : 2 * at + 2] for at, number in enumerate(numbered[: len(staged) // 2])}
    numbers = tuple(range(2, ctx_count, 2))
    *sums, gate_last, up_last = run_early(
        numbers, even, gain, [array for number in numbers for array in held[number]], sums, STAGE_AT[4], gate_hbm, up_hbm
    )
    out_even, out_odd, act = run_experts(
        tuple(range(3, ctx_count, 2)),
        odd,
        ctx_count,
        gain,
        [*held[3], gate_last, up_last, *held.get(7, ())],
        sums,
        gate_hbm,
        up_hbm,
        down_hbm,
    )
    pieces = device_call(
        pair_total_kernel,
        "pair_total",
        (like((capacity, d_local)),) * (half - 1),
        [out_even, swap(out_odd, "ctx", 1)],
    )
    act, *pieces = lax.optimization_barrier((act, *pieces))
    returned = spread(pieces, "ctx", 2)
    own_even, own_odd = device_call(
        own_columns_kernel,
        "own_columns",
        (like((capacity, d_local)),) * 2,
        [act, down_hbm],
        [
            pltpu.VMEM((capacity, 2 * d_local), F32),
            pltpu.VMEM((2, act.shape[1] // 2, 2 * d_local), BF16),
            pltpu.SemaphoreType.DMA((2,)),
        ],
        specs=[VMEM_SPEC, HBM_SPEC],
        moved=1,
    )
    pieces = returned + [own_even, swap(own_odd, "ctx", 1)]
    kept, *sent = device_call(
        functools.partial(combine_kernel, shape),
        "combine",
        (like((res_rows, d_local), F32),) + (block,) * (mp_count - 1),
        [high, low] + pieces,
    )
    arrived = spread(sent, "mp")
    return device_call(total_kernel, "layer_out", block, [kept, hidden] + arrived[::-1])


def on_device(*args):
    queries, cache_keys, out_proj, gate_proj, down_proj = (args[i] for i in (0, 1, 5, 8, 10))
    ctx_count, mp_count = lax.axis_size("ctx"), lax.axis_size("mp")
    per_row = max(1, EXPERTS // mp_count)
    fits = (
        ctx_count == 2 * mp_count
        and ctx_count & (ctx_count - 1) == 0
        and (ctx_count // per_row) % 2 == 0
        and out_proj.shape[1] % 256 == 0
        and gate_proj.shape[2] % 2048 == 0
        and queries.shape[0] % 16 == 0
        and 3 * (queries.shape[1] // cache_keys.shape[2]) <= cache_keys.shape[2]
    )
    return exchange_path(*args) if fits else gathered_path(*args)


def solution(mesh):
    placed = (
        P("ctx", "mp"),
        P("mp", "ctx", None),
        P("mp", "ctx", None),
        P("mp", "ctx", None),
        P("mp", "ctx", None),
        P("mp", "ctx"),
        P("mp", "ctx"),
        P(),
        P("ctx", None, "mp"),
        P("ctx", None, "mp"),
        P("ctx", "mp", None),
        P(),
        P(),
    )
    return jax.shard_map(
        on_device, mesh=mesh, in_specs=placed, out_specs=P("mp", "ctx"), check_vma=False
    )
```

```python
import functools
import math

import jax
import jax.numpy as jnp
from jax import lax
from jax.experimental import pallas as pl
from jax.experimental.pallas import tpu as pltpu
from jax.sharding import PartitionSpec as P

D = 6144
EXPERTS = 8
TOP = 2


neg_big = -1e30
norm_eps = 1e-05


def route_slots(expert_ids):
    flat = expert_ids.reshape(-1)
    onehot = (flat[:, None] == jnp.arange(EXPERTS, dtype=jnp.int32)[None, :]).astype(jnp.int32)
    before = jnp.cumsum(onehot, axis=0, dtype=jnp.int32) - onehot
    return jnp.sum(before * onehot, axis=1, dtype=jnp.int32).reshape(expert_ids.shape)


def softmax_pieces(query_block, keys_local, values_local, allowed, scale):
    scores = (
        jnp.einsum("srd,skd->srk", query_block, keys_local, preferred_element_type=jnp.float32)
        * scale
    )
    scores = jnp.where(allowed[None, :, :], scores, neg_big)
    highest = jnp.max(scores, axis=2)
    expo = jnp.exp(scores - highest[:, :, None])
    denom = jnp.sum(expo, axis=2)
    summed = jnp.einsum(
        "srk,skd->srd", expo.astype(jnp.bfloat16), values_local, preferred_element_type=jnp.float32
    )
    return (highest, denom, summed)


def join_softmax(former, latter):
    highest = jnp.maximum(former[0], latter[0])
    right = jnp.exp(latter[0] - highest)
    denom = latter[1] * right
    summed = latter[2] * right[:, :, None]
    return (highest, denom, summed)


def gathered_path(
    queries,
    cache_keys,
    cache_values,
    new_keys,
    new_values,
    out_proj,
    residual,
    norm_gain,
    gate_proj,
    up_proj,
    down_proj,
    expert_ids,
    route_logits,
):
    ctx_count = lax.axis_size("ctx")
    mp_count = lax.axis_size("mp")
    ctx_index = lax.axis_index("ctx")
    mp_index = lax.axis_index("mp")
    tok_local = queries.shape[0]
    tokens = tok_local * ctx_count
    slot_local = cache_keys.shape[0]
    cache_local = cache_keys.shape[1]
    head_dim = cache_keys.shape[2]
    heads_local = queries.shape[1] // head_dim
    group_size = heads_local // slot_local
    width = cache_local + tok_local
    scale = 1.0 / math.sqrt(head_dim)
    d_local = out_proj.shape[1]
    key_value = jnp.stack(
        [
            jnp.concatenate([cache_keys, new_keys], axis=1),
            jnp.concatenate([cache_values, new_values], axis=1),
        ]
    )
    shaped = queries.reshape(tok_local, slot_local, group_size, head_dim)
    query_block = jnp.transpose(shaped, (1, 2, 0, 3)).reshape(
        slot_local, group_size * tok_local, head_dim
    )
    query_tok = ctx_index * tok_local + jnp.tile(jnp.arange(tok_local, dtype=jnp.int32), group_size)
    query_count = group_size * tok_local
    start_state = (
        jnp.full((slot_local, query_count), neg_big, jnp.float32),
        jnp.zeros((slot_local, query_count), jnp.float32),
        jnp.zeros((slot_local, query_count, head_dim), jnp.float32),
    )
    piece = lax.all_gather(key_value, "ctx", axis=2, tiled=True)
    position = jnp.arange(piece.shape[2], dtype=jnp.int32)
    shard = position // width
    within = position % width
    new_tok = shard * tok_local + within - cache_local
    allowed = (within[None, :] < cache_local) | (new_tok[None, :] <= query_tok[:, None])
    highest, denom, summed = join_softmax(
        start_state, softmax_pieces(query_block, piece[0], piece[1], allowed, scale)
    )
    shaped = (
        (summed / denom[:, :, None])
        .astype(jnp.bfloat16)
        .reshape(slot_local, group_size, tok_local, head_dim)
    )
    attn = jnp.transpose(shaped, (2, 0, 1, 3)).reshape(tok_local, heads_local * head_dim)
    projected = jnp.dot(
        lax.all_gather(attn, "ctx", axis=0, tiled=True),
        out_proj,
        preferred_element_type=jnp.float32,
    )
    res_rows = residual.shape[0]
    res_start = mp_index * res_rows
    current = lax.dynamic_slice_in_dim(projected, res_start, res_rows, 0)
    projected = lax.dynamic_update_slice_in_dim(
        projected, current + residual.astype(jnp.float32), res_start, 0
    )
    hidden = lax.psum(projected.astype(jnp.bfloat16), "mp")
    capacity = tokens * TOP // 4
    slots = route_slots(expert_ids)
    per_row = max(1, EXPERTS // mp_count)
    first_expert = mp_index * EXPERTS // mp_count
    own_expert = (mp_index * ctx_count + ctx_index) * EXPERTS // (ctx_count * mp_count)
    local = own_expert - first_expert
    row_experts = first_expert + jnp.arange(per_row, dtype=jnp.int32)
    match = expert_ids[None, :, :] == row_experts[:, None, None]
    place = jnp.where(match, slots[None, :, :], capacity)
    table = place[:, :, :, None] == jnp.arange(capacity, dtype=jnp.int32)[None, None, None, :]
    pick = jnp.any(table, axis=2)
    packed = jnp.einsum(
        "rtc,td->rcd", pick.astype(jnp.bfloat16), hidden, preferred_element_type=jnp.float32
    ).astype(jnp.bfloat16)
    gate_local = gate_proj[0]
    up_local = up_proj[0]
    down_local = down_proj[0]
    chosen = lax.dynamic_index_in_dim(
        lax.all_gather(packed, "ctx", axis=2, tiled=True), local, 0, keepdims=False
    )
    wide = chosen.astype(jnp.float32)
    gains = norm_gain.astype(jnp.float32)
    scaled = (wide * gains[None, :]).astype(jnp.bfloat16)
    gate_sum = jnp.dot(scaled, gate_local, preferred_element_type=jnp.float32)
    up_sum = jnp.dot(scaled, up_local, preferred_element_type=jnp.float32)
    gate_sum, up_sum, squares = (gate_sum, up_sum, jnp.sum(wide * wide, axis=1))
    rms = lax.rsqrt(squares / D + norm_eps)
    act = (jax.nn.silu(rms[:, None] * gate_sum) * (rms[:, None] * up_sum)).astype(jnp.bfloat16)
    part = lax.dot_general(
        down_local, act, (((0,), (1,)), ((), ())), preferred_element_type=jnp.float32
    )
    returned = lax.psum_scatter(
        jnp.concatenate(
            [jnp.where(local == which, part, 0.0) for which in range(per_row)], axis=1
        ).astype(jnp.bfloat16),
        "ctx",
        scatter_dimension=0,
        tiled=True,
    ).astype(jnp.float32)
    weights = jax.nn.softmax(route_logits, axis=1)
    combine = jnp.sum(jnp.where(table, weights[None, :, :, None], 0.0), axis=2)
    moe = jnp.einsum(
        "drc,rtc->td",
        returned.reshape(d_local, per_row, capacity),
        combine,
        precision=lax.Precision.HIGHEST,
        preferred_element_type=jnp.float32,
    )
    share = lax.psum_scatter(
        moe.astype(jnp.bfloat16), "mp", scatter_dimension=0, tiled=True
    ).astype(jnp.float32)
    own_hidden = lax.dynamic_slice_in_dim(hidden, res_start, res_rows, 0).astype(jnp.float32)
    return (own_hidden + share).astype(jnp.bfloat16)


BF16 = jnp.bfloat16
F32 = jnp.float32
VMEM_SPEC = pl.BlockSpec(memory_space=pltpu.VMEM)
HBM_SPEC = pl.BlockSpec(memory_space=pl.ANY)
SMALL_MIB = 8
STAGE_AT = ((0, 1, 2), (4, 6), (3,), (7,), (5,))
EXPERTS_MIB = 12


def swap(array, axis_name, mask):
    count = lax.axis_size(axis_name)
    return lax.ppermute(array, axis_name, [(i, i ^ mask) for i in range(count)])


def spread(arrays, axis_name, unit=1):
    masks = range(unit, unit * (len(arrays) + 1), unit)
    moved = [swap(array, axis_name, mask) for mask, array in reversed(list(zip(masks, arrays)))]
    return moved[::-1]


def device_call(kernel, name, outs, arrays, scratch=(), flops=0, limit=SMALL_MIB, specs=None, moved=0):
    moved = moved or sum(a.size * a.dtype.itemsize for a in arrays)
    return pl.pallas_call(
        kernel,
        out_shape=outs,
        in_specs=specs or [VMEM_SPEC] * len(arrays),
        out_specs=jax.tree.map(lambda _: VMEM_SPEC, outs),
        scratch_shapes=list(scratch),
        compiler_params=pltpu.CompilerParams(vmem_limit_bytes=limit << 20),
        cost_estimate=pl.CostEstimate(flops=flops, bytes_accessed=moved, transcendentals=0),
        name=name,
    )(*arrays)


def in_hbm(array):
    return pltpu.with_memory_space_constraint(array, pltpu.HBM)


def in_vmem(array):
    return pltpu.with_memory_space_constraint(array, pltpu.VMEM)


def like(shape, dtype=BF16):
    return jax.ShapeDtypeStruct(shape, dtype)


def expert_at(shape, ctx_at):
    ctx_count, mp_count = shape
    mp_index = lax.axis_index("mp")
    own = lax.div((mp_index * ctx_count + ctx_at) * EXPERTS, ctx_count * mp_count)
    return own - lax.div(mp_index * EXPERTS, mp_count)


def tables_kernel(shape, ids_ref, logits_ref, pick_ref, high_ref, low_ref):
    mp_index = lax.axis_index("mp")
    mp_count = shape[1]
    per_row, capacity, tokens = pick_ref.shape
    rows = tokens // mp_count
    first = lax.div(mp_index * EXPERTS, mp_count)
    lane = lax.broadcasted_iota(jnp.int32, (1, tokens), 1)

    def by_block(values):
        for bit in range(mp_count.bit_length() - 1):
            size = rows << bit
            forward = pltpu.roll(values, size, 1)
            back = pltpu.roll(values, tokens - size, 1)
            moved = jnp.where((lane & size) != 0, forward, back)
            values = jnp.where(((mp_index >> bit) & 1) == 1, moved, values)
        return values

    logits = logits_ref[...]
    weights = jnp.exp(logits - jnp.max(logits, axis=0, keepdims=True))
    weights = weights / jnp.sum(weights, axis=0, keepdims=True)
    ids = ids_ref[...]
    earlier = lax.broadcasted_iota(jnp.int32, (tokens, tokens), 0) < lax.broadcasted_iota(
        jnp.int32, (tokens, tokens), 1
    )
    earlier = earlier.astype(F32).astype(BF16)
    for which in range(per_row):
        named = (ids == first + which).astype(F32)
        member = jnp.max(named, axis=0, keepdims=True)
        weight = jnp.sum(named * weights, axis=0, keepdims=True)
        slot = jnp.dot(
            jnp.broadcast_to(member, (8, tokens)).astype(BF16), earlier, preferred_element_type=F32
        )[0:1]
        slot = by_block(jnp.where(member > 0, slot, float(capacity)))
        weight = by_block(weight)
        taken = lax.broadcasted_iota(jnp.int32, (capacity, tokens), 0) == slot.astype(jnp.int32)
        pick_ref[which] = jnp.where(taken, 1.0, 0.0).astype(BF16)
        weight = jnp.where(taken, weight, 0.0)
        high = weight.astype(BF16)
        high_ref[which] = high
        low_ref[which] = (weight - high.astype(F32)).astype(BF16)


def attention_kernel(*refs):
    half = len(refs) - 8 - 1 - 3
    query_refs = refs[:half]
    own_k, own_v, new_k, new_v, pair_k, pair_v, pair_nk, pair_nv = refs[half : half + 8]
    mine_ref, query_buf, key_buf, value_buf = refs[half + 8 :]
    own = lax.axis_index("ctx")
    slots, _, head_dim = own_k.shape
    tok_local = new_k.shape[1]
    rows = half * tok_local
    group = query_refs[0].shape[1] // head_dim // slots
    heads = slots * group
    factor = math.log2(math.e) / math.sqrt(head_dim)
    for at, query_ref in enumerate(query_refs):
        for head in range(heads):
            start = (head % group) * rows + at * tok_local
            query_buf[head // group, start : start + tok_local, :] = query_ref[
                :, head * head_dim : (head + 1) * head_dim
            ]
    for part, (key_ref, value_ref) in enumerate(((new_k, new_v), (pair_nk, pair_nv))):
        for slot in range(slots):
            key_buf[slot, part * tok_local : (part + 1) * tok_local, :] = key_ref[slot]
            value_buf[slot, part * tok_local : (part + 1) * tok_local, :] = value_ref[slot]
    row = lax.rem(lax.broadcasted_iota(jnp.int32, (group * rows, 1), 0), rows)
    block = lax.div(row, tok_local)
    row_tok = (own ^ (2 * block)) * tok_local + row - block * tok_local
    column = lax.broadcasted_iota(jnp.int32, (1, 2 * tok_local), 1)
    block = lax.div(column, tok_local)
    key_tok = (own ^ block) * tok_local + column - block * tok_local
    seen = key_tok <= row_tok
    lane = lax.broadcasted_iota(jnp.int32, (rows, head_dim), 1)
    stats = jnp.zeros((rows, head_dim), F32)

    def product(left, right):
        return lax.dot_general(left, right, (((1,), (1,)), ((), ())), preferred_element_type=F32)

    for slot in range(slots):
        query = query_buf[slot]
        first = product(query, own_k[slot]) * factor
        second = product(query, pair_k[slot]) * factor
        third = jnp.where(seen, product(query, key_buf[slot]) * factor, neg_big)
        top = jnp.maximum(
            jnp.max(jnp.maximum(first, second), axis=1, keepdims=True),
            jnp.max(third, axis=1, keepdims=True),
        )
        shift = top.astype(BF16).astype(F32)
        first = jnp.exp2(first - shift)
        second = jnp.exp2(second - shift)
        third = jnp.exp2(third - shift)
        denom = jnp.sum(first + second, axis=1, keepdims=True) + jnp.sum(third, axis=1, keepdims=True)
        summed = jnp.dot(first.astype(BF16), own_v[slot], preferred_element_type=F32)
        summed += jnp.dot(second.astype(BF16), pair_v[slot], preferred_element_type=F32)
        summed += jnp.dot(third.astype(BF16), value_buf[slot], preferred_element_type=F32)
        summed = summed.astype(BF16)
        high = denom.astype(BF16).astype(F32)
        low = denom - high
        for index in range(group):
            head = slot * group + index
            span = slice(index * rows, (index + 1) * rows)
            mine_ref[head] = summed[span]
            stats = jnp.where(lane == head, shift[span], stats)
            stats = jnp.where(lane == heads + head, high[span], stats)
            stats = jnp.where(lane == 2 * heads + head, low[span], stats)
    mine_ref[heads] = stats.astype(BF16)


def join_kernel(*refs):
    part_refs, attn_ref = refs[:-1], refs[-1]
    half = len(part_refs)
    heads, head_dim = part_refs[0].shape[0] - 1, part_refs[0].shape[2]
    tok = part_refs[0].shape[1] // half
    for block in range(half):
        spans = [slice((k ^ block) * tok, ((k ^ block) + 1) * tok) for k in range(half)]
        stats = [ref[heads, span, :].astype(F32) for ref, span in zip(part_refs, spans)]
        highest = functools.reduce(jnp.maximum, stats)
        lifts = [jnp.exp2(stat - highest) for stat in stats]
        denoms = [
            pltpu.roll(stat, head_dim - heads, 1) + pltpu.roll(stat, head_dim - 2 * heads, 1)
            for stat in stats
        ]
        total = sum(lift * denom for lift, denom in zip(lifts, denoms))
        shares = [lift / total for lift in lifts]
        for head in range(heads):
            mixed = sum(
                share[:, head : head + 1] * ref[head, span, :].astype(F32)
                for share, ref, span in zip(shares, part_refs, spans)
            )
            attn_ref[block * tok : (block + 1) * tok, head * head_dim : (head + 1) * head_dim] = mixed.astype(BF16)


def project_kernel(own_ref, pair_ref, weight_ref, kept_ref, *refs):
    sent_refs, left = refs[:-1], refs[-1]
    ctx_index, mp_index = lax.axis_index("ctx"), lax.axis_index("mp")
    mp_count = len(sent_refs) + 1
    tok = own_ref.shape[0] // mp_count
    odd = ctx_index & 1
    pair_at = (ctx_index >> 1) ^ mp_index
    for k in range(mp_count):
        source = pl.ds(pl.multiple_of((pair_at ^ k) * tok, tok), tok)
        left[pl.ds(pl.multiple_of((2 * k + odd) * tok, tok), tok), :] = own_ref[source, :]
        left[pl.ds(pl.multiple_of((2 * k + 1 - odd) * tok, tok), tok), :] = pair_ref[source, :]
    projected = jnp.dot(left[...], weight_ref[...], preferred_element_type=F32)
    kept_ref[...] = projected[: 2 * tok]
    for k, ref in enumerate(sent_refs, 1):
        ref[...] = projected[2 * k * tok : 2 * (k + 1) * tok].astype(BF16)


def total_kernel(*refs):
    total = refs[0][...].astype(F32)
    for ref in refs[1:-1]:
        total = total + ref[...].astype(F32)
    refs[-1][...] = total.astype(BF16)


def pack_kernel(shape, pick_ref, *refs):
    mp_count, half = shape[1], shape[0] // 2
    hidden_refs, out_refs, packed = refs[:mp_count], refs[mp_count:-1], refs[-1]
    hidden = jnp.concatenate([ref[...] for ref in hidden_refs], axis=0)
    for which in range(pick_ref.shape[0]):
        packed[which] = jnp.dot(pick_ref[which], hidden, preferred_element_type=F32).astype(BF16)
    for k in range(half):
        out_refs[k][...] = packed[expert_at(shape, lax.axis_index("ctx") ^ (2 * k))]


def own_block(body):
    pl.when(lax.axis_index("ctx") >= 0)(body)


def block_rows(step, deep):
    return pl.ds(pl.multiple_of((lax.axis_index("ctx") ^ step) * deep, deep), deep)


def stage_copies(steps, gate_hbm, up_hbm, outs, sem):
    copies = []
    for at, step in enumerate(steps):
        rows = block_rows(step, outs[0].shape[0])
        copies.append(pltpu.make_async_copy(gate_hbm.at[0, rows, :], outs[2 * at], sem.at[2 * at]))
        copies.append(pltpu.make_async_copy(up_hbm.at[0, rows, :], outs[2 * at + 1], sem.at[2 * at + 1]))
    return copies


def stage_kernel(steps, *refs):
    gate_hbm, up_hbm = refs[:2]
    extra = (len(refs) - 4 - 2 * len(steps)) // 2
    plain, outs = refs[2 : 2 + extra], refs[2 + extra : -2 - extra]
    plain_out, sem, plain_sem = refs[-2 - extra : -2], refs[-2], refs[-1]
    copies = [
        pltpu.make_async_copy(source, target, plain_sem.at[at])
        for at, (source, target) in enumerate(zip(plain, plain_out))
    ]
    copies += stage_copies(steps, gate_hbm, up_hbm, outs, sem)
    for copy in copies:
        copy.start()
    for copy in copies:
        copy.wait()


def staged_like(steps, deep, units):
    return (pltpu.VMEM((deep, units), BF16),) * (2 * len(steps))


def stage(gate_proj, up_proj, deep, steps, *plain):
    units = gate_proj.shape[2]
    return pl.pallas_call(
        functools.partial(stage_kernel, steps),
        out_shape=staged_like(steps, deep, units) + tuple(pltpu.VMEM(a.shape, a.dtype) for a in plain),
        in_specs=[HBM_SPEC] * (2 + len(plain)),
        out_specs=(VMEM_SPEC,) * (2 * len(steps) + len(plain)),
        scratch_shapes=[
            pltpu.SemaphoreType.DMA((max(1, 2 * len(steps)),)),
            pltpu.SemaphoreType.DMA((max(1, len(plain)),)),
        ],
        compiler_params=pltpu.CompilerParams(vmem_limit_bytes=2 << 20),
        cost_estimate=pl.CostEstimate(flops=0, bytes_accessed=4 * len(steps) * deep * units, transcendentals=0),
        name="stage",
    )(gate_proj, up_proj, *plain)


def scaled_rows(row_ref, gain_ref, step):
    wide = row_ref[...].astype(F32)
    squares = jnp.sum(wide * wide, axis=1, keepdims=True)
    return squares, (wide * gain_ref[lax.axis_index("ctx") ^ step]).astype(BF16)


def early_kernel(numbers, steps, *refs):
    count, begun = len(numbers), 0 not in numbers
    row_refs, gain_ref, weight_refs, refs = refs[:count], refs[count], refs[count + 1 : 3 * count + 1], refs[3 * count + 1 :]
    sums_in, refs = (refs[:3], refs[3:]) if begun else (None, refs)
    gate_hbm, up_hbm, gate_acc, up_acc, squares_ref = refs[:5]
    scaled_ref = refs[-1]
    copies = stage_copies(steps, gate_hbm, up_hbm, refs[5:-2], refs[-2]) if steps else []
    for copy in copies:
        copy.start()
    squares = sums_in[2][:, 0:1] if begun else 0.0
    for at, number in enumerate(numbers):
        more, scaled_ref[at] = scaled_rows(row_refs[at], gain_ref, number)
        squares = squares + more
    for at in range(count):

        @own_block
        def _():
            for which, acc in enumerate((gate_acc, up_acc)):
                term = jnp.dot(scaled_ref[at], weight_refs[2 * at + which][...], preferred_element_type=F32)
                if at:
                    term = acc[...] + term
                elif begun:
                    term = sums_in[which][...] + term
                acc[...] = term

    squares_ref[...] = jnp.broadcast_to(squares, squares_ref.shape)
    for copy in copies:
        copy.wait()


def experts_kernel(numbers, *refs):
    count = len(numbers)
    row_refs, gain_ref, weight_refs, refs = refs[:count], refs[count], refs[count + 1 : 3 * count + 1], refs[3 * count + 1 :]
    gate_in, up_in, squares_ref, down_hbm, odd_ref, act_ref = refs[:6]
    even_refs, (gate_acc, up_acc, scaled_ref, squares_acc, odd_buf, sem) = refs[6:-6], refs[-6:]
    chips = len(even_refs)
    deep = odd_ref.shape[2]
    targets = [(2 * k + 3, odd_buf.at[k]) for k in range(chips)] + [(2 * k + 2, ref) for k, ref in enumerate(even_refs)]
    copies = [
        pltpu.make_async_copy(down_hbm.at[0, :, block_rows(number, deep)], target, sem.at[at])
        for at, (number, target) in enumerate(targets)
    ]
    for copy in copies[:chips]:
        copy.start()
    squares = squares_ref[:, 0:1]
    for order, number in enumerate(numbers):
        more, scaled_ref[order] = scaled_rows(row_refs[order], gain_ref, number)
        squares = squares + more
    squares_acc[...] = jnp.broadcast_to(squares, squares_acc.shape)
    for order in range(count):

        @own_block
        def _():
            for which, (acc, start) in enumerate(((gate_acc, gate_in), (up_acc, up_in))):
                former = acc if order else start
                weights = weight_refs[2 * order + which]
                acc[...] = former[...] + jnp.dot(scaled_ref[order], weights[...], preferred_element_type=F32)

        for copy in copies[chips + order : chips + order + 1]:
            copy.start()
    rms = lax.rsqrt(squares_acc[:, 0:1] / D + norm_eps)
    gate = rms * gate_acc[...]
    act_ref[...] = (gate / (1.0 + jnp.exp(-gate)) * (rms * up_acc[...])).astype(BF16)
    for k in range(chips):
        copies[k].wait()

        @own_block
        def _():
            odd_ref[k] = jnp.dot(act_ref[...], odd_buf[k], preferred_element_type=F32).astype(BF16)

    for copy in copies[chips:]:
        copy.wait()


def even_columns_kernel(act_ref, *refs):
    for k, weight_ref in enumerate(refs[:-1]):
        refs[-1][k] = jnp.dot(act_ref[...], weight_ref[...], preferred_element_type=F32).astype(BF16)


def down_copy(down_hbm, target, sem, chip, part):
    rows, columns = target.shape
    start = pl.multiple_of(((lax.axis_index("ctx") >> 1) ^ chip) * columns, columns)
    return pltpu.make_async_copy(
        down_hbm.at[0, part * rows : (part + 1) * rows, pl.ds(start, columns)], target, sem
    )


def store_pair(pair_acc, even_ref, odd_ref, odd):
    deep = even_ref.shape[1]
    even_ref[...] = pair_acc[:, pl.ds(pl.multiple_of(odd * deep, deep), deep)].astype(BF16)
    odd_ref[...] = pair_acc[:, pl.ds(pl.multiple_of((1 - odd) * deep, deep), deep)].astype(BF16)


def own_columns_kernel(act_ref, down_hbm, even_ref, odd_ref, pair_acc, down_buf, down_sem):
    parts, down_rows = down_buf.shape[0], down_buf.shape[1]
    copies = [down_copy(down_hbm, down_buf.at[part], down_sem.at[part], 0, part) for part in range(parts)]
    for copy in copies:
        copy.start()
    for part, copy in enumerate(copies):
        copy.wait()

        @own_block
        def _():
            term = jnp.dot(
                act_ref[:, part * down_rows : (part + 1) * down_rows], down_buf[part], preferred_element_type=F32
            )
            pair_acc[...] = term if part == 0 else pair_acc[...] + term

    store_pair(pair_acc, even_ref, odd_ref, lax.axis_index("ctx") & 1)


def run_early(numbers, rows, gain, staged, sums, steps, gate_proj, up_proj):
    tokens, deep = rows[0].shape
    units = gate_proj.shape[2]
    acc = pltpu.VMEM((tokens, units), F32)
    outs = (acc, acc, pltpu.VMEM((tokens, 128), F32)) + (staged_like(steps, deep, units) if steps else ())
    return pl.pallas_call(
        functools.partial(early_kernel, numbers, steps),
        out_shape=outs,
        in_specs=[VMEM_SPEC] * (len(rows) + 1 + len(staged) + len(sums)) + [HBM_SPEC] * 2,
        out_specs=(VMEM_SPEC,) * len(outs),
        scratch_shapes=([pltpu.SemaphoreType.DMA((2 * len(steps),))] if steps else [])
        + [pltpu.VMEM((len(rows), tokens, deep), BF16)],
        compiler_params=pltpu.CompilerParams(vmem_limit_bytes=5 << 20),
        cost_estimate=pl.CostEstimate(
            flops=4 * tokens * deep * units * len(rows),
            bytes_accessed=4 * len(steps) * deep * units,
            transcendentals=0,
        ),
        name="early",
    )(*rows, gain, *[in_vmem(array) for array in staged], *sums, gate_proj, up_proj)


def run_experts(numbers, rows, gain, staged, sums, down_proj):
    tokens, deep = rows[0].shape
    units = down_proj.shape[1]
    count = len(rows)
    return pl.pallas_call(
        functools.partial(experts_kernel, numbers),
        out_shape=(like((count, tokens, deep)), pltpu.VMEM((tokens, units), BF16))
        + (pltpu.VMEM((units, deep), BF16),) * count,
        in_specs=[VMEM_SPEC] * (3 * count + 1 + 3) + [HBM_SPEC],
        out_specs=(VMEM_SPEC,) * (count + 2),
        scratch_shapes=[
            pltpu.VMEM((tokens, units), F32),
            pltpu.VMEM((tokens, units), F32),
            pltpu.VMEM((count, tokens, deep), BF16),
            pltpu.VMEM((tokens, 128), F32),
            pltpu.VMEM((count, units, deep), BF16),
            pltpu.SemaphoreType.DMA((2 * count,)),
        ],
        compiler_params=pltpu.CompilerParams(vmem_limit_bytes=EXPERTS_MIB << 20),
        cost_estimate=pl.CostEstimate(
            flops=6 * count * tokens * units * deep,
            bytes_accessed=4 * count * units * deep,
            transcendentals=tokens * units,
        ),
        name="experts",
    )(*rows, gain, *[in_vmem(array) for array in staged], *sums, down_proj)


def pair_total_kernel(even_ref, other_ref, *out_refs):
    for k, ref in enumerate(out_refs):
        ref[...] = (even_ref[k].astype(F32) + other_ref[k].astype(F32)).astype(BF16)


def combine_kernel(shape, high_ref, low_ref, *refs):
    half, mp_count = shape[0] // 2, shape[1]
    piece_refs, even_ref, other_ref = refs[: half - 1][::-1], refs[half - 1], refs[half]
    kept_ref, sent_refs = refs[half + 1], refs[half + 2 :]
    own_piece = (even_ref[...].astype(F32) + other_ref[...].astype(F32)).astype(BF16)
    pieces = jnp.concatenate([own_piece] + [ref[...] for ref in piece_refs], axis=0)
    experts = [expert_at(shape, lax.axis_index("ctx") ^ (2 * k)) for k in range(half)]
    total = None
    for table in (high_ref, low_ref):
        spread = jnp.concatenate([table[expert] for expert in experts], axis=0)
        term = lax.dot_general(spread, pieces, (((0,), (0,)), ((), ())), preferred_element_type=F32)
        total = term if total is None else total + term
    rows = kept_ref.shape[0]
    kept_ref[...] = total[:rows]
    for k, ref in enumerate(sent_refs, 1):
        ref[...] = total[k * rows : (k + 1) * rows].astype(BF16)


def exchange_path(
    queries,
    cache_keys,
    cache_values,
    new_keys,
    new_values,
    out_proj,
    residual,
    norm_gain,
    gate_proj,
    up_proj,
    down_proj,
    expert_ids,
    route_logits,
):
    ctx_count = lax.axis_size("ctx")
    mp_count = lax.axis_size("mp")
    shape = (ctx_count, mp_count)
    gate_hbm, up_hbm, down_hbm = in_hbm(gate_proj), in_hbm(up_proj), in_hbm(down_proj)
    tok_local = queries.shape[0]
    tokens = tok_local * ctx_count
    slot_local, cache_local, head_dim = cache_keys.shape
    heads = queries.shape[1] // head_dim
    d_local = out_proj.shape[1]
    res_rows = residual.shape[0]
    half = ctx_count // 2
    rows = half * tok_local
    capacity = tokens * TOP // 4
    per_row = max(1, EXPERTS // mp_count)

    blocks = [queries] + spread([queries] * (half - 1), "ctx", 2)
    own = [cache_keys, cache_values, new_keys, new_values]
    pair = [swap(array, "ctx", 1) for array in own]
    held = stage(gate_hbm, up_hbm, d_local, (), *[in_hbm(array) for array in (*own, queries)])
    held, blocks[1:], pair = lax.optimization_barrier((held, blocks[1:], pair))
    mine = device_call(
        attention_kernel,
        "attention",
        like((heads + 1, rows, head_dim)),
        [in_vmem(array) for array in (held[4], *blocks[1:], *held[:4], *pair)],
        [
            pltpu.VMEM((slot_local, heads // slot_local * rows, head_dim), BF16),
            pltpu.VMEM((slot_local, 2 * tok_local, head_dim), BF16),
            pltpu.VMEM((slot_local, 2 * tok_local, head_dim), BF16),
        ],
        flops=8 * heads * rows * (cache_local + tok_local) * head_dim,
        limit=24,
    )
    others = spread([mine] * (half - 1), "ctx", 2)
    ids, logits, _ = lax.optimization_barrier((expert_ids.T, route_logits.T, mine))
    pick, high, low = device_call(
        functools.partial(tables_kernel, shape),
        "tables",
        (like((per_row, capacity, tokens)),) * 3,
        [ids, logits],
    )
    gain = norm_gain.astype(F32).reshape(ctx_count, 1, d_local)
    gate_later, _ = lax.optimization_barrier((gate_proj, mine))
    *staged, out_proj, residual = stage(
        in_hbm(gate_later), up_hbm, d_local, STAGE_AT[0], in_hbm(out_proj), in_hbm(residual)
    )
    pick, high, low, gain, staged, out_proj, residual, others = lax.optimization_barrier(
        (pick, high, low, gain, staged, out_proj, residual, others)
    )
    attn = device_call(join_kernel, "join", like((rows, heads * head_dim)), [mine] + others)
    block = like((res_rows, d_local))

    kept, *sent = device_call(
        project_kernel,
        "project",
        (like((res_rows, d_local), F32),) + (block,) * (mp_count - 1),
        [attn, swap(attn, "ctx", 1), out_proj],
        [pltpu.VMEM((tokens, heads * head_dim), BF16)],
        flops=2 * tokens * heads * head_dim * d_local,
    )
    arrived = spread(sent, "mp")
    gate_later, _ = lax.optimization_barrier((gate_proj, kept))
    more = stage(in_hbm(gate_later), up_hbm, d_local, STAGE_AT[1])
    more, arrived = lax.optimization_barrier((more, arrived[::-1]))
    arrived = arrived[::-1]
    staged = [*staged, *more]
    hidden = device_call(total_kernel, "hidden", block, [kept, residual] + arrived[::-1])

    everyone = spread([hidden] * (mp_count - 1), "mp")
    gate_later, _ = lax.optimization_barrier((gate_proj, hidden))
    more = stage(in_hbm(gate_later), up_hbm, d_local, STAGE_AT[2])
    more, everyone = lax.optimization_barrier((more, everyone))
    staged, everyone = [*staged, *more], [hidden, *everyone]
    even = device_call(
        functools.partial(pack_kernel, shape),
        "pack",
        (like((capacity, d_local)),) * half,
        [pick] + everyone,
        [pltpu.VMEM((per_row, capacity, d_local), BF16)],
    )
    even = [even[0]] + spread(even[1:], "ctx", 2)
    numbered = [number for steps in STAGE_AT for number in steps]
    odd = swap(even[0], "ctx", 1)
    sums = run_early((0, 1), [even[0], odd], gain, staged[:4], (), STAGE_AT[3], gate_hbm, up_hbm)
    sums, even = lax.optimization_barrier((sums, even[:0:-1]))
    even = even[::-1]
    staged, sums = [*staged, *sums[3:]], sums[:3]
    odd = [swap(piece, "ctx", 1) for piece in even]
    held = {number: staged[2 * at : 2 * at + 2] for at, number in enumerate(numbered[: len(staged) // 2])}
    numbers = tuple(range(2, ctx_count, 2))
    *sums, gate_last, up_last = run_early(
        numbers, even, gain, [array for number in numbers for array in held[number]], sums, STAGE_AT[4], gate_hbm, up_hbm
    )
    odd_numbers = tuple(range(3, ctx_count, 2))
    held[5] = (gate_last, up_last)
    out_odd, act, *even_weights = run_experts(
        odd_numbers, odd, gain, [array for number in odd_numbers for array in held[number]], sums, down_hbm
    )
    out_even = device_call(
        even_columns_kernel,
        "even_columns",
        like((half - 1, capacity, d_local)),
        [in_vmem(array) for array in (act, *even_weights)],
    )
    pieces = device_call(
        pair_total_kernel,
        "pair_total",
        (like((capacity, d_local)),) * (half - 1),
        [out_even, swap(out_odd, "ctx", 1)],
    )
    act, *pieces = lax.optimization_barrier((act, *pieces))
    returned = spread(pieces, "ctx", 2)
    own_even, own_odd = device_call(
        own_columns_kernel,
        "own_columns",
        (like((capacity, d_local)),) * 2,
        [act, down_hbm],
        [
            pltpu.VMEM((capacity, 2 * d_local), F32),
            pltpu.VMEM((2, act.shape[1] // 2, 2 * d_local), BF16),
            pltpu.SemaphoreType.DMA((2,)),
        ],
        specs=[VMEM_SPEC, HBM_SPEC],
        moved=1,
    )
    pieces = returned[::-1] + [own_even, swap(own_odd, "ctx", 1)]
    kept, *sent = device_call(
        functools.partial(combine_kernel, shape),
        "combine",
        (like((res_rows, d_local), F32),) + (block,) * (mp_count - 1),
        [high, low] + pieces,
    )
    arrived = spread(sent, "mp")
    return device_call(total_kernel, "layer_out", block, [kept, hidden] + arrived[::-1])


def on_device(*args):
    queries, cache_keys, out_proj, gate_proj, down_proj = (args[i] for i in (0, 1, 5, 8, 10))
    ctx_count, mp_count = lax.axis_size("ctx"), lax.axis_size("mp")
    per_row = max(1, EXPERTS // mp_count)
    fits = (
        ctx_count == 2 * mp_count
        and ctx_count & (ctx_count - 1) == 0
        and (ctx_count // per_row) % 2 == 0
        and out_proj.shape[1] % 256 == 0
        and gate_proj.shape[2] % 2048 == 0
        and queries.shape[0] % 16 == 0
        and 3 * (queries.shape[1] // cache_keys.shape[2]) <= cache_keys.shape[2]
    )
    return exchange_path(*args) if fits else gathered_path(*args)


def solution(mesh):
    placed = (
        P("ctx", "mp"),
        P("mp", "ctx", None),
        P("mp", "ctx", None),
        P("mp", "ctx", None),
        P("mp", "ctx", None),
        P("mp", "ctx"),
        P("mp", "ctx"),
        P(),
        P("ctx", None, "mp"),
        P("ctx", None, "mp"),
        P("ctx", "mp", None),
        P(),
        P(),
    )
    return jax.shard_map(
        on_device, mesh=mesh, in_specs=placed, out_specs=P("mp", "ctx"), check_vma=False
    )
```

```python
import functools
import math

import jax
import jax.numpy as jnp
from jax import lax
from jax.experimental import pallas as pl
from jax.experimental.pallas import tpu as pltpu
from jax.sharding import PartitionSpec as P

D = 6144
EXPERTS = 8
TOP = 2


neg_big = -1e30
norm_eps = 1e-05


def route_slots(expert_ids):
    flat = expert_ids.reshape(-1)
    onehot = (flat[:, None] == jnp.arange(EXPERTS, dtype=jnp.int32)[None, :]).astype(jnp.int32)
    before = jnp.cumsum(onehot, axis=0, dtype=jnp.int32) - onehot
    return jnp.sum(before * onehot, axis=1, dtype=jnp.int32).reshape(expert_ids.shape)


def softmax_pieces(query_block, keys_local, values_local, allowed, scale):
    scores = (
        jnp.einsum("srd,skd->srk", query_block, keys_local, preferred_element_type=jnp.float32)
        * scale
    )
    scores = jnp.where(allowed[None, :, :], scores, neg_big)
    highest = jnp.max(scores, axis=2)
    expo = jnp.exp(scores - highest[:, :, None])
    denom = jnp.sum(expo, axis=2)
    summed = jnp.einsum(
        "srk,skd->srd", expo.astype(jnp.bfloat16), values_local, preferred_element_type=jnp.float32
    )
    return (highest, denom, summed)


def join_softmax(former, latter):
    highest = jnp.maximum(former[0], latter[0])
    right = jnp.exp(latter[0] - highest)
    denom = latter[1] * right
    summed = latter[2] * right[:, :, None]
    return (highest, denom, summed)


def gathered_path(
    queries,
    cache_keys,
    cache_values,
    new_keys,
    new_values,
    out_proj,
    residual,
    norm_gain,
    gate_proj,
    up_proj,
    down_proj,
    expert_ids,
    route_logits,
):
    ctx_count = lax.axis_size("ctx")
    mp_count = lax.axis_size("mp")
    ctx_index = lax.axis_index("ctx")
    mp_index = lax.axis_index("mp")
    tok_local = queries.shape[0]
    tokens = tok_local * ctx_count
    slot_local = cache_keys.shape[0]
    cache_local = cache_keys.shape[1]
    head_dim = cache_keys.shape[2]
    heads_local = queries.shape[1] // head_dim
    group_size = heads_local // slot_local
    width = cache_local + tok_local
    scale = 1.0 / math.sqrt(head_dim)
    d_local = out_proj.shape[1]
    key_value = jnp.stack(
        [
            jnp.concatenate([cache_keys, new_keys], axis=1),
            jnp.concatenate([cache_values, new_values], axis=1),
        ]
    )
    shaped = queries.reshape(tok_local, slot_local, group_size, head_dim)
    query_block = jnp.transpose(shaped, (1, 2, 0, 3)).reshape(
        slot_local, group_size * tok_local, head_dim
    )
    query_tok = ctx_index * tok_local + jnp.tile(jnp.arange(tok_local, dtype=jnp.int32), group_size)
    query_count = group_size * tok_local
    start_state = (
        jnp.full((slot_local, query_count), neg_big, jnp.float32),
        jnp.zeros((slot_local, query_count), jnp.float32),
        jnp.zeros((slot_local, query_count, head_dim), jnp.float32),
    )
    piece = lax.all_gather(key_value, "ctx", axis=2, tiled=True)
    position = jnp.arange(piece.shape[2], dtype=jnp.int32)
    shard = position // width
    within = position % width
    new_tok = shard * tok_local + within - cache_local
    allowed = (within[None, :] < cache_local) | (new_tok[None, :] <= query_tok[:, None])
    highest, denom, summed = join_softmax(
        start_state, softmax_pieces(query_block, piece[0], piece[1], allowed, scale)
    )
    shaped = (
        (summed / denom[:, :, None])
        .astype(jnp.bfloat16)
        .reshape(slot_local, group_size, tok_local, head_dim)
    )
    attn = jnp.transpose(shaped, (2, 0, 1, 3)).reshape(tok_local, heads_local * head_dim)
    projected = jnp.dot(
        lax.all_gather(attn, "ctx", axis=0, tiled=True),
        out_proj,
        preferred_element_type=jnp.float32,
    )
    res_rows = residual.shape[0]
    res_start = mp_index * res_rows
    current = lax.dynamic_slice_in_dim(projected, res_start, res_rows, 0)
    projected = lax.dynamic_update_slice_in_dim(
        projected, current + residual.astype(jnp.float32), res_start, 0
    )
    hidden = lax.psum(projected.astype(jnp.bfloat16), "mp")
    capacity = tokens * TOP // 4
    slots = route_slots(expert_ids)
    per_row = max(1, EXPERTS // mp_count)
    first_expert = mp_index * EXPERTS // mp_count
    own_expert = (mp_index * ctx_count + ctx_index) * EXPERTS // (ctx_count * mp_count)
    local = own_expert - first_expert
    row_experts = first_expert + jnp.arange(per_row, dtype=jnp.int32)
    match = expert_ids[None, :, :] == row_experts[:, None, None]
    place = jnp.where(match, slots[None, :, :], capacity)
    table = place[:, :, :, None] == jnp.arange(capacity, dtype=jnp.int32)[None, None, None, :]
    pick = jnp.any(table, axis=2)
    packed = jnp.einsum(
        "rtc,td->rcd", pick.astype(jnp.bfloat16), hidden, preferred_element_type=jnp.float32
    ).astype(jnp.bfloat16)
    gate_local = gate_proj[0]
    up_local = up_proj[0]
    down_local = down_proj[0]
    chosen = lax.dynamic_index_in_dim(
        lax.all_gather(packed, "ctx", axis=2, tiled=True), local, 0, keepdims=False
    )
    wide = chosen.astype(jnp.float32)
    gains = norm_gain.astype(jnp.float32)
    scaled = (wide * gains[None, :]).astype(jnp.bfloat16)
    gate_sum = jnp.dot(scaled, gate_local, preferred_element_type=jnp.float32)
    up_sum = jnp.dot(scaled, up_local, preferred_element_type=jnp.float32)
    gate_sum, up_sum, squares = (gate_sum, up_sum, jnp.sum(wide * wide, axis=1))
    rms = lax.rsqrt(squares / D + norm_eps)
    act = (jax.nn.silu(rms[:, None] * gate_sum) * (rms[:, None] * up_sum)).astype(jnp.bfloat16)
    part = lax.dot_general(
        down_local, act, (((0,), (1,)), ((), ())), preferred_element_type=jnp.float32
    )
    returned = lax.psum_scatter(
        jnp.concatenate(
            [jnp.where(local == which, part, 0.0) for which in range(per_row)], axis=1
        ).astype(jnp.bfloat16),
        "ctx",
        scatter_dimension=0,
        tiled=True,
    ).astype(jnp.float32)
    weights = jax.nn.softmax(route_logits, axis=1)
    combine = jnp.sum(jnp.where(table, weights[None, :, :, None], 0.0), axis=2)
    moe = jnp.einsum(
        "drc,rtc->td",
        returned.reshape(d_local, per_row, capacity),
        combine,
        precision=lax.Precision.HIGHEST,
        preferred_element_type=jnp.float32,
    )
    share = lax.psum_scatter(
        moe.astype(jnp.bfloat16), "mp", scatter_dimension=0, tiled=True
    ).astype(jnp.float32)
    own_hidden = lax.dynamic_slice_in_dim(hidden, res_start, res_rows, 0).astype(jnp.float32)
    return (own_hidden + share).astype(jnp.bfloat16)


BF16 = jnp.bfloat16
F32 = jnp.float32
VMEM_SPEC = pl.BlockSpec(memory_space=pltpu.VMEM)
HBM_SPEC = pl.BlockSpec(memory_space=pl.ANY)
SMALL_MIB = 8
STAGE_AT = ((0,), (1, 2, 4), (6,), (3,), (7,), (5,))
EXPERTS_MIB = 12


def swap(array, axis_name, mask):
    count = lax.axis_size(axis_name)
    return lax.ppermute(array, axis_name, [(i, i ^ mask) for i in range(count)])


def spread(arrays, axis_name, unit=1):
    masks = range(unit, unit * (len(arrays) + 1), unit)
    moved = [swap(array, axis_name, mask) for mask, array in reversed(list(zip(masks, arrays)))]
    return moved[::-1]


def device_call(kernel, name, outs, arrays, scratch=(), flops=0, limit=SMALL_MIB, specs=None, moved=0):
    moved = moved or sum(a.size * a.dtype.itemsize for a in arrays)
    return pl.pallas_call(
        kernel,
        out_shape=outs,
        in_specs=specs or [VMEM_SPEC] * len(arrays),
        out_specs=jax.tree.map(lambda _: VMEM_SPEC, outs),
        scratch_shapes=list(scratch),
        compiler_params=pltpu.CompilerParams(vmem_limit_bytes=limit << 20),
        cost_estimate=pl.CostEstimate(flops=flops, bytes_accessed=moved, transcendentals=0),
        name=name,
    )(*arrays)


def in_hbm(array):
    return pltpu.with_memory_space_constraint(array, pltpu.HBM)


def in_vmem(array):
    return pltpu.with_memory_space_constraint(array, pltpu.VMEM)


def like(shape, dtype=BF16):
    return jax.ShapeDtypeStruct(shape, dtype)


def expert_at(shape, ctx_at):
    ctx_count, mp_count = shape
    mp_index = lax.axis_index("mp")
    own = lax.div((mp_index * ctx_count + ctx_at) * EXPERTS, ctx_count * mp_count)
    return own - lax.div(mp_index * EXPERTS, mp_count)


def tables_kernel(shape, ids_ref, logits_ref, pick_ref, high_ref, low_ref):
    mp_index = lax.axis_index("mp")
    mp_count = shape[1]
    per_row, capacity, tokens = pick_ref.shape
    rows = tokens // mp_count
    first = lax.div(mp_index * EXPERTS, mp_count)
    lane = lax.broadcasted_iota(jnp.int32, (1, tokens), 1)

    def by_block(values):
        for bit in range(mp_count.bit_length() - 1):
            size = rows << bit
            forward = pltpu.roll(values, size, 1)
            back = pltpu.roll(values, tokens - size, 1)
            moved = jnp.where((lane & size) != 0, forward, back)
            values = jnp.where(((mp_index >> bit) & 1) == 1, moved, values)
        return values

    logits = logits_ref[...]
    weights = jnp.exp(logits - jnp.max(logits, axis=0, keepdims=True))
    weights = weights / jnp.sum(weights, axis=0, keepdims=True)
    ids = ids_ref[...]
    earlier = lax.broadcasted_iota(jnp.int32, (tokens, tokens), 0) < lax.broadcasted_iota(
        jnp.int32, (tokens, tokens), 1
    )
    earlier = earlier.astype(F32).astype(BF16)
    for which in range(per_row):
        named = (ids == first + which).astype(F32)
        member = jnp.max(named, axis=0, keepdims=True)
        weight = jnp.sum(named * weights, axis=0, keepdims=True)
        slot = jnp.dot(
            jnp.broadcast_to(member, (8, tokens)).astype(BF16), earlier, preferred_element_type=F32
        )[0:1]
        slot = by_block(jnp.where(member > 0, slot, float(capacity)))
        weight = by_block(weight)
        taken = lax.broadcasted_iota(jnp.int32, (capacity, tokens), 0) == slot.astype(jnp.int32)
        pick_ref[which] = jnp.where(taken, 1.0, 0.0).astype(BF16)
        weight = jnp.where(taken, weight, 0.0)
        high = weight.astype(BF16)
        high_ref[which] = high
        low_ref[which] = (weight - high.astype(F32)).astype(BF16)


def attention_kernel(*refs):
    half = len(refs) - 8 - 1 - 3
    query_refs = refs[:half]
    own_k, own_v, new_k, new_v, pair_k, pair_v, pair_nk, pair_nv = refs[half : half + 8]
    mine_ref, query_buf, key_buf, value_buf = refs[half + 8 :]
    own = lax.axis_index("ctx")
    slots, _, head_dim = own_k.shape
    tok_local = new_k.shape[1]
    rows = half * tok_local
    group = query_refs[0].shape[1] // head_dim // slots
    heads = slots * group
    factor = math.log2(math.e) / math.sqrt(head_dim)
    for at, query_ref in enumerate(query_refs):
        for head in range(heads):
            start = (head % group) * rows + at * tok_local
            query_buf[head // group, start : start + tok_local, :] = query_ref[
                :, head * head_dim : (head + 1) * head_dim
            ]
    for part, (key_ref, value_ref) in enumerate(((new_k, new_v), (pair_nk, pair_nv))):
        for slot in range(slots):
            key_buf[slot, part * tok_local : (part + 1) * tok_local, :] = key_ref[slot]
            value_buf[slot, part * tok_local : (part + 1) * tok_local, :] = value_ref[slot]
    row = lax.rem(lax.broadcasted_iota(jnp.int32, (group * rows, 1), 0), rows)
    block = lax.div(row, tok_local)
    row_tok = (own ^ (2 * block)) * tok_local + row - block * tok_local
    column = lax.broadcasted_iota(jnp.int32, (1, 2 * tok_local), 1)
    block = lax.div(column, tok_local)
    key_tok = (own ^ block) * tok_local + column - block * tok_local
    seen = key_tok <= row_tok
    lane = lax.broadcasted_iota(jnp.int32, (rows, head_dim), 1)
    stats = jnp.zeros((rows, head_dim), F32)

    def product(left, right):
        return lax.dot_general(left, right, (((1,), (1,)), ((), ())), preferred_element_type=F32)

    for slot in range(slots):
        query = query_buf[slot]
        first = product(query, own_k[slot]) * factor
        second = product(query, pair_k[slot]) * factor
        third = jnp.where(seen, product(query, key_buf[slot]) * factor, neg_big)
        top = jnp.maximum(
            jnp.max(jnp.maximum(first, second), axis=1, keepdims=True),
            jnp.max(third, axis=1, keepdims=True),
        )
        shift = top.astype(BF16).astype(F32)
        first = jnp.exp2(first - shift)
        second = jnp.exp2(second - shift)
        third = jnp.exp2(third - shift)
        denom = jnp.sum(first + second, axis=1, keepdims=True) + jnp.sum(third, axis=1, keepdims=True)
        summed = jnp.dot(first.astype(BF16), own_v[slot], preferred_element_type=F32)
        summed += jnp.dot(second.astype(BF16), pair_v[slot], preferred_element_type=F32)
        summed += jnp.dot(third.astype(BF16), value_buf[slot], preferred_element_type=F32)
        summed = summed.astype(BF16)
        high = denom.astype(BF16).astype(F32)
        low = denom - high
        for index in range(group):
            head = slot * group + index
            span = slice(index * rows, (index + 1) * rows)
            mine_ref[head] = summed[span]
            stats = jnp.where(lane == head, shift[span], stats)
            stats = jnp.where(lane == heads + head, high[span], stats)
            stats = jnp.where(lane == 2 * heads + head, low[span], stats)
    mine_ref[heads] = stats.astype(BF16)


def join_kernel(*refs):
    part_refs, attn_ref = refs[:-1], refs[-1]
    half = len(part_refs)
    heads, head_dim = part_refs[0].shape[0] - 1, part_refs[0].shape[2]
    tok = part_refs[0].shape[1] // half
    for block in range(half):
        spans = [slice((k ^ block) * tok, ((k ^ block) + 1) * tok) for k in range(half)]
        stats = [ref[heads, span, :].astype(F32) for ref, span in zip(part_refs, spans)]
        highest = functools.reduce(jnp.maximum, stats)
        lifts = [jnp.exp2(stat - highest) for stat in stats]
        denoms = [
            pltpu.roll(stat, head_dim - heads, 1) + pltpu.roll(stat, head_dim - 2 * heads, 1)
            for stat in stats
        ]
        total = sum(lift * denom for lift, denom in zip(lifts, denoms))
        shares = [lift / total for lift in lifts]
        for head in range(heads):
            mixed = sum(
                share[:, head : head + 1] * ref[head, span, :].astype(F32)
                for share, ref, span in zip(shares, part_refs, spans)
            )
            attn_ref[block * tok : (block + 1) * tok, head * head_dim : (head + 1) * head_dim] = mixed.astype(BF16)


def project_kernel(own_ref, pair_ref, weight_ref, kept_ref, *refs):
    sent_refs, left = refs[:-1], refs[-1]
    ctx_index, mp_index = lax.axis_index("ctx"), lax.axis_index("mp")
    mp_count = len(sent_refs) + 1
    tok = own_ref.shape[0] // mp_count
    odd = ctx_index & 1
    pair_at = (ctx_index >> 1) ^ mp_index
    for k in range(mp_count):
        source = pl.ds(pl.multiple_of((pair_at ^ k) * tok, tok), tok)
        left[pl.ds(pl.multiple_of((2 * k + odd) * tok, tok), tok), :] = own_ref[source, :]
        left[pl.ds(pl.multiple_of((2 * k + 1 - odd) * tok, tok), tok), :] = pair_ref[source, :]
    projected = jnp.dot(left[...], weight_ref[...], preferred_element_type=F32)
    kept_ref[...] = projected[: 2 * tok]
    for k, ref in enumerate(sent_refs, 1):
        ref[...] = projected[2 * k * tok : 2 * (k + 1) * tok].astype(BF16)


def total_kernel(*refs):
    total = refs[0][...].astype(F32)
    for ref in refs[1:-1]:
        total = total + ref[...].astype(F32)
    refs[-1][...] = total.astype(BF16)


def pack_kernel(shape, pick_ref, *refs):
    mp_count, half = shape[1], shape[0] // 2
    hidden_refs, out_refs, packed = refs[:mp_count], refs[mp_count:-1], refs[-1]
    hidden = jnp.concatenate([ref[...] for ref in hidden_refs], axis=0)
    for which in range(pick_ref.shape[0]):
        packed[which] = jnp.dot(pick_ref[which], hidden, preferred_element_type=F32).astype(BF16)
    for k in range(half):
        out_refs[k][...] = packed[expert_at(shape, lax.axis_index("ctx") ^ (2 * k))]


def own_block(body):
    pl.when(lax.axis_index("ctx") >= 0)(body)


def block_rows(step, deep):
    return pl.ds(pl.multiple_of((lax.axis_index("ctx") ^ step) * deep, deep), deep)


def stage_copies(steps, gate_hbm, up_hbm, outs, sem):
    copies = []
    for at, step in enumerate(steps):
        rows = block_rows(step, outs[0].shape[0])
        copies.append(pltpu.make_async_copy(gate_hbm.at[0, rows, :], outs[2 * at], sem.at[2 * at]))
        copies.append(pltpu.make_async_copy(up_hbm.at[0, rows, :], outs[2 * at + 1], sem.at[2 * at + 1]))
    return copies


def stage_kernel(steps, *refs):
    gate_hbm, up_hbm = refs[:2]
    extra = (len(refs) - 4 - 2 * len(steps)) // 2
    plain, outs = refs[2 : 2 + extra], refs[2 + extra : -2 - extra]
    plain_out, sem, plain_sem = refs[-2 - extra : -2], refs[-2], refs[-1]
    copies = [
        pltpu.make_async_copy(source, target, plain_sem.at[at])
        for at, (source, target) in enumerate(zip(plain, plain_out))
    ]
    copies += stage_copies(steps, gate_hbm, up_hbm, outs, sem)
    for copy in copies:
        copy.start()
    for copy in copies:
        copy.wait()


def staged_like(steps, deep, units):
    return (pltpu.VMEM((deep, units), BF16),) * (2 * len(steps))


def stage(gate_proj, up_proj, deep, steps, *plain):
    units = gate_proj.shape[2]
    return pl.pallas_call(
        functools.partial(stage_kernel, steps),
        out_shape=staged_like(steps, deep, units) + tuple(pltpu.VMEM(a.shape, a.dtype) for a in plain),
        in_specs=[HBM_SPEC] * (2 + len(plain)),
        out_specs=(VMEM_SPEC,) * (2 * len(steps) + len(plain)),
        scratch_shapes=[
            pltpu.SemaphoreType.DMA((max(1, 2 * len(steps)),)),
            pltpu.SemaphoreType.DMA((max(1, len(plain)),)),
        ],
        compiler_params=pltpu.CompilerParams(vmem_limit_bytes=2 << 20),
        cost_estimate=pl.CostEstimate(flops=0, bytes_accessed=4 * len(steps) * deep * units, transcendentals=0),
        name="stage",
    )(gate_proj, up_proj, *plain)


def scaled_rows(row_ref, gain_ref, step):
    wide = row_ref[...].astype(F32)
    squares = jnp.sum(wide * wide, axis=1, keepdims=True)
    return squares, (wide * gain_ref[lax.axis_index("ctx") ^ step]).astype(BF16)


def early_kernel(numbers, steps, *refs):
    count, begun = len(numbers), 0 not in numbers
    row_refs, gain_ref, weight_refs, refs = refs[:count], refs[count], refs[count + 1 : 3 * count + 1], refs[3 * count + 1 :]
    sums_in, refs = (refs[:3], refs[3:]) if begun else (None, refs)
    gate_hbm, up_hbm, gate_acc, up_acc, squares_ref = refs[:5]
    scaled_ref = refs[-1]
    copies = stage_copies(steps, gate_hbm, up_hbm, refs[5:-2], refs[-2]) if steps else []
    for copy in copies:
        copy.start()
    squares = sums_in[2][:, 0:1] if begun else 0.0
    for at, number in enumerate(numbers):
        more, scaled_ref[at] = scaled_rows(row_refs[at], gain_ref, number)
        squares = squares + more
    for at in range(count):

        @own_block
        def _():
            for which, acc in enumerate((gate_acc, up_acc)):
                term = jnp.dot(scaled_ref[at], weight_refs[2 * at + which][...], preferred_element_type=F32)
                if at:
                    term = acc[...] + term
                elif begun:
                    term = sums_in[which][...] + term
                acc[...] = term

    squares_ref[...] = jnp.broadcast_to(squares, squares_ref.shape)
    for copy in copies:
        copy.wait()


def experts_kernel(numbers, *refs):
    count = len(numbers)
    row_refs, gain_ref, weight_refs, refs = refs[:count], refs[count], refs[count + 1 : 3 * count + 1], refs[3 * count + 1 :]
    gate_in, up_in, squares_ref, down_hbm, odd_ref, act_ref = refs[:6]
    even_refs, (gate_acc, up_acc, scaled_ref, squares_acc, odd_buf, sem) = refs[6:-6], refs[-6:]
    chips = len(even_refs)
    deep = odd_ref.shape[2]
    targets = [(2 * k + 3, odd_buf.at[k]) for k in range(chips)] + [(2 * k + 2, ref) for k, ref in enumerate(even_refs)]
    copies = [
        pltpu.make_async_copy(down_hbm.at[0, :, block_rows(number, deep)], target, sem.at[at])
        for at, (number, target) in enumerate(targets)
    ]
    for copy in copies[:chips]:
        copy.start()
    squares = squares_ref[:, 0:1]
    for order, number in enumerate(numbers):
        more, scaled_ref[order] = scaled_rows(row_refs[order], gain_ref, number)
        squares = squares + more
    squares_acc[...] = jnp.broadcast_to(squares, squares_acc.shape)
    for order in range(count):

        @own_block
        def _():
            for which, (acc, start) in enumerate(((gate_acc, gate_in), (up_acc, up_in))):
                former = acc if order else start
                weights = weight_refs[2 * order + which]
                acc[...] = former[...] + jnp.dot(scaled_ref[order], weights[...], preferred_element_type=F32)

        for copy in copies[chips + order : chips + order + 1]:
            copy.start()
    rms = lax.rsqrt(squares_acc[:, 0:1] / D + norm_eps)
    gate = rms * gate_acc[...]
    act_ref[...] = (gate / (1.0 + jnp.exp(-gate)) * (rms * up_acc[...])).astype(BF16)
    for k in range(chips):
        copies[k].wait()

        @own_block
        def _():
            odd_ref[k] = jnp.dot(act_ref[...], odd_buf[k], preferred_element_type=F32).astype(BF16)

    for copy in copies[chips:]:
        copy.wait()


def even_columns_kernel(act_ref, *refs):
    weight_refs, (down_hbm, even_ref, odd_weight_ref, sem) = refs[:-4], refs[-4:]
    copy = pltpu.make_async_copy(down_hbm.at[0, :, block_rows(1, odd_weight_ref.shape[1])], odd_weight_ref, sem)
    copy.start()
    for k, weight_ref in enumerate(weight_refs):

        @own_block
        def _():
            even_ref[k] = jnp.dot(act_ref[...], weight_ref[...], preferred_element_type=F32).astype(BF16)

    copy.wait()


def own_columns_kernel(act_ref, odd_weight_ref, down_hbm, even_ref, odd_ref, even_weight, sem):
    parts, rows = even_weight.shape[0], even_weight.shape[1]
    columns = block_rows(0, even_weight.shape[2])
    copies = [
        pltpu.make_async_copy(down_hbm.at[0, part * rows : (part + 1) * rows, columns], even_weight.at[part], sem.at[part])
        for part in range(parts)
    ]
    for copy in copies:
        copy.start()

    @own_block
    def _():
        odd_ref[...] = jnp.dot(act_ref[...], odd_weight_ref[...], preferred_element_type=F32).astype(BF16)

    total = 0.0
    for copy in copies:
        copy.wait()
    for part in range(parts):
        total += jnp.dot(act_ref[:, part * rows : (part + 1) * rows], even_weight[part], preferred_element_type=F32)
    even_ref[...] = total.astype(BF16)


def run_early(numbers, rows, gain, staged, sums, steps, gate_proj, up_proj):
    tokens, deep = rows[0].shape
    units = gate_proj.shape[2]
    acc = pltpu.VMEM((tokens, units), F32)
    outs = (acc, acc, pltpu.VMEM((tokens, 128), F32)) + (staged_like(steps, deep, units) if steps else ())
    return pl.pallas_call(
        functools.partial(early_kernel, numbers, steps),
        out_shape=outs,
        in_specs=[VMEM_SPEC] * (len(rows) + 1 + len(staged) + len(sums)) + [HBM_SPEC] * 2,
        out_specs=(VMEM_SPEC,) * len(outs),
        scratch_shapes=([pltpu.SemaphoreType.DMA((2 * len(steps),))] if steps else [])
        + [pltpu.VMEM((len(rows), tokens, deep), BF16)],
        compiler_params=pltpu.CompilerParams(vmem_limit_bytes=5 << 20),
        cost_estimate=pl.CostEstimate(
            flops=4 * tokens * deep * units * len(rows),
            bytes_accessed=4 * len(steps) * deep * units,
            transcendentals=0,
        ),
        name="early",
    )(*rows, gain, *[in_vmem(array) for array in staged], *sums, gate_proj, up_proj)


def run_experts(numbers, rows, gain, staged, sums, down_proj):
    tokens, deep = rows[0].shape
    units = down_proj.shape[1]
    count = len(rows)
    return pl.pallas_call(
        functools.partial(experts_kernel, numbers),
        out_shape=(like((count, tokens, deep)), pltpu.VMEM((tokens, units), BF16))
        + (pltpu.VMEM((units, deep), BF16),) * count,
        in_specs=[VMEM_SPEC] * (3 * count + 1 + 3) + [HBM_SPEC],
        out_specs=(VMEM_SPEC,) * (count + 2),
        scratch_shapes=[
            pltpu.VMEM((tokens, units), F32),
            pltpu.VMEM((tokens, units), F32),
            pltpu.VMEM((count, tokens, deep), BF16),
            pltpu.VMEM((tokens, 128), F32),
            pltpu.VMEM((count, units, deep), BF16),
            pltpu.SemaphoreType.DMA((2 * count,)),
        ],
        compiler_params=pltpu.CompilerParams(vmem_limit_bytes=EXPERTS_MIB << 20),
        cost_estimate=pl.CostEstimate(
            flops=6 * count * tokens * units * deep,
            bytes_accessed=4 * count * units * deep,
            transcendentals=tokens * units,
        ),
        name="experts",
    )(*rows, gain, *[in_vmem(array) for array in staged], *sums, down_proj)


def pair_total_kernel(even_ref, other_ref, *out_refs):
    for k, ref in enumerate(out_refs):
        ref[...] = (even_ref[k].astype(F32) + other_ref[k].astype(F32)).astype(BF16)


def combine_kernel(shape, high_ref, low_ref, *refs):
    half, mp_count = shape[0] // 2, shape[1]
    piece_refs, even_ref, other_ref = refs[: half - 1][::-1], refs[half - 1], refs[half]
    kept_ref, sent_refs = refs[half + 1], refs[half + 2 :]
    own_piece = (even_ref[...].astype(F32) + other_ref[...].astype(F32)).astype(BF16)
    pieces = jnp.concatenate([own_piece] + [ref[...] for ref in piece_refs], axis=0)
    experts = [expert_at(shape, lax.axis_index("ctx") ^ (2 * k)) for k in range(half)]
    total = None
    for table in (high_ref, low_ref):
        spread = jnp.concatenate([table[expert] for expert in experts], axis=0)
        term = lax.dot_general(spread, pieces, (((0,), (0,)), ((), ())), preferred_element_type=F32)
        total = term if total is None else total + term
    rows = kept_ref.shape[0]
    kept_ref[...] = total[:rows]
    for k, ref in enumerate(sent_refs, 1):
        ref[...] = total[k * rows : (k + 1) * rows].astype(BF16)


def exchange_path(
    queries,
    cache_keys,
    cache_values,
    new_keys,
    new_values,
    out_proj,
    residual,
    norm_gain,
    gate_proj,
    up_proj,
    down_proj,
    expert_ids,
    route_logits,
):
    ctx_count = lax.axis_size("ctx")
    mp_count = lax.axis_size("mp")
    shape = (ctx_count, mp_count)
    gate_hbm, up_hbm, down_hbm = in_hbm(gate_proj), in_hbm(up_proj), in_hbm(down_proj)
    tok_local = queries.shape[0]
    tokens = tok_local * ctx_count
    slot_local, cache_local, head_dim = cache_keys.shape
    heads = queries.shape[1] // head_dim
    d_local = out_proj.shape[1]
    res_rows = residual.shape[0]
    half = ctx_count // 2
    rows = half * tok_local
    capacity = tokens * TOP // 4
    per_row = max(1, EXPERTS // mp_count)

    blocks = [queries] + spread([queries] * (half - 1), "ctx", 2)
    own = [cache_keys, cache_values, new_keys, new_values]
    pair = [swap(array, "ctx", 1) for array in own]
    held = stage(gate_hbm, up_hbm, d_local, STAGE_AT[0], *[in_hbm(array) for array in (*own, queries)])
    held, blocks[1:], pair = lax.optimization_barrier((held, blocks[1:], pair))
    begun, held = held[: 2 * len(STAGE_AT[0])], held[2 * len(STAGE_AT[0]) :]
    mine = device_call(
        attention_kernel,
        "attention",
        like((heads + 1, rows, head_dim)),
        [in_vmem(array) for array in (held[4], *blocks[1:], *held[:4], *pair)],
        [
            pltpu.VMEM((slot_local, heads // slot_local * rows, head_dim), BF16),
            pltpu.VMEM((slot_local, 2 * tok_local, head_dim), BF16),
            pltpu.VMEM((slot_local, 2 * tok_local, head_dim), BF16),
        ],
        flops=8 * heads * rows * (cache_local + tok_local) * head_dim,
        limit=24,
    )
    others = spread([mine] * (half - 1), "ctx", 2)
    ids, logits, _ = lax.optimization_barrier((expert_ids.T, route_logits.T, mine))
    pick, high, low = device_call(
        functools.partial(tables_kernel, shape),
        "tables",
        (like((per_row, capacity, tokens)),) * 3,
        [ids, logits],
    )
    gain = norm_gain.astype(F32).reshape(ctx_count, 1, d_local)
    gate_later, _ = lax.optimization_barrier((gate_proj, mine))
    *staged, out_proj, residual = stage(
        in_hbm(gate_later), up_hbm, d_local, STAGE_AT[1], in_hbm(out_proj), in_hbm(residual)
    )
    staged = [*begun, *staged]
    pick, high, low, gain, staged, out_proj, residual, others = lax.optimization_barrier(
        (pick, high, low, gain, staged, out_proj, residual, others)
    )
    attn = device_call(join_kernel, "join", like((rows, heads * head_dim)), [mine] + others)
    block = like((res_rows, d_local))

    kept, *sent = device_call(
        project_kernel,
        "project",
        (like((res_rows, d_local), F32),) + (block,) * (mp_count - 1),
        [attn, swap(attn, "ctx", 1), out_proj],
        [pltpu.VMEM((tokens, heads * head_dim), BF16)],
        flops=2 * tokens * heads * head_dim * d_local,
    )
    arrived = spread(sent, "mp")
    gate_later, _ = lax.optimization_barrier((gate_proj, kept))
    more = stage(in_hbm(gate_later), up_hbm, d_local, STAGE_AT[2])
    more, arrived = lax.optimization_barrier((more, arrived[::-1]))
    arrived = arrived[::-1]
    staged = [*staged, *more]
    hidden = device_call(total_kernel, "hidden", block, [kept, residual] + arrived[::-1])

    everyone = spread([hidden] * (mp_count - 1), "mp")
    gate_later, _ = lax.optimization_barrier((gate_proj, hidden))
    more = stage(in_hbm(gate_later), up_hbm, d_local, STAGE_AT[3])
    more, everyone = lax.optimization_barrier((more, everyone))
    staged, everyone = [*staged, *more], [hidden, *everyone]
    even = device_call(
        functools.partial(pack_kernel, shape),
        "pack",
        (like((capacity, d_local)),) * half,
        [pick] + everyone,
        [pltpu.VMEM((per_row, capacity, d_local), BF16)],
    )
    even = [even[0]] + spread(even[1:], "ctx", 2)
    numbered = [number for steps in STAGE_AT for number in steps]
    odd = swap(even[0], "ctx", 1)
    sums = run_early((0, 1), [even[0], odd], gain, staged[:4], (), STAGE_AT[4], gate_hbm, up_hbm)
    sums, even = lax.optimization_barrier((sums, even[:0:-1]))
    even = even[::-1]
    staged, sums = [*staged, *sums[3:]], sums[:3]
    odd = [swap(piece, "ctx", 1) for piece in even]
    held = {number: staged[2 * at : 2 * at + 2] for at, number in enumerate(numbered[: len(staged) // 2])}
    numbers = tuple(range(2, ctx_count, 2))
    *sums, gate_last, up_last = run_early(
        numbers, even, gain, [array for number in numbers for array in held[number]], sums, STAGE_AT[5], gate_hbm, up_hbm
    )
    odd_numbers = tuple(range(3, ctx_count, 2))
    held[5] = (gate_last, up_last)
    out_odd, act, *even_weights = run_experts(
        odd_numbers, odd, gain, [array for number in odd_numbers for array in held[number]], sums, down_hbm
    )
    out_even, odd_weight = device_call(
        even_columns_kernel,
        "even_columns",
        (like((half - 1, capacity, d_local)), pltpu.VMEM((act.shape[1], d_local), BF16)),
        [in_vmem(array) for array in (act, *even_weights)] + [down_hbm],
        [pltpu.SemaphoreType.DMA(())],
        specs=[VMEM_SPEC] * half + [HBM_SPEC],
        moved=2 * act.shape[1] * d_local,
    )
    pieces = device_call(
        pair_total_kernel,
        "pair_total",
        (like((capacity, d_local)),) * (half - 1),
        [out_even, swap(out_odd, "ctx", 1)],
    )
    act, *pieces = lax.optimization_barrier((act, *pieces))
    returned = spread(pieces, "ctx", 2)
    own_even, own_odd = device_call(
        own_columns_kernel,
        "own_columns",
        (like((capacity, d_local)),) * 2,
        [act, in_vmem(odd_weight), down_hbm],
        [pltpu.VMEM((2, act.shape[1] // 2, d_local), BF16), pltpu.SemaphoreType.DMA((2,))],
        specs=[VMEM_SPEC, VMEM_SPEC, HBM_SPEC],
        moved=1,
    )
    pieces = returned[::-1] + [own_even, swap(own_odd, "ctx", 1)]
    kept, *sent = device_call(
        functools.partial(combine_kernel, shape),
        "combine",
        (like((res_rows, d_local), F32),) + (block,) * (mp_count - 1),
        [high, low] + pieces,
    )
    arrived = spread(sent, "mp")
    return device_call(total_kernel, "layer_out", block, [kept, hidden] + arrived[::-1])


def on_device(*args):
    queries, cache_keys, out_proj, gate_proj, down_proj = (args[i] for i in (0, 1, 5, 8, 10))
    ctx_count, mp_count = lax.axis_size("ctx"), lax.axis_size("mp")
    per_row = max(1, EXPERTS // mp_count)
    fits = (
        ctx_count == 2 * mp_count
        and ctx_count & (ctx_count - 1) == 0
        and (ctx_count // per_row) % 2 == 0
        and out_proj.shape[1] % 256 == 0
        and gate_proj.shape[2] % 2048 == 0
        and queries.shape[0] % 16 == 0
        and 3 * (queries.shape[1] // cache_keys.shape[2]) <= cache_keys.shape[2]
    )
    return exchange_path(*args) if fits else gathered_path(*args)


def solution(mesh):
    placed = (
        P("ctx", "mp"),
        P("mp", "ctx", None),
        P("mp", "ctx", None),
        P("mp", "ctx", None),
        P("mp", "ctx", None),
        P("mp", "ctx"),
        P("mp", "ctx"),
        P(),
        P("ctx", None, "mp"),
        P("ctx", None, "mp"),
        P("ctx", "mp", None),
        P(),
        P(),
    )
    return jax.shard_map(
        on_device, mesh=mesh, in_specs=placed, out_specs=P("mp", "ctx"), check_vma=False
    )
```

```python
import functools
import math

import jax
import jax.numpy as jnp
from jax import lax
from jax.experimental import pallas as pl
from jax.experimental.pallas import tpu as pltpu
from jax.sharding import PartitionSpec as P

D = 6144
EXPERTS = 8
TOP = 2


neg_big = -1e30
norm_eps = 1e-05


def route_slots(expert_ids):
    flat = expert_ids.reshape(-1)
    onehot = (flat[:, None] == jnp.arange(EXPERTS, dtype=jnp.int32)[None, :]).astype(jnp.int32)
    before = jnp.cumsum(onehot, axis=0, dtype=jnp.int32) - onehot
    return jnp.sum(before * onehot, axis=1, dtype=jnp.int32).reshape(expert_ids.shape)


def softmax_pieces(query_block, keys_local, values_local, allowed, scale):
    scores = (
        jnp.einsum("srd,skd->srk", query_block, keys_local, preferred_element_type=jnp.float32)
        * scale
    )
    scores = jnp.where(allowed[None, :, :], scores, neg_big)
    highest = jnp.max(scores, axis=2)
    expo = jnp.exp(scores - highest[:, :, None])
    denom = jnp.sum(expo, axis=2)
    summed = jnp.einsum(
        "srk,skd->srd", expo.astype(jnp.bfloat16), values_local, preferred_element_type=jnp.float32
    )
    return (highest, denom, summed)


def join_softmax(former, latter):
    highest = jnp.maximum(former[0], latter[0])
    right = jnp.exp(latter[0] - highest)
    denom = latter[1] * right
    summed = latter[2] * right[:, :, None]
    return (highest, denom, summed)


def gathered_path(
    queries,
    cache_keys,
    cache_values,
    new_keys,
    new_values,
    out_proj,
    residual,
    norm_gain,
    gate_proj,
    up_proj,
    down_proj,
    expert_ids,
    route_logits,
):
    ctx_count = lax.axis_size("ctx")
    mp_count = lax.axis_size("mp")
    ctx_index = lax.axis_index("ctx")
    mp_index = lax.axis_index("mp")
    tok_local = queries.shape[0]
    tokens = tok_local * ctx_count
    slot_local = cache_keys.shape[0]
    cache_local = cache_keys.shape[1]
    head_dim = cache_keys.shape[2]
    heads_local = queries.shape[1] // head_dim
    group_size = heads_local // slot_local
    width = cache_local + tok_local
    scale = 1.0 / math.sqrt(head_dim)
    d_local = out_proj.shape[1]
    key_value = jnp.stack(
        [
            jnp.concatenate([cache_keys, new_keys], axis=1),
            jnp.concatenate([cache_values, new_values], axis=1),
        ]
    )
    shaped = queries.reshape(tok_local, slot_local, group_size, head_dim)
    query_block = jnp.transpose(shaped, (1, 2, 0, 3)).reshape(
        slot_local, group_size * tok_local, head_dim
    )
    query_tok = ctx_index * tok_local + jnp.tile(jnp.arange(tok_local, dtype=jnp.int32), group_size)
    query_count = group_size * tok_local
    start_state = (
        jnp.full((slot_local, query_count), neg_big, jnp.float32),
        jnp.zeros((slot_local, query_count), jnp.float32),
        jnp.zeros((slot_local, query_count, head_dim), jnp.float32),
    )
    piece = lax.all_gather(key_value, "ctx", axis=2, tiled=True)
    position = jnp.arange(piece.shape[2], dtype=jnp.int32)
    shard = position // width
    within = position % width
    new_tok = shard * tok_local + within - cache_local
    allowed = (within[None, :] < cache_local) | (new_tok[None, :] <= query_tok[:, None])
    highest, denom, summed = join_softmax(
        start_state, softmax_pieces(query_block, piece[0], piece[1], allowed, scale)
    )
    shaped = (
        (summed / denom[:, :, None])
        .astype(jnp.bfloat16)
        .reshape(slot_local, group_size, tok_local, head_dim)
    )
    attn = jnp.transpose(shaped, (2, 0, 1, 3)).reshape(tok_local, heads_local * head_dim)
    projected = jnp.dot(
        lax.all_gather(attn, "ctx", axis=0, tiled=True),
        out_proj,
        preferred_element_type=jnp.float32,
    )
    res_rows = residual.shape[0]
    res_start = mp_index * res_rows
    current = lax.dynamic_slice_in_dim(projected, res_start, res_rows, 0)
    projected = lax.dynamic_update_slice_in_dim(
        projected, current + residual.astype(jnp.float32), res_start, 0
    )
    hidden = lax.psum(projected.astype(jnp.bfloat16), "mp")
    capacity = tokens * TOP // 4
    slots = route_slots(expert_ids)
    per_row = max(1, EXPERTS // mp_count)
    first_expert = mp_index * EXPERTS // mp_count
    own_expert = (mp_index * ctx_count + ctx_index) * EXPERTS // (ctx_count * mp_count)
    local = own_expert - first_expert
    row_experts = first_expert + jnp.arange(per_row, dtype=jnp.int32)
    match = expert_ids[None, :, :] == row_experts[:, None, None]
    place = jnp.where(match, slots[None, :, :], capacity)
    table = place[:, :, :, None] == jnp.arange(capacity, dtype=jnp.int32)[None, None, None, :]
    pick = jnp.any(table, axis=2)
    packed = jnp.einsum(
        "rtc,td->rcd", pick.astype(jnp.bfloat16), hidden, preferred_element_type=jnp.float32
    ).astype(jnp.bfloat16)
    gate_local = gate_proj[0]
    up_local = up_proj[0]
    down_local = down_proj[0]
    chosen = lax.dynamic_index_in_dim(
        lax.all_gather(packed, "ctx", axis=2, tiled=True), local, 0, keepdims=False
    )
    wide = chosen.astype(jnp.float32)
    gains = norm_gain.astype(jnp.float32)
    scaled = (wide * gains[None, :]).astype(jnp.bfloat16)
    gate_sum = jnp.dot(scaled, gate_local, preferred_element_type=jnp.float32)
    up_sum = jnp.dot(scaled, up_local, preferred_element_type=jnp.float32)
    gate_sum, up_sum, squares = (gate_sum, up_sum, jnp.sum(wide * wide, axis=1))
    rms = lax.rsqrt(squares / D + norm_eps)
    act = (jax.nn.silu(rms[:, None] * gate_sum) * (rms[:, None] * up_sum)).astype(jnp.bfloat16)
    part = lax.dot_general(
        down_local, act, (((0,), (1,)), ((), ())), preferred_element_type=jnp.float32
    )
    returned = lax.psum_scatter(
        jnp.concatenate(
            [jnp.where(local == which, part, 0.0) for which in range(per_row)], axis=1
        ).astype(jnp.bfloat16),
        "ctx",
        scatter_dimension=0,
        tiled=True,
    ).astype(jnp.float32)
    weights = jax.nn.softmax(route_logits, axis=1)
    combine = jnp.sum(jnp.where(table, weights[None, :, :, None], 0.0), axis=2)
    moe = jnp.einsum(
        "drc,rtc->td",
        returned.reshape(d_local, per_row, capacity),
        combine,
        precision=lax.Precision.HIGHEST,
        preferred_element_type=jnp.float32,
    )
    share = lax.psum_scatter(
        moe.astype(jnp.bfloat16), "mp", scatter_dimension=0, tiled=True
    ).astype(jnp.float32)
    own_hidden = lax.dynamic_slice_in_dim(hidden, res_start, res_rows, 0).astype(jnp.float32)
    return (own_hidden + share).astype(jnp.bfloat16)


BF16 = jnp.bfloat16
F32 = jnp.float32
VMEM_SPEC = pl.BlockSpec(memory_space=pltpu.VMEM)
HBM_SPEC = pl.BlockSpec(memory_space=pl.ANY)
SMALL_MIB = 8
STAGE_AT = ((0,), (1, 2, 4), (6,), (3,), (7,), (5,))
EXPERTS_MIB = 9


def swap(array, axis_name, mask):
    count = lax.axis_size(axis_name)
    return lax.ppermute(array, axis_name, [(i, i ^ mask) for i in range(count)])


def spread(arrays, axis_name, unit=1):
    masks = range(unit, unit * (len(arrays) + 1), unit)
    moved = [swap(array, axis_name, mask) for mask, array in reversed(list(zip(masks, arrays)))]
    return moved[::-1]


def device_call(kernel, name, outs, arrays, scratch=(), flops=0, limit=SMALL_MIB, specs=None, moved=0):
    moved = moved or sum(a.size * a.dtype.itemsize for a in arrays)
    return pl.pallas_call(
        kernel,
        out_shape=outs,
        in_specs=specs or [VMEM_SPEC] * len(arrays),
        out_specs=jax.tree.map(lambda _: VMEM_SPEC, outs),
        scratch_shapes=list(scratch),
        compiler_params=pltpu.CompilerParams(vmem_limit_bytes=limit << 20),
        cost_estimate=pl.CostEstimate(flops=flops, bytes_accessed=moved, transcendentals=0),
        name=name,
    )(*arrays)


def in_hbm(array):
    return pltpu.with_memory_space_constraint(array, pltpu.HBM)


def in_vmem(array):
    return pltpu.with_memory_space_constraint(array, pltpu.VMEM)


def like(shape, dtype=BF16):
    return jax.ShapeDtypeStruct(shape, dtype)


def expert_at(shape, ctx_at):
    ctx_count, mp_count = shape
    mp_index = lax.axis_index("mp")
    own = lax.div((mp_index * ctx_count + ctx_at) * EXPERTS, ctx_count * mp_count)
    return own - lax.div(mp_index * EXPERTS, mp_count)


def tables_kernel(shape, ids_ref, logits_ref, pick_ref, high_ref, low_ref):
    mp_index = lax.axis_index("mp")
    mp_count = shape[1]
    per_row, capacity, tokens = pick_ref.shape
    rows = tokens // mp_count
    first = lax.div(mp_index * EXPERTS, mp_count)
    lane = lax.broadcasted_iota(jnp.int32, (1, tokens), 1)

    def by_block(values):
        for bit in range(mp_count.bit_length() - 1):
            size = rows << bit
            forward = pltpu.roll(values, size, 1)
            back = pltpu.roll(values, tokens - size, 1)
            moved = jnp.where((lane & size) != 0, forward, back)
            values = jnp.where(((mp_index >> bit) & 1) == 1, moved, values)
        return values

    logits = logits_ref[...]
    weights = jnp.exp(logits - jnp.max(logits, axis=0, keepdims=True))
    weights = weights / jnp.sum(weights, axis=0, keepdims=True)
    ids = ids_ref[...]
    earlier = lax.broadcasted_iota(jnp.int32, (tokens, tokens), 0) < lax.broadcasted_iota(
        jnp.int32, (tokens, tokens), 1
    )
    earlier = earlier.astype(F32).astype(BF16)
    for which in range(per_row):
        named = (ids == first + which).astype(F32)
        member = jnp.max(named, axis=0, keepdims=True)
        weight = jnp.sum(named * weights, axis=0, keepdims=True)
        slot = jnp.dot(
            jnp.broadcast_to(member, (8, tokens)).astype(BF16), earlier, preferred_element_type=F32
        )[0:1]
        slot = by_block(jnp.where(member > 0, slot, float(capacity)))
        weight = by_block(weight)
        taken = lax.broadcasted_iota(jnp.int32, (capacity, tokens), 0) == slot.astype(jnp.int32)
        pick_ref[which] = jnp.where(taken, 1.0, 0.0).astype(BF16)
        weight = jnp.where(taken, weight, 0.0)
        high = weight.astype(BF16)
        high_ref[which] = high
        low_ref[which] = (weight - high.astype(F32)).astype(BF16)


def attention_kernel(*refs):
    half = len(refs) - 8 - 1 - 3
    query_refs = refs[:half]
    own_k, own_v, new_k, new_v, pair_k, pair_v, pair_nk, pair_nv = refs[half : half + 8]
    mine_ref, query_buf, key_buf, value_buf = refs[half + 8 :]
    own = lax.axis_index("ctx")
    slots, _, head_dim = own_k.shape
    tok_local = new_k.shape[1]
    rows = half * tok_local
    group = query_refs[0].shape[1] // head_dim // slots
    heads = slots * group
    factor = math.log2(math.e) / math.sqrt(head_dim)
    for at, query_ref in enumerate(query_refs):
        for head in range(heads):
            start = (head % group) * rows + at * tok_local
            query_buf[head // group, start : start + tok_local, :] = query_ref[
                :, head * head_dim : (head + 1) * head_dim
            ]
    for part, (key_ref, value_ref) in enumerate(((new_k, new_v), (pair_nk, pair_nv))):
        for slot in range(slots):
            key_buf[slot, part * tok_local : (part + 1) * tok_local, :] = key_ref[slot]
            value_buf[slot, part * tok_local : (part + 1) * tok_local, :] = value_ref[slot]
    row = lax.rem(lax.broadcasted_iota(jnp.int32, (group * rows, 1), 0), rows)
    block = lax.div(row, tok_local)
    row_tok = (own ^ (2 * block)) * tok_local + row - block * tok_local
    column = lax.broadcasted_iota(jnp.int32, (1, 2 * tok_local), 1)
    block = lax.div(column, tok_local)
    key_tok = (own ^ block) * tok_local + column - block * tok_local
    seen = key_tok <= row_tok
    lane = lax.broadcasted_iota(jnp.int32, (rows, head_dim), 1)
    stats = jnp.zeros((rows, head_dim), F32)

    def product(left, right):
        return lax.dot_general(left, right, (((1,), (1,)), ((), ())), preferred_element_type=F32)

    for slot in range(slots):
        query = query_buf[slot]
        first = product(query, own_k[slot]) * factor
        second = product(query, pair_k[slot]) * factor
        third = jnp.where(seen, product(query, key_buf[slot]) * factor, neg_big)
        top = jnp.maximum(
            jnp.max(jnp.maximum(first, second), axis=1, keepdims=True),
            jnp.max(third, axis=1, keepdims=True),
        )
        shift = top.astype(BF16).astype(F32)
        first = jnp.exp2(first - shift)
        second = jnp.exp2(second - shift)
        third = jnp.exp2(third - shift)
        denom = jnp.sum(first + second, axis=1, keepdims=True) + jnp.sum(third, axis=1, keepdims=True)
        summed = jnp.dot(first.astype(BF16), own_v[slot], preferred_element_type=F32)
        summed += jnp.dot(second.astype(BF16), pair_v[slot], preferred_element_type=F32)
        summed += jnp.dot(third.astype(BF16), value_buf[slot], preferred_element_type=F32)
        summed = summed.astype(BF16)
        high = denom.astype(BF16).astype(F32)
        low = denom - high
        for index in range(group):
            head = slot * group + index
            span = slice(index * rows, (index + 1) * rows)
            mine_ref[head] = summed[span]
            stats = jnp.where(lane == head, shift[span], stats)
            stats = jnp.where(lane == heads + head, high[span], stats)
            stats = jnp.where(lane == 2 * heads + head, low[span], stats)
    mine_ref[heads] = stats.astype(BF16)


def join_kernel(*refs):
    part_refs, attn_ref = refs[:-1], refs[-1]
    half = len(part_refs)
    heads, head_dim = part_refs[0].shape[0] - 1, part_refs[0].shape[2]
    tok = part_refs[0].shape[1] // half
    width = heads * head_dim
    lane = lax.broadcasted_iota(jnp.int32, (tok, head_dim), 1)
    collected = [[] for _ in range(half)]
    for block in range(half):
        spans = [slice((k ^ block) * tok, ((k ^ block) + 1) * tok) for k in range(half)]
        stats = [ref[heads, span, :].astype(F32) for ref, span in zip(part_refs, spans)]
        highest = functools.reduce(jnp.maximum, stats)
        lifts = [jnp.exp2(stat - highest) for stat in stats]
        denoms = [
            pltpu.roll(stat, head_dim - heads, 1) + pltpu.roll(stat, head_dim - 2 * heads, 1)
            for stat in stats
        ]
        total = sum(lift * denom for lift, denom in zip(lifts, denoms))
        total = jnp.where(lane < heads, total, 1.0)
        for k, lift in enumerate(lifts):
            collected[k].append(jnp.where(lane < heads, lift / total, 0.0))
    shares = jnp.concatenate([share for column in collected for share in column], axis=0)
    high = shares.astype(BF16)
    low = (shares - high.astype(F32)).astype(BF16)
    row = lax.broadcasted_iota(jnp.int32, (head_dim, width), 0)
    column = lax.broadcasted_iota(jnp.int32, (head_dim, width), 1)
    spread_out = (lax.div(column, head_dim) == row).astype(F32).astype(BF16)
    wide = jnp.dot(high, spread_out, preferred_element_type=F32) + jnp.dot(low, spread_out, preferred_element_type=F32)
    rows = half * tok
    for block in range(half):
        for head in range(heads):
            mixed = sum(
                wide[k * rows + block * tok : k * rows + (block + 1) * tok, head * head_dim : (head + 1) * head_dim]
                * ref[head, (k ^ block) * tok : ((k ^ block) + 1) * tok, :].astype(F32)
                for k, ref in enumerate(part_refs)
            )
            attn_ref[block * tok : (block + 1) * tok, head * head_dim : (head + 1) * head_dim] = mixed.astype(BF16)


def project_kernel(own_ref, pair_ref, weight_ref, kept_ref, *refs):
    sent_refs, left = refs[:-1], refs[-1]
    ctx_index, mp_index = lax.axis_index("ctx"), lax.axis_index("mp")
    mp_count = len(sent_refs) + 1
    tok = own_ref.shape[0] // mp_count
    odd = ctx_index & 1
    pair_at = (ctx_index >> 1) ^ mp_index
    for k in range(mp_count):
        source = pl.ds(pl.multiple_of((pair_at ^ k) * tok, tok), tok)
        left[pl.ds(pl.multiple_of((2 * k + odd) * tok, tok), tok), :] = own_ref[source, :]
        left[pl.ds(pl.multiple_of((2 * k + 1 - odd) * tok, tok), tok), :] = pair_ref[source, :]
    projected = jnp.dot(left[...], weight_ref[...], preferred_element_type=F32)
    kept_ref[...] = projected[: 2 * tok]
    for k, ref in enumerate(sent_refs, 1):
        ref[...] = projected[2 * k * tok : 2 * (k + 1) * tok].astype(BF16)


def total_kernel(*refs):
    total = refs[0][...].astype(F32)
    for ref in refs[1:-1]:
        total = total + ref[...].astype(F32)
    refs[-1][...] = total.astype(BF16)


def pack_kernel(shape, pick_ref, *refs):
    mp_count, half = shape[1], shape[0] // 2
    hidden_refs, out_refs, packed = refs[:mp_count], refs[mp_count:-1], refs[-1]
    hidden = jnp.concatenate([ref[...] for ref in hidden_refs], axis=0)
    for which in range(pick_ref.shape[0]):
        packed[which] = jnp.dot(pick_ref[which], hidden, preferred_element_type=F32).astype(BF16)
    for k in range(half):
        out_refs[k][...] = packed[expert_at(shape, lax.axis_index("ctx") ^ (2 * k))]


def own_block(body):
    pl.when(lax.axis_index("ctx") >= 0)(body)


def block_rows(step, deep):
    return pl.ds(pl.multiple_of((lax.axis_index("ctx") ^ step) * deep, deep), deep)


def stage_copies(steps, gate_hbm, up_hbm, outs, sem):
    copies = []
    for at, step in enumerate(steps):
        rows = block_rows(step, outs[0].shape[0])
        copies.append(pltpu.make_async_copy(gate_hbm.at[0, rows, :], outs[2 * at], sem.at[2 * at]))
        copies.append(pltpu.make_async_copy(up_hbm.at[0, rows, :], outs[2 * at + 1], sem.at[2 * at + 1]))
    return copies


def stage_kernel(steps, *refs):
    gate_hbm, up_hbm = refs[:2]
    extra = (len(refs) - 4 - 2 * len(steps)) // 2
    plain, outs = refs[2 : 2 + extra], refs[2 + extra : -2 - extra]
    plain_out, sem, plain_sem = refs[-2 - extra : -2], refs[-2], refs[-1]
    copies = [
        pltpu.make_async_copy(source, target, plain_sem.at[at])
        for at, (source, target) in enumerate(zip(plain, plain_out))
    ]
    copies += stage_copies(steps, gate_hbm, up_hbm, outs, sem)
    for copy in copies:
        copy.start()
    for copy in copies:
        copy.wait()


def staged_like(steps, deep, units):
    return (pltpu.VMEM((deep, units), BF16),) * (2 * len(steps))


def stage(gate_proj, up_proj, deep, steps, *plain):
    units = gate_proj.shape[2]
    return pl.pallas_call(
        functools.partial(stage_kernel, steps),
        out_shape=staged_like(steps, deep, units) + tuple(pltpu.VMEM(a.shape, a.dtype) for a in plain),
        in_specs=[HBM_SPEC] * (2 + len(plain)),
        out_specs=(VMEM_SPEC,) * (2 * len(steps) + len(plain)),
        scratch_shapes=[
            pltpu.SemaphoreType.DMA((max(1, 2 * len(steps)),)),
            pltpu.SemaphoreType.DMA((max(1, len(plain)),)),
        ],
        compiler_params=pltpu.CompilerParams(vmem_limit_bytes=2 << 20),
        cost_estimate=pl.CostEstimate(flops=0, bytes_accessed=4 * len(steps) * deep * units, transcendentals=0),
        name="stage",
    )(gate_proj, up_proj, *plain)


def scaled_rows(row_ref, gain_ref, step):
    wide = row_ref[...].astype(F32)
    squares = jnp.sum(wide * wide, axis=1, keepdims=True)
    return squares, (wide * gain_ref[lax.axis_index("ctx") ^ step]).astype(BF16)


def early_kernel(numbers, steps, *refs):
    count, begun = len(numbers), 0 not in numbers
    row_refs, gain_ref, weight_refs, refs = refs[:count], refs[count], refs[count + 1 : 3 * count + 1], refs[3 * count + 1 :]
    sums_in, refs = (refs[:3], refs[3:]) if begun else (None, refs)
    columns_in, columns_out, columns_sem = (None,) * 3
    if not begun:
        columns_in, columns_out, columns_sem, refs = refs[2], refs[-4], refs[-1], (*refs[:2], *refs[3:-4], *refs[-3:-1])
    gate_hbm, up_hbm, gate_acc, up_acc, squares_ref = refs[:5]
    scaled_ref = refs[-1]
    copies = stage_copies(steps, gate_hbm, up_hbm, refs[5:-2], refs[-2]) if steps else []
    if columns_in is not None:
        columns = block_rows(3, columns_out.shape[1])
        copies.append(pltpu.make_async_copy(columns_in.at[0, :, columns], columns_out, columns_sem))
    for copy in copies:
        copy.start()
    squares = sums_in[2][:, 0:1] if begun else 0.0
    for at, number in enumerate(numbers):
        more, scaled_ref[at] = scaled_rows(row_refs[at], gain_ref, number)
        squares = squares + more
    for at in range(count):

        @own_block
        def _():
            for which, acc in enumerate((gate_acc, up_acc)):
                term = jnp.dot(scaled_ref[at], weight_refs[2 * at + which][...], preferred_element_type=F32)
                if at:
                    term = acc[...] + term
                elif begun:
                    term = sums_in[which][...] + term
                acc[...] = term

    squares_ref[...] = jnp.broadcast_to(squares, squares_ref.shape)
    for copy in copies:
        copy.wait()


def experts_kernel(numbers, *refs):
    count = len(numbers)
    row_refs, gain_ref, weight_refs, refs = refs[:count], refs[count], refs[count + 1 : 3 * count + 1], refs[3 * count + 1 :]
    gate_in, up_in, squares_ref, first_odd, down_hbm, odd_ref, act_ref = refs[:7]
    even_refs, (gate_acc, up_acc, scaled_ref, squares_acc, odd_buf, sem) = refs[7:-6], refs[-6:]
    chips = len(even_refs)
    deep = odd_ref.shape[2]
    targets = [(2 * k + 3, odd_buf.at[k - 1]) for k in range(1, chips)] + [(2 * k + 2, ref) for k, ref in enumerate(even_refs)]
    copies = [
        pltpu.make_async_copy(down_hbm.at[0, :, block_rows(number, deep)], target, sem.at[at])
        for at, (number, target) in enumerate(targets)
    ]
    for copy in copies[:chips]:
        copy.start()
    odd_weights = [first_odd] + [odd_buf.at[k] for k in range(chips - 1)]
    squares = squares_ref[:, 0:1]
    for order, number in enumerate(numbers):
        more, scaled_ref[order] = scaled_rows(row_refs[order], gain_ref, number)
        squares = squares + more
    squares_acc[...] = jnp.broadcast_to(squares, squares_acc.shape)
    for order in range(count):

        @own_block
        def _():
            for which, (acc, start) in enumerate(((gate_acc, gate_in), (up_acc, up_in))):
                former = acc if order else start
                weights = weight_refs[2 * order + which]
                acc[...] = former[...] + jnp.dot(scaled_ref[order], weights[...], preferred_element_type=F32)

        for copy in copies[chips + order : chips + order + 1]:
            copy.start()
    rms = lax.rsqrt(squares_acc[:, 0:1] / D + norm_eps)
    gate = rms * gate_acc[...]
    act_ref[...] = (gate / (1.0 + jnp.exp(-gate)) * (rms * up_acc[...])).astype(BF16)
    for k in range(chips):
        if k:
            copies[k - 1].wait()

        @own_block
        def _():
            odd_ref[k] = jnp.dot(act_ref[...], odd_weights[k][...], preferred_element_type=F32).astype(BF16)

    for copy in copies[chips - 1 :]:
        copy.wait()


def even_columns_kernel(act_ref, *refs):
    weight_refs, (down_hbm, even_ref, odd_weight_ref, sem) = refs[:-4], refs[-4:]
    copy = pltpu.make_async_copy(down_hbm.at[0, :, block_rows(1, odd_weight_ref.shape[1])], odd_weight_ref, sem)
    copy.start()
    for k, weight_ref in enumerate(weight_refs):

        @own_block
        def _():
            even_ref[k] = jnp.dot(act_ref[...], weight_ref[...], preferred_element_type=F32).astype(BF16)

    copy.wait()


def own_columns_kernel(act_ref, odd_weight_ref, down_hbm, even_ref, odd_ref, even_weight, sem):
    parts, rows = even_weight.shape[0], even_weight.shape[1]
    columns = block_rows(0, even_weight.shape[2])
    copies = [
        pltpu.make_async_copy(down_hbm.at[0, part * rows : (part + 1) * rows, columns], even_weight.at[part], sem.at[part])
        for part in range(parts)
    ]
    for copy in copies:
        copy.start()

    @own_block
    def _():
        odd_ref[...] = jnp.dot(act_ref[...], odd_weight_ref[...], preferred_element_type=F32).astype(BF16)

    total = 0.0
    for copy in copies:
        copy.wait()
    for part in range(parts):
        total += jnp.dot(act_ref[:, part * rows : (part + 1) * rows], even_weight[part], preferred_element_type=F32)
    even_ref[...] = total.astype(BF16)


def run_early(numbers, rows, gain, staged, sums, steps, gate_proj, up_proj, *down):
    tokens, deep = rows[0].shape
    units = gate_proj.shape[2]
    acc = pltpu.VMEM((tokens, units), F32)
    outs = (acc, acc, pltpu.VMEM((tokens, 128), F32)) + (staged_like(steps, deep, units) if steps else ())
    outs += tuple(pltpu.VMEM((units, deep), BF16) for _ in down)
    return pl.pallas_call(
        functools.partial(early_kernel, numbers, steps),
        out_shape=outs,
        in_specs=[VMEM_SPEC] * (len(rows) + 1 + len(staged) + len(sums)) + [HBM_SPEC] * (2 + len(down)),
        out_specs=(VMEM_SPEC,) * len(outs),
        scratch_shapes=([pltpu.SemaphoreType.DMA((2 * len(steps),))] if steps else [])
        + [pltpu.VMEM((len(rows), tokens, deep), BF16)]
        + [pltpu.SemaphoreType.DMA(()) for _ in down],
        compiler_params=pltpu.CompilerParams(vmem_limit_bytes=5 << 20),
        cost_estimate=pl.CostEstimate(
            flops=4 * tokens * deep * units * len(rows),
            bytes_accessed=4 * len(steps) * deep * units,
            transcendentals=0,
        ),
        name="early",
    )(*rows, gain, *[in_vmem(array) for array in staged], *sums, gate_proj, up_proj, *down)


def run_experts(numbers, rows, gain, staged, sums, first_odd, down_proj):
    tokens, deep = rows[0].shape
    units = down_proj.shape[1]
    count = len(rows)
    return pl.pallas_call(
        functools.partial(experts_kernel, numbers),
        out_shape=(like((count, tokens, deep)), pltpu.VMEM((tokens, units), BF16))
        + (pltpu.VMEM((units, deep), BF16),) * count,
        in_specs=[VMEM_SPEC] * (3 * count + 1 + 4) + [HBM_SPEC],
        out_specs=(VMEM_SPEC,) * (count + 2),
        scratch_shapes=[
            pltpu.VMEM((tokens, units), F32),
            pltpu.VMEM((tokens, units), F32),
            pltpu.VMEM((count, tokens, deep), BF16),
            pltpu.VMEM((tokens, 128), F32),
            pltpu.VMEM((count - 1, units, deep), BF16),
            pltpu.SemaphoreType.DMA((2 * count - 1,)),
        ],
        compiler_params=pltpu.CompilerParams(vmem_limit_bytes=EXPERTS_MIB << 20),
        cost_estimate=pl.CostEstimate(
            flops=6 * count * tokens * units * deep,
            bytes_accessed=4 * count * units * deep,
            transcendentals=tokens * units,
        ),
        name="experts",
    )(*rows, gain, *[in_vmem(array) for array in staged], *sums, in_vmem(first_odd), down_proj)


def pair_total_kernel(even_ref, other_ref, *out_refs):
    for k, ref in enumerate(out_refs):
        ref[...] = (even_ref[k].astype(F32) + other_ref[k].astype(F32)).astype(BF16)


def combine_kernel(shape, high_ref, low_ref, *refs):
    half, mp_count = shape[0] // 2, shape[1]
    piece_refs, even_ref, other_ref = refs[: half - 1][::-1], refs[half - 1], refs[half]
    kept_ref, sent_refs = refs[half + 1], refs[half + 2 :]
    own_piece = (even_ref[...].astype(F32) + other_ref[...].astype(F32)).astype(BF16)
    pieces = jnp.concatenate([own_piece] + [ref[...] for ref in piece_refs], axis=0)
    experts = [expert_at(shape, lax.axis_index("ctx") ^ (2 * k)) for k in range(half)]
    total = None
    for table in (high_ref, low_ref):
        spread = jnp.concatenate([table[expert] for expert in experts], axis=0)
        term = lax.dot_general(spread, pieces, (((0,), (0,)), ((), ())), preferred_element_type=F32)
        total = term if total is None else total + term
    rows = kept_ref.shape[0]
    kept_ref[...] = total[:rows]
    for k, ref in enumerate(sent_refs, 1):
        ref[...] = total[k * rows : (k + 1) * rows].astype(BF16)


def exchange_path(
    queries,
    cache_keys,
    cache_values,
    new_keys,
    new_values,
    out_proj,
    residual,
    norm_gain,
    gate_proj,
    up_proj,
    down_proj,
    expert_ids,
    route_logits,
):
    ctx_count = lax.axis_size("ctx")
    mp_count = lax.axis_size("mp")
    shape = (ctx_count, mp_count)
    gate_hbm, up_hbm, down_hbm = in_hbm(gate_proj), in_hbm(up_proj), in_hbm(down_proj)
    tok_local = queries.shape[0]
    tokens = tok_local * ctx_count
    slot_local, cache_local, head_dim = cache_keys.shape
    heads = queries.shape[1] // head_dim
    d_local = out_proj.shape[1]
    res_rows = residual.shape[0]
    half = ctx_count // 2
    rows = half * tok_local
    capacity = tokens * TOP // 4
    per_row = max(1, EXPERTS // mp_count)

    blocks = [queries] + spread([queries] * (half - 1), "ctx", 2)
    own = [cache_keys, cache_values, new_keys, new_values]
    pair = [swap(array, "ctx", 1) for array in own]
    held = stage(gate_hbm, up_hbm, d_local, STAGE_AT[0], *[in_hbm(array) for array in (*own, queries)])
    held, blocks[1:], pair = lax.optimization_barrier((held, blocks[1:], pair))
    begun, held = held[: 2 * len(STAGE_AT[0])], held[2 * len(STAGE_AT[0]) :]
    mine = device_call(
        attention_kernel,
        "attention",
        like((heads + 1, rows, head_dim)),
        [in_vmem(array) for array in (held[4], *blocks[1:], *held[:4], *pair)],
        [
            pltpu.VMEM((slot_local, heads // slot_local * rows, head_dim), BF16),
            pltpu.VMEM((slot_local, 2 * tok_local, head_dim), BF16),
            pltpu.VMEM((slot_local, 2 * tok_local, head_dim), BF16),
        ],
        flops=8 * heads * rows * (cache_local + tok_local) * head_dim,
        limit=24,
    )
    others = spread([mine] * (half - 1), "ctx", 2)
    ids, logits, _ = lax.optimization_barrier((expert_ids.T, route_logits.T, mine))
    pick, high, low = device_call(
        functools.partial(tables_kernel, shape),
        "tables",
        (like((per_row, capacity, tokens)),) * 3,
        [ids, logits],
    )
    gain = norm_gain.astype(F32).reshape(ctx_count, 1, d_local)
    gate_later, _ = lax.optimization_barrier((gate_proj, mine))
    *staged, out_proj, residual = stage(
        in_hbm(gate_later), up_hbm, d_local, STAGE_AT[1], in_hbm(out_proj), in_hbm(residual)
    )
    staged = [*begun, *staged]
    pick, high, low, gain, staged, out_proj, residual, others = lax.optimization_barrier(
        (pick, high, low, gain, staged, out_proj, residual, others)
    )
    attn = device_call(join_kernel, "join", like((rows, heads * head_dim)), [mine] + others)
    block = like((res_rows, d_local))

    kept, *sent = device_call(
        project_kernel,
        "project",
        (like((res_rows, d_local), F32),) + (block,) * (mp_count - 1),
        [attn, swap(attn, "ctx", 1), out_proj],
        [pltpu.VMEM((tokens, heads * head_dim), BF16)],
        flops=2 * tokens * heads * head_dim * d_local,
    )
    arrived = spread(sent, "mp")
    gate_later, _ = lax.optimization_barrier((gate_proj, kept))
    more = stage(in_hbm(gate_later), up_hbm, d_local, STAGE_AT[2])
    more, arrived = lax.optimization_barrier((more, arrived[::-1]))
    arrived = arrived[::-1]
    staged = [*staged, *more]
    hidden = device_call(total_kernel, "hidden", block, [kept, residual] + arrived[::-1])

    everyone = spread([hidden] * (mp_count - 1), "mp")
    gate_later, _ = lax.optimization_barrier((gate_proj, hidden))
    more = stage(in_hbm(gate_later), up_hbm, d_local, STAGE_AT[3])
    more, everyone = lax.optimization_barrier((more, everyone))
    staged, everyone = [*staged, *more], [hidden, *everyone]
    even = device_call(
        functools.partial(pack_kernel, shape),
        "pack",
        (like((capacity, d_local)),) * half,
        [pick] + everyone,
        [pltpu.VMEM((per_row, capacity, d_local), BF16)],
    )
    even = [even[0]] + spread(even[1:], "ctx", 2)
    numbered = [number for steps in STAGE_AT for number in steps]
    odd = swap(even[0], "ctx", 1)
    sums = run_early((0, 1), [even[0], odd], gain, staged[:4], (), STAGE_AT[4], gate_hbm, up_hbm, down_hbm)
    sums, even = lax.optimization_barrier((sums, even[:0:-1]))
    even = even[::-1]
    staged, sums, first_odd = [*staged, *sums[3:-1]], sums[:3], sums[-1]
    odd = [swap(piece, "ctx", 1) for piece in even]
    held = {number: staged[2 * at : 2 * at + 2] for at, number in enumerate(numbered[: len(staged) // 2])}
    numbers = tuple(range(2, ctx_count, 2))
    *sums, gate_last, up_last = run_early(
        numbers, even, gain, [array for number in numbers for array in held[number]], sums, STAGE_AT[5], gate_hbm, up_hbm
    )
    odd_numbers = tuple(range(3, ctx_count, 2))
    held[5] = (gate_last, up_last)
    out_odd, act, *even_weights = run_experts(
        odd_numbers, odd, gain, [array for number in odd_numbers for array in held[number]], sums, first_odd, down_hbm
    )
    out_even, odd_weight = device_call(
        even_columns_kernel,
        "even_columns",
        (like((half - 1, capacity, d_local)), pltpu.VMEM((act.shape[1], d_local), BF16)),
        [in_vmem(array) for array in (act, *even_weights)] + [down_hbm],
        [pltpu.SemaphoreType.DMA(())],
        specs=[VMEM_SPEC] * half + [HBM_SPEC],
        moved=2 * act.shape[1] * d_local,
    )
    pieces = device_call(
        pair_total_kernel,
        "pair_total",
        (like((capacity, d_local)),) * (half - 1),
        [out_even, swap(out_odd, "ctx", 1)],
    )
    act, *pieces = lax.optimization_barrier((act, *pieces))
    returned = spread(pieces, "ctx", 2)
    own_even, own_odd = device_call(
        own_columns_kernel,
        "own_columns",
        (like((capacity, d_local)),) * 2,
        [act, in_vmem(odd_weight), down_hbm],
        [pltpu.VMEM((2, act.shape[1] // 2, d_local), BF16), pltpu.SemaphoreType.DMA((2,))],
        specs=[VMEM_SPEC, VMEM_SPEC, HBM_SPEC],
        moved=1,
    )
    pieces = returned[::-1] + [own_even, swap(own_odd, "ctx", 1)]
    kept, *sent = device_call(
        functools.partial(combine_kernel, shape),
        "combine",
        (like((res_rows, d_local), F32),) + (block,) * (mp_count - 1),
        [high, low] + pieces,
    )
    arrived = spread(sent, "mp")
    return device_call(total_kernel, "layer_out", block, [kept, hidden] + arrived[::-1])


def on_device(*args):
    queries, cache_keys, out_proj, gate_proj, down_proj = (args[i] for i in (0, 1, 5, 8, 10))
    ctx_count, mp_count = lax.axis_size("ctx"), lax.axis_size("mp")
    per_row = max(1, EXPERTS // mp_count)
    fits = (
        ctx_count == 2 * mp_count
        and ctx_count & (ctx_count - 1) == 0
        and (ctx_count // per_row) % 2 == 0
        and out_proj.shape[1] % 256 == 0
        and gate_proj.shape[2] % 2048 == 0
        and queries.shape[0] % 16 == 0
        and 3 * (queries.shape[1] // cache_keys.shape[2]) <= cache_keys.shape[2]
    )
    return exchange_path(*args) if fits else gathered_path(*args)


def solution(mesh):
    placed = (
        P("ctx", "mp"),
        P("mp", "ctx", None),
        P("mp", "ctx", None),
        P("mp", "ctx", None),
        P("mp", "ctx", None),
        P("mp", "ctx"),
        P("mp", "ctx"),
        P(),
        P("ctx", None, "mp"),
        P("ctx", None, "mp"),
        P("ctx", "mp", None),
        P(),
        P(),
    )
    return jax.shard_map(
        on_device, mesh=mesh, in_specs=placed, out_specs=P("mp", "ctx"), check_vma=False
    )
```
